32 devices in a mesh: batch: 2 (over core), seq: 8 (over z, x), head: 2 (over y).
Axes of the slice: x: 2, y: 2, z: 4, core: 2. Of those that a mesh axis runs over, the one named last changes fastest.
Arguments:
- tokens: bfloat16 [2048, 8, 768], P(('seq', 'head'), 'batch'), may hold values from -6 to 6
- attn_gain: float32 [768], replicated, may hold values from 0.5 to 1.5
- attn_shift: float32 [768], replicated, may hold values from -0.6 to 0.6
- w_query: bfloat16 [768, 768], P(None, 'head'), may hold values from -0.3125 to 0.3125
- b_query: float32 [768], P('head'), may hold values from -1.2 to 1.2
- w_keyval: bfloat16 [768, 128], replicated, may hold values from -0.21875 to 0.21875
- b_value: float32 [64], replicated, may hold values from -0.6 to 0.6
- w_out: bfloat16 [768, 768], P('head'), may hold values from -1.25 to 1.25
- b_out: float32 [768], replicated, may hold values from -0.6 to 0.6
- mlp_gain: float32 [768], replicated, may hold values from 0.5 to 1.5
- mlp_shift: float32 [768], replicated, may hold values from -0.6 to 0.6
- w_up: bfloat16 [768, 3072], replicated, may hold values from -0.21875 to 0.21875
- b_up: float32 [3072], replicated, may hold values from -0.6 to 0.6
- w_down: bfloat16 [3072, 768], replicated, may hold values from -0.109375 to 0.109375
- b_down: float32 [768], replicated, may hold values from -0.6 to 0.6
- doc_lengths: int32 [8, 8], P('batch'), may hold values from 1 to 1280, 2048 in all within a row
- cotangent: bfloat16 [2048, 8, 768], P(('seq', 'head'), 'batch'), may hold values from -6 to 6
Outputs:
- result: bfloat16 [2048, 8, 768], P(('seq', 'head'), 'batch')
- grad_tokens: float32 [2048, 8, 768], P(('seq', 'head'), 'batch')
- grad_attn_gain: float32 [768], replicated
- grad_attn_shift: float32 [768], replicated
- grad_w_query: float32 [768, 768], P(None, 'head')
- grad_b_query: float32 [768], P('head')
- grad_w_keyval: float32 [768, 128], replicated
- grad_b_value: float32 [64], replicated
- grad_w_out: float32 [768, 768], P('head')
- grad_b_out: float32 [768], replicated
- grad_mlp_gain: float32 [768], replicated
- grad_mlp_shift: float32 [768], replicated
- grad_w_up: float32 [768, 3072], replicated
- grad_b_up: float32 [3072], replicated
- grad_w_down: float32 [3072, 768], replicated
- grad_b_down: float32 [768], replicated
The draws below stay inside these ranges and needn't reach their ends.
Inputs may be any that keep to these rules, and one draw needn't show every extreme that they name: `doc_lengths`: each row holds the lengths of the 8 documents of one packed sequence in order; they sum to 2048, and the longest is exactly 1280.
All inputs are finite; a program needn't handle non-finite values.
Results may differ from the reference program's by a relative error of at most 0.014.
Values may be sent and summed in bfloat16 or wider, within the bound.
No kernel may reach another device: no remote copies, remote signals or barrier semaphores. Data moves between devices by JAX's collectives and lax.ppermute only.
A program may use at most 256 MiB of HBM per device.

```python
import math
from functools import partial
import jax
import jax.numpy as jnp
import numpy as np
from jax import lax

D = 768
HEADS = 12
HD = 64
FF = 3072
DOCS = 8
SEQ_LEN = 2048
DOC_MOST = 1280
SEQUENCES = 8


def levels(rng, shape, split, smallest, top_value):
    factor_of, own = 1.0, jax.random.fold_in(rng, 6)
    for axis_at, parts in split:
        heights = jnp.exp(jax.random.uniform(jax.random.fold_in(own, axis_at), (parts,), jnp.float32, smallest / len(split), top_value / len(split)))
        factor_of = factor_of * jnp.repeat(heights, shape[axis_at] // parts).reshape([-1 if axis == axis_at else 1 for axis in range(len(shape))])
    return factor_of


def profile(amount, total, most, skew):
    weights = [(1 << 20) // math.isqrt(rank ** skew) + 1 for rank in range(2, amount + 1)]
    rest, given = total - most - (amount - 1), [1] * (amount - 1)
    while rest > 0:
        free = [i for i in range(amount - 1) if given[i] < most]
        mass, left = sum([weights[i] for i in free]), rest
        for i in free:
            addition = min(most - given[i], max(1, left * weights[i] // mass), rest)
            given[i] = given[i] + addition
            rest = rest - addition
    return np.array([most] + given)


def ragged_sizes(rng, number_of, total, bound, lean):
    if number_of == 2:
        one = jax.random.randint(rng, (), max(1, total - bound), min(bound, total - 1) + 1)
        return jnp.stack([one, total - one])
    sizes = jnp.asarray(profile(number_of, total, bound, lean), jnp.int32)
    twos = (number_of - 1) // 2
    donor, taker = sizes[1:1 + 2 * twos:2], sizes[2:2 + 2 * twos:2]
    room = jnp.minimum(donor - 1, bound - taker)
    passed = jax.random.randint(jax.random.fold_in(rng, 1), (twos,), 0, 1 << 20) % (room + 1)
    sizes = sizes.at[1:1 + 2 * twos:2].set(donor - passed).at[2:2 + 2 * twos:2].set(taker + passed)
    return sizes[jax.random.permutation(jax.random.fold_in(rng, 2), number_of)]


def scatter_about(stream_key, dims, scale, reach, cuts=(), held_as=jnp.bfloat16):
    factor_of = levels(stream_key, dims, cuts, -0.22, 0.18) if cuts else 1.0
    values = jax.random.normal(stream_key, dims, jnp.float32) * scale * factor_of
    return jnp.minimum(jnp.maximum(values, -reach), reach).astype(held_as)


def setup_inputs(seed: int = 0) -> dict:
    seeds = jax.random.split(jax.random.key(seed), 18)
    tokens = scatter_about(seeds[0], (SEQ_LEN, SEQUENCES, D), 1.0, 6.0, ((0, 16), (1, 2)))
    attn_gain = jnp.clip(1.0 + 0.1 * jax.random.normal(seeds[1], (D,), jnp.float32), 0.5, 1.5)
    attn_shift = scatter_about(seeds[2], (D,), 0.1, 0.6, (), jnp.float32)
    w_query = scatter_about(seeds[3], (D, HEADS * HD), (D // 2) ** -0.5, 0.3125, ((1, 2),))
    b_query = scatter_about(seeds[4], (HEADS * HD,), 0.2, 1.2, ((0, 2),), jnp.float32)
    w_keyval = scatter_about(seeds[5], (D, 2 * HD), D ** -0.5, 0.21875)
    b_value = scatter_about(seeds[6], (HD,), 0.1, 0.6, (), jnp.float32)
    w_out = scatter_about(seeds[7], (HEADS * HD, D), (D // 32) ** -0.5, 1.25, ((0, 2),))
    b_out = scatter_about(seeds[8], (D,), 0.1, 0.6, (), jnp.float32)
    mlp_gain = jnp.clip(1.0 + 0.1 * jax.random.normal(seeds[9], (D,), jnp.float32), 0.5, 1.5)
    mlp_shift = scatter_about(seeds[10], (D,), 0.1, 0.6, (), jnp.float32)
    w_up = scatter_about(seeds[11], (D, FF), D ** -0.5, 0.21875)
    b_up = scatter_about(seeds[12], (FF,), 0.1, 0.6, (), jnp.float32)
    w_down = scatter_about(seeds[13], (FF, D), FF ** -0.5, 0.109375)
    b_down = scatter_about(seeds[14], (D,), 0.1, 0.6, (), jnp.float32)
    doc_lengths = jax.vmap(lambda own: ragged_sizes(own, DOCS, SEQ_LEN, DOC_MOST, 2))(jax.random.split(seeds[15], SEQUENCES)).reshape((SEQUENCES, DOCS)).astype(jnp.int32)
    cotangent = scatter_about(seeds[16], (SEQ_LEN, SEQUENCES, D), 1.0, 6.0, ((0, 16), (1, 2)))
    return dict(tokens=tokens, attn_gain=attn_gain, attn_shift=attn_shift, w_query=w_query, b_query=b_query, w_keyval=w_keyval, b_value=b_value, w_out=w_out, b_out=b_out, mlp_gain=mlp_gain, mlp_shift=mlp_shift, w_up=w_up, b_up=b_up, w_down=w_down, b_down=b_down, doc_lengths=doc_lengths, cotangent=cotangent)


EPSILON = 1e-05
MASKED = -1e+30
HIGHEST = lax.Precision.HIGHEST

@jax.custom_vjp
def low(v):
    return lax.optimization_barrier(v.astype(jnp.bfloat16)).astype(jnp.float32)

@jax.custom_vjp
def low_back(v):
    return v

def low_keep(v):
    return (low(v), None)

def low_pass(kept, grad):
    return (grad,)

def back_keep(v):
    return (v, None)

def back_low(kept, grad):
    return (low(grad),)
low.defvjp(low_keep, low_pass)
low_back.defvjp(back_keep, back_low)

def layer_norm(inputs, norm_gain, norm_shift):
    center = inputs - lax.optimization_barrier(jnp.mean(inputs, axis=-1, keepdims=True))
    spread = lax.optimization_barrier(jnp.mean(center * center, axis=-1, keepdims=True))
    return center * lax.rsqrt(spread + EPSILON) * norm_gain + norm_shift

def segment_ids(lengths_row, length):
    bounds = jnp.cumsum(lengths_row).astype(jnp.int32)
    places = jnp.arange(length, dtype=jnp.int32)
    return lax.optimization_barrier(jnp.sum((places[:, None] >= bounds[None, :]).astype(jnp.int32), axis=1))

def attend_sequence(members):
    query_seq, key_seq, value_seq, seg_seq = members
    length = key_seq.shape[0]
    head_dim = key_seq.shape[1]
    block_rows = min(512, length)
    score_scale = 1.0 / math.sqrt(head_dim)
    key_places = jnp.arange(length, dtype=jnp.int32)

    def one_block(pieces):
        query_block, block_start = pieces
        query_places = block_start + jnp.arange(block_rows, dtype=jnp.int32)
        seg_block = lax.dynamic_slice_in_dim(seg_seq, block_start, block_rows)
        raw_scores = jnp.einsum('qhd,kd->hqk', query_block, key_seq, precision=HIGHEST)
        scores = low_back(raw_scores * score_scale)
        allowed = (key_places[None, :] <= query_places[:, None]) & (seg_block[:, None] == seg_seq[None, :])
        scores = jnp.where(allowed[None], scores, MASKED)
        weights = low(jax.nn.softmax(scores, axis=-1))
        return jnp.einsum('hqk,kd->qhd', weights, value_seq, precision=HIGHEST)
    blocks = query_seq.reshape(length // block_rows, block_rows, query_seq.shape[1], head_dim)
    starts = jnp.arange(length // block_rows, dtype=jnp.int32) * block_rows
    mixed_heads = lax.map(jax.checkpoint(one_block), (blocks, starts))
    return mixed_heads.reshape(length, query_seq.shape[1], head_dim)

def layer_forward(segments, tokens, attn_gain, attn_shift, w_query, b_query, w_keyval, b_value, w_out, b_out, mlp_gain, mlp_shift, w_up, b_up, w_down, b_down):
    head_dim = w_keyval.shape[1] // 2
    head_count = w_query.shape[1] // head_dim
    length = tokens.shape[0]
    batches = tokens.shape[1]
    normed = low(layer_norm(tokens, attn_gain, attn_shift))
    queries = low(low_back(jnp.dot(normed, w_query, precision=HIGHEST) + b_query))
    keyval = jnp.dot(normed, w_keyval, precision=HIGHEST)
    key_rows = low(low_back(keyval[:, :, :head_dim]))
    values = low(low_back(keyval[:, :, head_dim:] + b_value))
    mixed_heads = lax.map(attend_sequence, (jnp.moveaxis(queries.reshape(length, batches, head_count, head_dim), 1, 0), jnp.moveaxis(key_rows, 1, 0), jnp.moveaxis(values, 1, 0), segments))
    mixed_heads = jnp.moveaxis(mixed_heads, 0, 1).reshape(length, batches, head_count * head_dim)
    mixed_heads = low(low_back(mixed_heads))
    branch = low_back(jnp.dot(mixed_heads, w_out, precision=HIGHEST) + b_out)
    middle = tokens + branch
    inner_normed = low(layer_norm(middle, mlp_gain, mlp_shift))
    upward = low_back(jnp.dot(inner_normed, w_up, precision=HIGHEST) + b_up)
    active = low(jax.nn.gelu(upward, approximate=True))
    return middle + (jnp.dot(active, w_down, precision=HIGHEST) + b_down)

def reference(tokens, attn_gain, attn_shift, w_query, b_query, w_keyval, b_value, w_out, b_out, mlp_gain, mlp_shift, w_up, b_up, w_down, b_down, doc_lengths, cotangent):
    segments = jnp.stack([segment_ids(doc_lengths[window], SEQ_LEN) for window in range(SEQUENCES)])
    inputs = (tokens, attn_gain, attn_shift, w_query, b_query, w_keyval, b_value, w_out, b_out, mlp_gain, mlp_shift, w_up, b_up, w_down, b_down)
    floats = tuple((member.astype(jnp.float32) for member in inputs))
    result, pullback = jax.vjp(partial(layer_forward, segments), *floats)
    gradients = pullback(cotangent.astype(jnp.float32))
    return (result.astype(jnp.bfloat16), gradients[0], gradients[1], gradients[2], gradients[3], gradients[4], gradients[5], gradients[6], gradients[7], gradients[8], gradients[9], gradients[10], gradients[11], gradients[12], gradients[13], gradients[14])
```

```python
from functools import partial
import math

import jax
import jax.numpy as jnp
from jax import lax
from jax.experimental import pallas as pl
from jax.experimental.pallas import tpu as pltpu
from jax.sharding import PartitionSpec as P

EPSILON = 1e-05
MASKED = -1e30
BF = jnp.bfloat16
F32 = jnp.float32
LOG2E = math.log2(math.e)


def layer_norm(inputs, norm_gain, norm_shift):
    center = inputs - jnp.mean(inputs, axis=-1, keepdims=True)
    spread = jnp.mean(center * center, axis=-1, keepdims=True)
    return center * lax.rsqrt(spread + EPSILON) * norm_gain + norm_shift


def swap(value, step):
    axis, flip = step
    size = lax.axis_size(axis)
    return lax.ppermute(value, axis, [(i, i ^ flip) for i in range(size)])


def bit_of(step):
    axis, flip = step
    return (lax.axis_index(axis) // flip) % 2


def split_dim(shape):
    if (shape[0] // 2) % 16 == 0:
        return 0
    return 1


def halve(value, step):
    dim = split_dim(value.shape)
    half = value.shape[dim] // 2
    bit = bit_of(step)
    got = swap(lax.dynamic_slice_in_dim(value, (1 - bit) * half, half, dim), step)
    kept = lax.dynamic_slice_in_dim(value, bit * half, half, dim)
    return (kept.astype(F32) + got.astype(F32)).astype(value.dtype), dim


def double(value, step, dim):
    got = swap(value, step)
    return jnp.where(
        bit_of(step) == 1,
        jnp.concatenate([got, value], dim),
        jnp.concatenate([value, got], dim),
    )


def reduce_all(pieces):
    arrays = [piece for piece, _ in pieces]
    dims = [[] for _ in pieces]
    longest = max(len(order) for _, order in pieces)
    for i in range(longest):
        for at, (_, order) in enumerate(pieces):
            if i < len(order):
                arrays[at], dim = halve(arrays[at], order[i])
                dims[at].append(dim)
    for i in range(longest - 1, -1, -1):
        for at, (_, order) in enumerate(pieces):
            if i < len(order):
                arrays[at] = double(arrays[at], order[i], dims[at][i])
    return arrays


def dot(a, b, dims):
    return lax.dot_general(a, b, (dims, ((), ())), preferred_element_type=F32)


def side_by_side(rows, heads, hd):
    return jnp.concatenate([rows[h * hd : (h + 1) * hd, :] for h in range(heads)], axis=1)


def chunk_pos(me, j, chunk, tq):
    base = ((me * tq) // chunk) ^ j
    rows = lax.broadcasted_iota(jnp.int32, (chunk, tq), 0)
    return base * chunk, base * chunk + (rows ^ ((me * tq) % chunk))


def forward_kernel(scal, q_ref, kv_ref, lo_ref, out_ref, lse_ref, m_s, l_s, acc_s, *, heads, hd, chunk):
    w = pl.program_id(0)
    me = scal[0]
    tq = q_ref.shape[2]
    lo_min = scal[1 + w]
    first = me * tq
    scale2 = LOG2E / math.sqrt(hd)
    group = 2
    lanes = group * tq
    zeros = jnp.zeros((hd, lanes), BF)
    lo = lo_ref[0]
    query = first + lax.broadcasted_iota(jnp.int32, (chunk, tq), 1)
    m_s[...] = jnp.full(m_s.shape, MASKED, F32)
    l_s[...] = jnp.zeros(l_s.shape, F32)
    acc_s[...] = jnp.zeros(acc_s.shape, F32)

    def body(j, carry):
        base, pos = chunk_pos(me, j, chunk, tq)

        @pl.when((base < first + tq) & (base + chunk > lo_min))
        def _():
            kv = kv_ref[0, pl.ds(pl.multiple_of(j * chunk, chunk), chunk), :]
            kv_t = kv.T
            allowed = (pos >= lo) & (pos <= query)
            allowed = jnp.concatenate([allowed] * group, axis=1)
            for g in range(heads // group):
                cols = slice(g * lanes, (g + 1) * lanes)
                rows = q_ref[0, g * group * hd : (g + 1) * group * hd, :]
                q_pad = jnp.concatenate([side_by_side(rows, group, hd), zeros], axis=0)
                s = dot(kv, q_pad, ((1,), (0,))) * scale2
                s = jnp.where(allowed, s, MASKED)
                m_old = m_s[:, cols]
                m_new = jnp.maximum(m_old, jnp.max(s, axis=0, keepdims=True))
                p = jnp.exp2(s - m_new)
                alpha = jnp.exp2(m_old - m_new)
                m_s[:, cols] = m_new
                l_s[:, cols] = l_s[:, cols] * alpha + jnp.sum(p, axis=0, keepdims=True)
                pv = dot(kv_t, p.astype(BF), ((1,), (0,)))
                acc_s[:, cols] = acc_s[:, cols] * alpha + pv[hd:, :]

        return carry

    lax.fori_loop(0, kv_ref.shape[1] // chunk, body, 0)
    total = l_s[...]
    out = acc_s[...] / total
    lse_ref[0] = m_s[...] + jnp.log2(total)
    for h in range(heads):
        out_ref[0, h * hd : (h + 1) * hd, :] = out[:, h * tq : (h + 1) * tq].astype(BF)


def backward_kernel(
    scal, q_ref, kv_ref, lo_ref, out_ref, lse_ref, do_ref, dq_ref, dkv_ref, delta_s, dq_s, *, heads, hd, chunk
):
    w = pl.program_id(0)
    me = scal[0]
    tq = q_ref.shape[2]
    lo_min = scal[1 + w]
    first = me * tq
    scale = 1.0 / math.sqrt(hd)
    scale2 = LOG2E * scale
    group = 2
    lanes = group * tq
    zeros = jnp.zeros((hd, lanes), BF)
    lo = lo_ref[0]
    query = first + lax.broadcasted_iota(jnp.int32, (chunk, tq), 1)
    dq_s[...] = jnp.zeros(dq_s.shape, F32)
    for h in range(heads):
        rows = slice(h * hd, (h + 1) * hd)
        delta_s[:, h * tq : (h + 1) * tq] = jnp.sum(
            out_ref[0, rows, :].astype(F32) * do_ref[0, rows, :].astype(F32), axis=0, keepdims=True
        )
    lane = lax.broadcasted_iota(jnp.int32, (chunk, 2 * hd), 1)

    def body(j, carry):
        base, pos = chunk_pos(me, j, chunk, tq)
        here = pl.ds(pl.multiple_of(j * chunk, chunk), chunk)
        needed = (base < first + tq) & (base + chunk > lo_min)

        @pl.when(jnp.logical_not(needed))
        def _():
            dkv_ref[0, here, :] = jnp.zeros((chunk, 2 * hd), BF)

        @pl.when(needed)
        def _():
            kv = kv_ref[0, here, :]
            kv_t = kv.T
            allowed = (pos >= lo) & (pos <= query)
            allowed = jnp.concatenate([allowed] * group, axis=1)
            dkv = jnp.zeros((chunk, 2 * hd), F32)
            for g in range(heads // group):
                cols = slice(g * lanes, (g + 1) * lanes)
                rows = slice(g * group * hd, (g + 1) * group * hd)
                q_pad = jnp.concatenate([side_by_side(q_ref[0, rows, :], group, hd), zeros], axis=0)
                do_pad = jnp.concatenate([zeros, side_by_side(do_ref[0, rows, :], group, hd)], axis=0)
                s = dot(kv, q_pad, ((1,), (0,))) * scale2
                p = jnp.where(allowed, jnp.exp2(s - lse_ref[0, :, cols]), 0.0)
                dp = dot(kv, do_pad, ((1,), (0,)))
                ds = (p * (dp - delta_s[:, cols])).astype(BF)
                dkv = dkv + dot(ds, q_pad, ((1,), (1,))) * scale + dot(p.astype(BF), do_pad, ((1,), (1,)))
                dq_s[:, cols] = dq_s[:, cols] + dot(kv_t, ds, ((1,), (0,)))[:hd, :]
            dkv_ref[0, here, :] = dkv.astype(BF)

        return carry

    lax.fori_loop(0, kv_ref.shape[1] // chunk, body, 0)
    for h in range(heads):
        dq_ref[0, h * hd : (h + 1) * hd, :] = (dq_s[:, h * tq : (h + 1) * tq] * scale).astype(BF)


def per_window(shape):
    zeros = (0,) * (len(shape) - 1)
    return pl.BlockSpec((1, *shape[1:]), lambda w, scal: (w, *zeros))


def attention_call(kernel, scalars, inputs, outs, scratch, name, flops):
    moved = sum(math.prod(a.shape) * a.dtype.itemsize for a in (*inputs, *outs))
    return pl.pallas_call(
        kernel,
        out_shape=outs,
        grid_spec=pltpu.PrefetchScalarGridSpec(
            num_scalar_prefetch=1,
            grid=(inputs[0].shape[0],),
            in_specs=[per_window(a.shape) for a in inputs],
            out_specs=[per_window(a.shape) for a in outs],
            scratch_shapes=scratch,
        ),
        cost_estimate=pl.CostEstimate(flops=flops, bytes_accessed=moved, transcendentals=0),
        name=name,
    )(scalars, *inputs)


def local(
    tokens,
    attn_gain,
    attn_shift,
    w_query,
    b_query,
    w_keyval,
    b_value,
    w_out,
    b_out,
    mlp_gain,
    mlp_shift,
    w_up,
    b_up,
    w_down,
    b_down,
    doc_lengths,
    cotangent,
):
    tq, windows, width = tokens.shape
    hd = w_keyval.shape[1] // 2
    own_cols = w_query.shape[1]
    seq_size = lax.axis_size("seq")
    cols = own_cols * lax.axis_size("head")
    heads = cols // hd
    seq_total = tq * seq_size * lax.axis_size("head")
    me = lax.axis_index("seq") * lax.axis_size("head") + lax.axis_index("head")
    chunk = min(2 * tq, seq_total)

    core = ("batch", 1)
    head = ("head", 1)
    low = ("seq", 1)
    highs = [("seq", 1 << i) for i in range(1, int(math.log2(seq_size)))]

    def other_half(weight):
        half = weight.shape[0] // 2
        part = lax.dynamic_slice_in_dim(weight, lax.axis_index("batch") * half, half, 0)
        return double(swap(part, head), core, 0)

    wq_other = other_half(w_query)
    bq_other = swap(b_query, head)
    wq_all = jnp.concatenate([w_query, wq_other], 1)
    bq_all = jnp.concatenate([b_query, bq_other])
    wo_all = jnp.concatenate([w_out, other_half(w_out)], 0)

    bounds = jnp.cumsum(doc_lengths, axis=1)
    places = me * tq + jnp.arange(tq, dtype=jnp.int32)
    starts = jnp.max(
        jnp.where(bounds[:, :, None] <= places[None, None, :], bounds[:, :, None], 0), axis=1
    )
    scalars = jnp.concatenate([me[None].astype(jnp.int32), starts[:, 0]])
    starts = starts[:, None, :]

    residual = jnp.transpose(tokens, (1, 0, 2)).astype(F32)
    normed = layer_norm(residual, attn_gain, attn_shift).astype(BF)
    value_bias = jnp.concatenate([jnp.zeros((hd,), F32), b_value])
    keyval = (
        jnp.einsum("wtd,dc->wtc", normed, w_keyval, preferred_element_type=F32) + value_bias
    ).astype(BF)

    def gather_blocks(value, order):
        block = value.reshape(value.shape[0], 1, 1, 1, tq, 2 * hd)
        for step in order:
            dim = 3 if step == head else 2 if step == low else 1
            block = jnp.concatenate([block, swap(block, step)], dim)
        return block.reshape(value.shape[0], seq_total, 2 * hd)

    def reduce_blocks(value, order):
        block = value.reshape(value.shape[0], seq_size // 2, 2, 2, tq, 2 * hd)
        for step in reversed(order):
            dim = 3 if step == head else 2 if step == low else 1
            kept, sent = jnp.split(block, 2, dim)
            block = (kept.astype(F32) + swap(sent, step).astype(F32)).astype(BF)
        return block.reshape(value.shape[0], tq, 2 * hd)

    half_w = windows // 2
    order_a, order_b = highs + [low, head], highs + [head, low]
    keyval_all = jnp.concatenate(
        [gather_blocks(keyval[:half_w], order_a), gather_blocks(keyval[half_w:], order_b)], 0
    )

    queries = (
        jnp.einsum("do,wtd->wot", wq_all, normed, preferred_element_type=F32) + bq_all[None, :, None]
    ).astype(BF)

    struct = jax.ShapeDtypeStruct
    lanes = heads * tq
    work = 2 * windows * lanes * (seq_total // 4) * hd
    mixed, log_total = attention_call(
        partial(forward_kernel, heads=heads, hd=hd, chunk=chunk),
        scalars,
        (queries, keyval_all, starts),
        (struct((windows, cols, tq), BF), struct((windows, 1, lanes), F32)),
        [pltpu.VMEM((1, lanes), F32), pltpu.VMEM((1, lanes), F32), pltpu.VMEM((hd, lanes), F32)],
        "attend",
        8 * work,
    )

    branch = jnp.einsum("wot,od->wtd", mixed, wo_all, preferred_element_type=F32)
    middle = residual + (branch + b_out)
    inner = layer_norm(middle, mlp_gain, mlp_shift).astype(BF)
    upstream_low = jnp.transpose(cotangent, (1, 0, 2))
    upstream = upstream_low.astype(F32)

    upward = jnp.einsum("wtd,df->wtf", inner, w_up, preferred_element_type=F32) + b_up
    active = jax.nn.gelu(upward, approximate=True).astype(BF)
    grad_w_down = jnp.einsum("wtf,wtd->fd", active, upstream_low, preferred_element_type=F32).astype(BF)
    grad_active = jnp.einsum("wtd,fd->wtf", upstream_low, w_down, preferred_element_type=F32)
    gelu_back = jax.vjp(partial(jax.nn.gelu, approximate=True), upward)[1]
    grad_upward = gelu_back(grad_active)[0].astype(BF)
    grad_w_up = jnp.einsum("wtd,wtf->df", inner, grad_upward, preferred_element_type=F32).astype(BF)
    grad_b_up = jnp.sum(grad_upward.astype(F32), axis=(0, 1))
    grad_inner = jnp.einsum("wtf,df->wtd", grad_upward, w_up, preferred_element_type=F32)
    result = (
        middle + (jnp.einsum("wtf,fd->wtd", active, w_down, preferred_element_type=F32) + b_down)
    ).astype(BF)
    grad_b_down = jnp.sum(upstream, axis=(0, 1))
    norm_back = jax.vjp(layer_norm, middle, mlp_gain, mlp_shift)[1]
    grad_mid_norm, grad_mlp_gain, grad_mlp_shift = norm_back(grad_inner)
    grad_middle = upstream + grad_mid_norm
    grad_branch = grad_middle.astype(BF)
    grad_b_out = jnp.sum(grad_branch.astype(F32), axis=(0, 1))
    grad_mixed = jnp.einsum("od,wtd->wot", wo_all, grad_branch, preferred_element_type=F32).astype(BF)
    grad_w_out = jnp.einsum("wot,wtd->od", mixed, grad_branch, preferred_element_type=F32).astype(BF)

    wide = [core, low, head, *highs], [core, head, low, *highs]
    own_sum = [core, low, *highs]
    grad_w_out = (
        grad_w_out[:own_cols].astype(F32) + swap(grad_w_out[own_cols:], head).astype(F32)
    ).astype(BF)
    grad_w_down, grad_w_up, grad_w_out = reduce_all(
        [(grad_w_down, wide[0]), (grad_w_up, wide[1]), (grad_w_out, own_sum)]
    )

    grad_queries, grad_keyval_all = attention_call(
        partial(backward_kernel, heads=heads, hd=hd, chunk=chunk),
        scalars,
        (queries, keyval_all, starts, mixed, log_total, grad_mixed),
        (struct((windows, cols, tq), BF), struct(keyval_all.shape, BF)),
        [pltpu.VMEM((1, lanes), F32), pltpu.VMEM((hd, lanes), F32)],
        "attend_back",
        20 * work,
    )

    grad_w_query = jnp.einsum("wot,wtd->od", grad_queries, normed, preferred_element_type=F32).astype(BF)
    grad_w_query = (
        grad_w_query[:own_cols].astype(F32) + swap(grad_w_query[own_cols:], head).astype(F32)
    ).astype(BF)
    (grad_w_query,) = reduce_all([(grad_w_query, own_sum)])
    grad_b_query = jnp.sum(grad_queries.astype(F32), axis=(0, 2))
    grad_b_query = grad_b_query[:own_cols] + swap(grad_b_query[own_cols:], head)

    grad_keyval = jnp.concatenate(
        [reduce_blocks(grad_keyval_all[:half_w], order_a), reduce_blocks(grad_keyval_all[half_w:], order_b)],
        0,
    )
    grad_w_keyval = jnp.einsum("wtd,wtc->dc", normed, grad_keyval, preferred_element_type=F32)
    grad_b_value = jnp.sum(grad_keyval[:, :, hd:].astype(F32), axis=(0, 1))
    grad_normed = jnp.einsum("wot,do->wtd", grad_queries, wq_all, preferred_element_type=F32)
    grad_normed = grad_normed + jnp.einsum(
        "wtc,dc->wtd", grad_keyval, w_keyval, preferred_element_type=F32
    )
    first_back = jax.vjp(layer_norm, residual, attn_gain, attn_shift)[1]
    grad_input, grad_attn_gain, grad_attn_shift = first_back(grad_normed)
    grad_tokens = grad_middle + grad_input

    everyone = [core, head, low, *highs]
    ff = w_up.shape[1]
    early = jnp.concatenate(
        [grad_b_up.reshape(ff // width, width), grad_b_down[None], grad_mlp_gain[None], grad_mlp_shift[None], grad_b_out[None]],
        0,
    )
    for step in everyone:
        early = early + swap(early, step)
    pad = (-hd) % 128
    tail = jnp.concatenate([grad_attn_gain, grad_attn_shift, grad_b_value, jnp.zeros((pad,), F32)])
    tail = tail.reshape(-1, 128)
    half_tail = grad_w_keyval
    for step in everyone:
        tail = tail + swap(tail, step)
    for step in [core, low, *highs]:
        grad_b_query = grad_b_query + swap(grad_b_query, step)
    (half_tail,) = reduce_all([(half_tail, everyone)])
    tail = tail.reshape(-1)

    rows_up = ff // width
    return (
        jnp.transpose(result, (1, 0, 2)),
        jnp.transpose(grad_tokens, (1, 0, 2)),
        tail[:width],
        tail[width : 2 * width],
        grad_w_query.astype(F32).T,
        grad_b_query,
        half_tail,
        tail[2 * width : 2 * width + hd],
        grad_w_out.astype(F32),
        early[rows_up + 3],
        early[rows_up + 1],
        early[rows_up + 2],
        grad_w_up.astype(F32),
        early[:rows_up].reshape(-1),
        grad_w_down.astype(F32),
        early[rows_up],
    )


def solution(mesh):
    return jax.shard_map(
        local,
        mesh=mesh,
        in_specs=(
            P(("seq", "head"), "batch", None),
            P(),
            P(),
            P(None, "head"),
            P("head"),
            P(),
            P(),
            P("head", None),
            P(),
            P(),
            P(),
            P(),
            P(),
            P(),
            P(),
            P("batch", None),
            P(("seq", "head"), "batch", None),
        ),
        out_specs=(
            P(("seq", "head"), "batch", None),
            P(("seq", "head"), "batch", None),
            P(),
            P(),
            P(None, "head"),
            P("head"),
            P(),
            P(),
            P("head", None),
            P(),
            P(),
            P(),
            P(),
            P(),
            P(),
            P(),
        ),
        check_vma=False,
    )
```

```python
from functools import partial
import math

import jax
import jax.numpy as jnp
from jax import lax
from jax.experimental import pallas as pl
from jax.experimental.pallas import tpu as pltpu
from jax.sharding import PartitionSpec as P

EPSILON = 1e-05
MASKED = -1e30
BF = jnp.bfloat16
F32 = jnp.float32
LOG2E = math.log2(math.e)


def layer_norm(inputs, norm_gain, norm_shift):
    center = inputs - jnp.mean(inputs, axis=-1, keepdims=True)
    spread = jnp.mean(center * center, axis=-1, keepdims=True)
    return center * lax.rsqrt(spread + EPSILON) * norm_gain + norm_shift


def swap(value, step):
    axis, flip = step
    size = lax.axis_size(axis)
    return lax.ppermute(value, axis, [(i, i ^ flip) for i in range(size)])


def bit_of(step):
    axis, flip = step
    return (lax.axis_index(axis) // flip) % 2


def split_dim(shape):
    if (shape[0] // 2) % 16 == 0:
        return 0
    return 1


def add_low(kept, got):
    return (kept.astype(F32) + got.astype(F32)).astype(kept.dtype)


def tie(*trees):
    leaves, shape = jax.tree.flatten(trees)
    return jax.tree.unflatten(shape, lax.optimization_barrier(leaves))


def halve(arrays, step):
    bit = bit_of(step)
    dims = [split_dim(a.shape) for a in arrays]
    halves = [a.shape[d] // 2 for a, d in zip(arrays, dims)]
    sent = [lax.dynamic_slice_in_dim(a, (1 - bit) * h, h, d) for a, h, d in zip(arrays, halves, dims)]
    kept = [lax.dynamic_slice_in_dim(a, bit * h, h, d) for a, h, d in zip(arrays, halves, dims)]
    return [add_low(k, g) for k, g in zip(kept, swap_all(sent, step))], dims


def swap_all(arrays, step):
    if len({a.shape[1] for a in arrays}) > 1:
        return [swap(a, step) for a in arrays]
    got = swap(jnp.concatenate(arrays, 0) if len(arrays) > 1 else arrays[0], step)
    at, out = 0, []
    for a in arrays:
        out.append(got[at : at + a.shape[0]])
        at += a.shape[0]
    return out


def double(arrays, step, dims):
    got = swap_all(arrays, step)
    first = bit_of(step) == 0
    return [
        jnp.concatenate([jnp.where(first, a, g), jnp.where(first, g, a)], d) for a, g, d in zip(arrays, got, dims)
    ]


def dot(a, b, dims):
    return lax.dot_general(a, b, (dims, ((), ())), preferred_element_type=F32)


def side_by_side(rows, heads, hd):
    return jnp.concatenate([rows[h * hd : (h + 1) * hd, :] for h in range(heads)], axis=1)


def chunk_pos(me, j, chunk, tq):
    base = ((me * tq) // chunk) ^ j
    rows = lax.broadcasted_iota(jnp.int32, (chunk, tq), 0)
    return base * chunk, base * chunk + (rows ^ ((me * tq) % chunk))


def forward_kernel(scal, q_ref, kv_ref, lo_ref, out_ref, lse_ref, m_s, l_s, acc_s, *, heads, hd, chunk):
    w = pl.program_id(0)
    me = scal[0]
    tq = q_ref.shape[2]
    lo_min = scal[1 + w]
    first = me * tq
    scale2 = LOG2E / math.sqrt(hd)
    group = 2
    lanes = group * tq
    zeros = jnp.zeros((hd, lanes), BF)
    lo = lo_ref[0]
    query = first + lax.broadcasted_iota(jnp.int32, (chunk, tq), 1)
    m_s[...] = jnp.full(m_s.shape, MASKED, F32)
    l_s[...] = jnp.zeros(l_s.shape, F32)
    acc_s[...] = jnp.zeros(acc_s.shape, F32)

    def body(j, carry):
        base, pos = chunk_pos(me, j, chunk, tq)

        @pl.when((base < first + tq) & (base + chunk > lo_min))
        def _():
            kv = kv_ref[0, pl.ds(pl.multiple_of(j * chunk, chunk), chunk), :]
            kv_t = kv.T
            allowed = (pos >= lo) & (pos <= query)
            allowed = jnp.concatenate([allowed] * group, axis=1)
            for g in range(heads // group):
                cols = slice(g * lanes, (g + 1) * lanes)
                rows = q_ref[0, g * group * hd : (g + 1) * group * hd, :]
                q_pad = jnp.concatenate([side_by_side(rows, group, hd), zeros], axis=0)
                s = dot(kv, q_pad, ((1,), (0,))) * scale2
                s = jnp.where(allowed, s, MASKED)
                m_old = m_s[:, cols]
                m_new = jnp.maximum(m_old, jnp.max(s, axis=0, keepdims=True))
                p = jnp.exp2(s - m_new)
                alpha = jnp.exp2(m_old - m_new)
                m_s[:, cols] = m_new
                l_s[:, cols] = l_s[:, cols] * alpha + jnp.sum(p, axis=0, keepdims=True)
                pv = dot(kv_t, p.astype(BF), ((1,), (0,)))
                acc_s[:, cols] = acc_s[:, cols] * alpha + pv[hd:, :]

        return carry

    lax.fori_loop(0, kv_ref.shape[1] // chunk, body, 0)
    total = l_s[...]
    out = acc_s[...] / total
    lse_ref[0] = m_s[...] + jnp.log2(total)
    for h in range(heads):
        out_ref[0, h * hd : (h + 1) * hd, :] = out[:, h * tq : (h + 1) * tq].astype(BF)


def backward_kernel(
    scal, q_ref, kv_ref, lo_ref, out_ref, lse_ref, do_ref, dq_ref, dkv_ref, delta_s, dq_s, *, heads, hd, chunk
):
    w = pl.program_id(0)
    me = scal[0]
    tq = q_ref.shape[2]
    lo_min = scal[1 + w]
    first = me * tq
    scale = 1.0 / math.sqrt(hd)
    scale2 = LOG2E * scale
    group = 2
    lanes = group * tq
    zeros = jnp.zeros((hd, lanes), BF)
    lo = lo_ref[0]
    query = first + lax.broadcasted_iota(jnp.int32, (chunk, tq), 1)
    dq_s[...] = jnp.zeros(dq_s.shape, F32)
    for h in range(heads):
        rows = slice(h * hd, (h + 1) * hd)
        delta_s[:, h * tq : (h + 1) * tq] = jnp.sum(
            out_ref[0, rows, :].astype(F32) * do_ref[0, rows, :].astype(F32), axis=0, keepdims=True
        )
    lane = lax.broadcasted_iota(jnp.int32, (chunk, 2 * hd), 1)

    def body(j, carry):
        base, pos = chunk_pos(me, j, chunk, tq)
        here = pl.ds(pl.multiple_of(j * chunk, chunk), chunk)
        needed = (base < first + tq) & (base + chunk > lo_min)

        @pl.when(jnp.logical_not(needed))
        def _():
            dkv_ref[0, here, :] = jnp.zeros((chunk, 2 * hd), BF)

        @pl.when(needed)
        def _():
            kv = kv_ref[0, here, :]
            kv_t = kv.T
            allowed = (pos >= lo) & (pos <= query)
            allowed = jnp.concatenate([allowed] * group, axis=1)
            dkv = jnp.zeros((chunk, 2 * hd), F32)
            for g in range(heads // group):
                cols = slice(g * lanes, (g + 1) * lanes)
                rows = slice(g * group * hd, (g + 1) * group * hd)
                q_pad = jnp.concatenate([side_by_side(q_ref[0, rows, :], group, hd), zeros], axis=0)
                do_pad = jnp.concatenate([zeros, side_by_side(do_ref[0, rows, :], group, hd)], axis=0)
                s = dot(kv, q_pad, ((1,), (0,))) * scale2
                p = jnp.where(allowed, jnp.exp2(s - lse_ref[0, :, cols]), 0.0)
                dp = dot(kv, do_pad, ((1,), (0,)))
                ds = (p * (dp - delta_s[:, cols])).astype(BF)
                dkv = dkv + dot(ds, q_pad, ((1,), (1,))) * scale + dot(p.astype(BF), do_pad, ((1,), (1,)))
                dq_s[:, cols] = dq_s[:, cols] + dot(kv_t, ds, ((1,), (0,)))[:hd, :]
            dkv_ref[0, here, :] = dkv.astype(BF)

        return carry

    lax.fori_loop(0, kv_ref.shape[1] // chunk, body, 0)
    for h in range(heads):
        dq_ref[0, h * hd : (h + 1) * hd, :] = (dq_s[:, h * tq : (h + 1) * tq] * scale).astype(BF)


def per_window(shape):
    zeros = (0,) * (len(shape) - 1)
    return pl.BlockSpec((1, *shape[1:]), lambda w, scal: (w, *zeros))


def attention_call(kernel, scalars, inputs, outs, scratch, name, flops):
    moved = sum(math.prod(a.shape) * a.dtype.itemsize for a in (*inputs, *outs))
    return pl.pallas_call(
        kernel,
        out_shape=outs,
        grid_spec=pltpu.PrefetchScalarGridSpec(
            num_scalar_prefetch=1,
            grid=(inputs[0].shape[0],),
            in_specs=[per_window(a.shape) for a in inputs],
            out_specs=[per_window(a.shape) for a in outs],
            scratch_shapes=scratch,
        ),
        cost_estimate=pl.CostEstimate(flops=flops, bytes_accessed=moved, transcendentals=0),
        name=name,
    )(scalars, *inputs)


def local(
    tokens,
    attn_gain,
    attn_shift,
    w_query,
    b_query,
    w_keyval,
    b_value,
    w_out,
    b_out,
    mlp_gain,
    mlp_shift,
    w_up,
    b_up,
    w_down,
    b_down,
    doc_lengths,
    cotangent,
):
    tq, windows, width = tokens.shape
    hd = w_keyval.shape[1] // 2
    own_cols = w_query.shape[1]
    seq_size = lax.axis_size("seq")
    cols = own_cols * lax.axis_size("head")
    heads = cols // hd
    seq_total = tq * seq_size * lax.axis_size("head")
    me = lax.axis_index("seq") * lax.axis_size("head") + lax.axis_index("head")
    chunk = min(2 * tq, seq_total)

    core = ("batch", 1)
    head = ("head", 1)
    low = ("seq", 1)
    highs = [("seq", 1 << i) for i in range(1, int(math.log2(seq_size)))]

    def other_half(weight):
        half = weight.shape[0] // 2
        part = lax.dynamic_slice_in_dim(weight, lax.axis_index("batch") * half, half, 0)
        return double([swap(part, head)], core, [0])[0]

    wq_other = other_half(w_query)
    bq_other = swap(b_query, head)
    head_first = bit_of(head) == 0

    def in_order(own, other, dim):
        return jnp.concatenate([jnp.where(head_first, own, other), jnp.where(head_first, other, own)], dim)

    wq_all = in_order(w_query, wq_other, 1)
    bq_all = in_order(b_query, bq_other, 0)
    wo_all = in_order(w_out, other_half(w_out), 0)

    bounds = jnp.cumsum(doc_lengths, axis=1)
    places = me * tq + jnp.arange(tq, dtype=jnp.int32)
    starts = jnp.max(
        jnp.where(bounds[:, :, None] <= places[None, None, :], bounds[:, :, None], 0), axis=1
    )
    scalars = jnp.concatenate([me[None].astype(jnp.int32), starts[:, 0]])
    starts = starts[:, None, :]

    residual = jnp.transpose(tokens, (1, 0, 2)).astype(F32)
    normed = layer_norm(residual, attn_gain, attn_shift).astype(BF)
    value_bias = jnp.concatenate([jnp.zeros((hd,), F32), b_value])
    keyval = (
        jnp.einsum("wtd,dc->wtc", normed, w_keyval, preferred_element_type=F32) + value_bias
    ).astype(BF)

    bits = [*reversed(highs), low, head]

    def gather_blocks(value, order):
        block = value.reshape(value.shape[0], *[1] * len(bits), tq, 2 * hd)
        for step in order:
            block = jnp.concatenate([block, swap(block, step)], 1 + bits.index(step))
        return block.reshape(value.shape[0], seq_total, 2 * hd)

    def open_blocks(value):
        return value.reshape(value.shape[0], *[2] * len(bits), tq, 2 * hd)

    def reduce_block(block, step):
        kept, sent = jnp.split(block, 2, 1 + bits.index(step))
        return add_low(kept, swap(sent, step))

    half_w = windows // 2
    order_a, order_b = [*reversed(highs), low, head], [*reversed(highs), head, low]
    keyval_all = jnp.concatenate(
        [gather_blocks(keyval[:half_w], order_a), gather_blocks(keyval[half_w:], order_b)], 0
    )

    queries = (
        jnp.einsum("do,wtd->wot", wq_all, normed, preferred_element_type=F32) + bq_all[None, :, None]
    ).astype(BF)

    struct = jax.ShapeDtypeStruct
    lanes = heads * tq
    work = 2 * windows * lanes * (seq_total // 4) * hd
    mixed, log_total = attention_call(
        partial(forward_kernel, heads=heads, hd=hd, chunk=chunk),
        scalars,
        (queries, keyval_all, starts),
        (struct((windows, cols, tq), BF), struct((windows, 1, lanes), F32)),
        [pltpu.VMEM((1, lanes), F32), pltpu.VMEM((1, lanes), F32), pltpu.VMEM((hd, lanes), F32)],
        "attend",
        8 * work,
    )

    branch = jnp.einsum("wot,od->wtd", mixed, wo_all, preferred_element_type=F32)
    middle = residual + (branch + b_out)
    inner = layer_norm(middle, mlp_gain, mlp_shift).astype(BF)
    upstream_low = jnp.transpose(cotangent, (1, 0, 2))
    upstream = upstream_low.astype(F32)

    upward = jnp.einsum("wtd,df->wtf", inner, w_up, preferred_element_type=F32) + b_up
    active = jax.nn.gelu(upward, approximate=True).astype(BF)
    grad_active = jnp.einsum("wtd,fd->wtf", upstream_low, w_down, preferred_element_type=F32)
    gelu_back = jax.vjp(partial(jax.nn.gelu, approximate=True), upward)[1]
    grad_upward = gelu_back(grad_active)[0].astype(BF)

    ff = w_up.shape[1]
    cut = 2 * ff // 3
    spans = (0, cut // 2), (cut, (ff - cut) // 2)
    on_first = bit_of(core) == 0

    def columns(array, span, other):
        first, size = span
        start = first + size * (bit_of(core) ^ other)
        return lax.dynamic_slice_in_dim(array, start, size, 2)

    def part_down(span, other):
        return jnp.einsum("wtf,wtd->fd", columns(active, span, other), upstream_low, preferred_element_type=F32)

    def part_up(span, other):
        return jnp.einsum("wtd,wtf->df", inner, columns(grad_upward, span, other), preferred_element_type=F32)

    def part_up_turned(span, other):
        return jnp.einsum("wtf,wtd->fd", columns(grad_upward, span, other), inner, preferred_element_type=F32)

    def own_part(make, span, got):
        return (make(span, 0) + got.astype(F32)).astype(BF)

    got_down = swap(part_down(spans[0], 1).astype(BF), core)
    got_up = swap(part_up(spans[0], 1).astype(BF), core)
    got_mix = swap(jnp.concatenate([part_down(spans[1], 1).astype(BF), part_up_turned(spans[1], 1).astype(BF)], 0), core)
    rows_mix = spans[1][1]
    pieces = [
        own_part(part_down, spans[0], got_down),
        own_part(part_up, spans[0], got_up),
        jnp.concatenate(
            [
                own_part(part_down, spans[1], got_mix[:rows_mix]),
                own_part(part_up_turned, spans[1], got_mix[rows_mix:]),
            ],
            0,
        ),
    ]

    grad_inner = jnp.einsum("wtf,df->wtd", grad_upward, w_up, preferred_element_type=F32)
    norm_back = jax.vjp(layer_norm, middle, mlp_gain, mlp_shift)[1]
    grad_mid_norm, grad_mlp_gain, grad_mlp_shift = norm_back(grad_inner)
    grad_middle = upstream + grad_mid_norm
    grad_branch = grad_middle.astype(BF)
    grad_mixed = jnp.einsum("od,wtd->wot", wo_all, grad_branch, preferred_element_type=F32).astype(BF)

    near, far = highs[0], highs[1:]
    orders = [low, head, near, *far], [head, near, low, *far], [near, low, head, *far]
    last = len(orders[0]) - 1
    groups = [[piece] for piece in pieces]
    dims = [[], [], []]

    def reduce_step(at):
        for i in range(3):
            groups[i], dim = halve(groups[i], orders[i][at])
            dims[i].append(dim)

    def gather_step(at):
        for i in range(3):
            groups[i] = double(groups[i], orders[i][at], dims[i][at][:1])

    groups, grad_mixed = tie(groups, grad_mixed)
    reduce_step(0)
    grad_queries, grad_keyval_all = attention_call(
        partial(backward_kernel, heads=heads, hd=hd, chunk=chunk),
        scalars,
        (queries, keyval_all, starts, mixed, log_total, grad_mixed),
        (struct((windows, cols, tq), BF), struct(keyval_all.shape, BF)),
        [pltpu.VMEM((1, lanes), F32), pltpu.VMEM((hd, lanes), F32)],
        "attend_back",
        20 * work,
    )
    groups, grad_queries, grad_keyval_all, active, grad_upward, mixed, grad_branch = tie(
        groups, grad_queries, grad_keyval_all, active, grad_upward, mixed, grad_branch
    )

    grad_w_out = jnp.einsum("wot,wtd->od", mixed, grad_branch, preferred_element_type=F32).astype(BF)
    grad_w_query = jnp.einsum("wtd,wot->do", normed, grad_queries, preferred_element_type=F32).astype(BF)
    half_d = width // 2
    grad_w_query = jnp.concatenate(
        [
            jnp.concatenate([grad_w_query[:half_d, at : at + own_cols], grad_w_query[half_d:, at : at + own_cols]], 1)
            for at in range(0, cols, own_cols)
        ],
        0,
    )
    square = add_low(
        jnp.where(on_first, grad_w_out, grad_w_query), swap(jnp.where(on_first, grad_w_query, grad_w_out), core)
    )
    result = (
        middle + (jnp.einsum("wtf,fd->wtd", active, w_down, preferred_element_type=F32) + b_down)
    ).astype(BF)
    result = jnp.transpose(result, (1, 0, 2))
    grad_b_up = jnp.sum(grad_upward.astype(F32), axis=(0, 1))
    grad_b_down = jnp.sum(upstream, axis=(0, 1))
    grad_b_out = jnp.sum(grad_branch.astype(F32), axis=(0, 1))
    grad_b_query = jnp.sum(grad_queries.astype(F32), axis=(0, 2))
    vectors = [grad_b_up, grad_b_down, grad_mlp_gain, grad_mlp_shift, grad_b_out, grad_b_query]

    blocks = [open_blocks(grad_keyval_all[:half_w]), open_blocks(grad_keyval_all[half_w:])]
    block_orders = [order_a[::-1], order_b[::-1]]
    groups[0].append(square)
    for at in range(1, last + 1):
        reduce_step(at)
        for step in range(at - 1, at if at < last else len(bits)):
            blocks = [reduce_block(block, order[step]) for block, order in zip(blocks, block_orders)]
        if at == 1:
            groups, blocks, vectors = tie(groups, blocks, vectors)
        elif at == 2:
            groups, blocks, result = tie(groups, blocks, result)
        else:
            groups, blocks = tie(groups, blocks)
    square = groups[0].pop()
    grad_keyval = jnp.concatenate([block.reshape(half_w, tq, 2 * hd) for block in blocks], 0)

    grad_w_keyval = jnp.einsum("wtd,wtc->dc", normed, grad_keyval, preferred_element_type=F32)
    grad_b_value = jnp.sum(grad_keyval[:, :, hd:].astype(F32), axis=(0, 1))
    grad_normed = jnp.einsum("wot,do->wtd", grad_queries, wq_all, preferred_element_type=F32)
    grad_normed = grad_normed + jnp.einsum(
        "wtc,dc->wtd", grad_keyval, w_keyval, preferred_element_type=F32
    )
    first_back = jax.vjp(layer_norm, residual, attn_gain, attn_shift)[1]
    grad_input, grad_attn_gain, grad_attn_shift = first_back(grad_normed)
    grad_tokens = jnp.transpose(grad_middle + grad_input, (1, 0, 2))

    vectors = [*vectors, grad_attn_gain, grad_attn_shift, grad_b_value]
    flat = jnp.concatenate(vectors)
    used = width * 2 * hd + flat.shape[0]
    flat = jnp.pad(flat, (0, (-used) % (32 * 2 * hd)))
    small = jnp.concatenate([grad_w_keyval, flat.reshape(-1, 2 * hd)], 0).astype(BF)

    small_steps = [low, head, *highs]
    for at in range(last, -1, -1):
        gather_step(at)
        if at == last:
            (small,), small_dim = halve([small], core)
            square = add_low(square, swap(square, low))
        else:
            for step in small_steps[:2]:
                small = add_low(small, swap(small, step))
            small_steps = small_steps[2:]
            if at:
                (square,) = double([square], orders[0][at + 1], dims[0][at + 1][1:])
            else:
                (small,) = double([small], core, small_dim)
                other = swap(square, core)
        if at == last - 1:
            groups, small, square, grad_tokens = tie(groups, small, square, grad_tokens)
        elif at:
            groups, small, square = tie(groups, small, square)

    down, up, mix = (group[0] for group in groups)
    got_down, got_up, got_mix = swap(down, core), swap(up, core), swap(mix, core)

    def both(own, got, dim):
        own, got = own.astype(F32), got.astype(F32)
        return [jnp.where(on_first, own, got), jnp.where(on_first, got, own)]

    grad_w_down = jnp.concatenate(both(down, got_down, 0) + both(mix[:rows_mix], got_mix[:rows_mix], 0), 0)
    grad_w_up = jnp.concatenate(both(up, got_up, 1) + both(mix[rows_mix:].T, got_mix[rows_mix:].T, 1), 1)
    grad_w_out = jnp.where(on_first, square, other).astype(F32)
    grad_w_query = jnp.where(on_first, other, square).astype(F32)
    grad_w_query = jnp.concatenate([grad_w_query[:, :own_cols], grad_w_query[:, own_cols:]], 0)

    small = small.astype(F32)
    flat = small[width:].reshape(-1)
    sums, at = [], 0
    for vector in vectors:
        sums.append(flat[at : at + vector.shape[0]])
        at += vector.shape[0]
    b_up_sum, b_down_sum, mlp_gain_sum, mlp_shift_sum, b_out_sum, b_query_sum, gain_sum, shift_sum, b_value_sum = sums

    return (
        result,
        grad_tokens,
        gain_sum,
        shift_sum,
        grad_w_query,
        lax.dynamic_slice_in_dim(b_query_sum, lax.axis_index("head") * own_cols, own_cols, 0),
        small[:width],
        b_value_sum,
        grad_w_out,
        b_out_sum,
        mlp_gain_sum,
        mlp_shift_sum,
        grad_w_up,
        b_up_sum,
        grad_w_down,
        b_down_sum,
    )


def solution(mesh):
    return jax.shard_map(
        local,
        mesh=mesh,
        in_specs=(
            P(("seq", "head"), "batch", None),
            P(),
            P(),
            P(None, "head"),
            P("head"),
            P(),
            P(),
            P("head", None),
            P(),
            P(),
            P(),
            P(),
            P(),
            P(),
            P(),
            P("batch", None),
            P(("seq", "head"), "batch", None),
        ),
        out_specs=(
            P(("seq", "head"), "batch", None),
            P(("seq", "head"), "batch", None),
            P(),
            P(),
            P(None, "head"),
            P("head"),
            P(),
            P(),
            P("head", None),
            P(),
            P(),
            P(),
            P(),
            P(),
            P(),
            P(),
        ),
        check_vma=False,
    )
```

```python
from functools import partial
import math

import jax
import jax.numpy as jnp
from jax import lax
from jax.experimental import pallas as pl
from jax.experimental.pallas import tpu as pltpu
from jax.sharding import PartitionSpec as P

EPSILON = 1e-05
MASKED = -1e30
BF = jnp.bfloat16
F32 = jnp.float32
LOG2E = math.log2(math.e)


def layer_norm(inputs, norm_gain, norm_shift):
    center = inputs - jnp.mean(inputs, axis=-1, keepdims=True)
    spread = jnp.mean(center * center, axis=-1, keepdims=True)
    return center * lax.rsqrt(spread + EPSILON) * norm_gain + norm_shift


def swap(value, step):
    axis, flip = step
    size = lax.axis_size(axis)
    return lax.ppermute(value, axis, [(i, i ^ flip) for i in range(size)])


def bit_of(step):
    axis, flip = step
    return (lax.axis_index(axis) // flip) % 2


def split_dim(shape):
    if (shape[0] // 2) % 8 == 0:
        return 0
    return 1


def add_low(kept, got):
    return (kept.astype(F32) + got.astype(F32)).astype(kept.dtype)


def tie(*trees):
    leaves, shape = jax.tree.flatten(trees)
    return jax.tree.unflatten(shape, lax.optimization_barrier(leaves))


def halve(arrays, step):
    bit = bit_of(step)
    dims = [split_dim(a.shape) for a in arrays]
    halves = [a.shape[d] // 2 for a, d in zip(arrays, dims)]
    sent = [lax.dynamic_slice_in_dim(a, (1 - bit) * h, h, d) for a, h, d in zip(arrays, halves, dims)]
    kept = [lax.dynamic_slice_in_dim(a, bit * h, h, d) for a, h, d in zip(arrays, halves, dims)]
    return [add_low(k, g) for k, g in zip(kept, swap_all(sent, step))], dims


def swap_all(arrays, step):
    if len({a.shape[1] for a in arrays}) > 1:
        return [swap(a, step) for a in arrays]
    got = swap(jnp.concatenate(arrays, 0) if len(arrays) > 1 else arrays[0], step)
    at, out = 0, []
    for a in arrays:
        out.append(got[at : at + a.shape[0]])
        at += a.shape[0]
    return out


def double(arrays, step, dims):
    got = swap_all(arrays, step)
    first = bit_of(step) == 0
    return [
        jnp.concatenate([jnp.where(first, a, g), jnp.where(first, g, a)], d) for a, g, d in zip(arrays, got, dims)
    ]


def dot(a, b, dims):
    return lax.dot_general(a, b, (dims, ((), ())), preferred_element_type=F32)


def side_by_side(rows, heads, hd):
    return jnp.concatenate([rows[h * hd : (h + 1) * hd, :] for h in range(heads)], axis=1)


def chunk_pos(me, j, chunk, tq):
    base = ((me * tq) // chunk) ^ j
    rows = lax.broadcasted_iota(jnp.int32, (chunk, tq), 0)
    return base * chunk, base * chunk + (rows ^ ((me * tq) % chunk))


def forward_kernel(scal, q_ref, kv_ref, lo_ref, out_ref, lse_ref, m_s, l_s, acc_s, *, heads, hd, chunk):
    w = pl.program_id(0)
    me = scal[0]
    tq = q_ref.shape[2]
    lo_min = scal[1 + w]
    first = me * tq
    scale2 = LOG2E / math.sqrt(hd)
    group = 2
    lanes = group * tq
    zeros = jnp.zeros((hd, lanes), BF)
    lo = lo_ref[0]
    query = first + lax.broadcasted_iota(jnp.int32, (chunk, tq), 1)
    m_s[...] = jnp.full(m_s.shape, MASKED, F32)
    l_s[...] = jnp.zeros(l_s.shape, F32)
    acc_s[...] = jnp.zeros(acc_s.shape, F32)

    def body(j, carry):
        base, pos = chunk_pos(me, j, chunk, tq)

        @pl.when((base < first + tq) & (base + chunk > lo_min))
        def _():
            kv = kv_ref[0, pl.ds(pl.multiple_of(j * chunk, chunk), chunk), :]
            kv_t = kv.T
            allowed = (pos >= lo) & (pos <= query)
            allowed = jnp.concatenate([allowed] * group, axis=1)
            for g in range(heads // group):
                cols = slice(g * lanes, (g + 1) * lanes)
                rows = q_ref[0, g * group * hd : (g + 1) * group * hd, :]
                q_pad = jnp.concatenate([side_by_side(rows, group, hd), zeros], axis=0)
                s = dot(kv, q_pad, ((1,), (0,))) * scale2
                s = jnp.where(allowed, s, MASKED)
                m_old = m_s[:, cols]
                m_new = jnp.maximum(m_old, jnp.max(s, axis=0, keepdims=True))
                p = jnp.exp2(s - m_new)
                alpha = jnp.exp2(m_old - m_new)
                m_s[:, cols] = m_new
                l_s[:, cols] = l_s[:, cols] * alpha + jnp.sum(p, axis=0, keepdims=True)
                pv = dot(kv_t, p.astype(BF), ((1,), (0,)))
                acc_s[:, cols] = acc_s[:, cols] * alpha + pv[hd:, :]

        return carry

    lax.fori_loop(0, kv_ref.shape[1] // chunk, body, 0)
    total = l_s[...]
    out = acc_s[...] / total
    lse_ref[0] = m_s[...] + jnp.log2(total)
    for h in range(heads):
        out_ref[0, h * hd : (h + 1) * hd, :] = out[:, h * tq : (h + 1) * tq].astype(BF)


def backward_kernel(
    scal, q_ref, kv_ref, lo_ref, out_ref, lse_ref, do_ref, dq_ref, *refs, heads, hd, chunk
):
    *dkv_refs, delta_s, dq_s = refs
    w = pl.program_id(0)
    me = scal[0]
    tq = q_ref.shape[2]
    lo_min = scal[1 + w]
    first = me * tq
    scale = 1.0 / math.sqrt(hd)
    scale2 = LOG2E * scale
    group = 2
    lanes = group * tq
    zeros = jnp.zeros((hd, lanes), BF)
    lo = lo_ref[0]
    query = first + lax.broadcasted_iota(jnp.int32, (chunk, tq), 1)
    dq_s[...] = jnp.zeros(dq_s.shape, F32)
    for h in range(heads):
        rows = slice(h * hd, (h + 1) * hd)
        delta_s[:, h * tq : (h + 1) * tq] = jnp.sum(
            out_ref[0, rows, :].astype(F32) * do_ref[0, rows, :].astype(F32), axis=0, keepdims=True
        )
    lane = lax.broadcasted_iota(jnp.int32, (chunk, 2 * hd), 1)

    def body(j, carry):
        base, pos = chunk_pos(me, j, chunk, tq)
        here = pl.ds(pl.multiple_of(j * chunk, chunk), chunk)
        needed = (base < first + tq) & (base + chunk > lo_min)

        def store(value):
            kept_a, sent_a, kept_b, sent_b = dkv_refs

            @pl.when(w < pl.num_programs(0) // 2)
            def _():
                rows = pl.ds(pl.multiple_of(j * tq, tq), tq)
                kept_a[0, rows, :] = value[:tq]
                sent_a[0, rows, :] = value[tq:]

            @pl.when(w >= pl.num_programs(0) // 2)
            def _():
                rows = pl.ds(pl.multiple_of((j // 2) * chunk, chunk), chunk)

                @pl.when(j % 2 == 0)
                def _():
                    kept_b[0, rows, :] = value

                @pl.when(j % 2 == 1)
                def _():
                    sent_b[0, rows, :] = value

        @pl.when(jnp.logical_not(needed))
        def _():
            store(jnp.zeros((chunk, 2 * hd), BF))

        @pl.when(needed)
        def _():
            kv = kv_ref[0, here, :]
            kv_t = kv.T
            allowed = (pos >= lo) & (pos <= query)
            allowed = jnp.concatenate([allowed] * group, axis=1)
            dkv = jnp.zeros((chunk, 2 * hd), F32)
            for g in range(heads // group):
                cols = slice(g * lanes, (g + 1) * lanes)
                rows = slice(g * group * hd, (g + 1) * group * hd)
                q_pad = jnp.concatenate([side_by_side(q_ref[0, rows, :], group, hd), zeros], axis=0)
                do_pad = jnp.concatenate([zeros, side_by_side(do_ref[0, rows, :], group, hd)], axis=0)
                s = dot(kv, q_pad, ((1,), (0,))) * scale2
                p = jnp.where(allowed, jnp.exp2(s - lse_ref[0, :, cols]), 0.0)
                dp = dot(kv, do_pad, ((1,), (0,)))
                ds = (p * (dp - delta_s[:, cols])).astype(BF)
                dkv = dkv + dot(ds, q_pad, ((1,), (1,))) * scale + dot(p.astype(BF), do_pad, ((1,), (1,)))
                dq_s[:, cols] = dq_s[:, cols] + dot(kv_t, ds, ((1,), (0,)))[:hd, :]
            store(dkv.astype(BF))

        return carry

    lax.fori_loop(0, kv_ref.shape[1] // chunk, body, 0)
    for h in range(heads):
        dq_ref[0, h * hd : (h + 1) * hd, :] = (dq_s[:, h * tq : (h + 1) * tq] * scale).astype(BF)


def assemble_down(core, own, got, own_mix, got_mix, out, *, wide, rows):
    i = pl.program_id(0)
    step, width = out.shape
    first = own.shape[0] // step
    second = rows // step

    def write(mine, array, at):
        @pl.when(mine & (i < 2 * first))
        def _():
            out[...] = array[pl.ds(pl.multiple_of(at * step, step), step), :].astype(F32)

    def write_mix(mine, array, at):
        @pl.when(mine & (i >= 2 * first))
        def _():
            for c in range(width // wide):
                here = pl.ds(pl.multiple_of(c * rows + at * step, step), step)
                out[:, c * wide : (c + 1) * wide] = array[here, :].astype(F32)

    late = i - 2 * first
    from_second = jnp.where(late >= 0, late // second, i // first)
    mine = from_second == core[0]
    at = jnp.where(late >= 0, late % second, i % first)
    at_first, at_mix = jnp.minimum(at, first - 1), jnp.minimum(at, second - 1)
    write(mine, own, at_first)
    write(jnp.logical_not(mine), got, at_first)
    write_mix(mine, own_mix, at_mix)
    write_mix(jnp.logical_not(mine), got_mix, at_mix)


def assemble_up(core, own, got, own_mix, got_mix, out, *, wide, skip):
    i = pl.program_id(0)
    height, step = out.shape
    first = own.shape[1] // step

    def write(mine, array):
        for at in range(first):
            @pl.when(mine & (i < 2 * first) & (i % first == at))
            def _():
                out[...] = array[:, at * step : (at + 1) * step].astype(F32)

    def write_mix(mine, array):
        @pl.when(mine & (i >= 2 * first))
        def _():
            for c in range(step // wide):
                out[:, c * wide : (c + 1) * wide] = array[skip + c * height : skip + (c + 1) * height, :].astype(F32)

    late = i - 2 * first
    mine = jnp.where(late >= 0, late, i // first) == core[0]
    write(mine, own)
    write(jnp.logical_not(mine), got)
    write_mix(mine, own_mix)
    write_mix(jnp.logical_not(mine), got_mix)


def assemble(kernel, core, arrays, shape, block, name):
    rows = block[0] != shape[0]
    return pl.pallas_call(
        kernel,
        out_shape=jax.ShapeDtypeStruct(shape, F32),
        grid_spec=pltpu.PrefetchScalarGridSpec(
            num_scalar_prefetch=1,
            grid=(shape[0] // block[0] * (shape[1] // block[1]),),
            in_specs=[pl.BlockSpec(memory_space=pltpu.VMEM) for _ in arrays],
            out_specs=pl.BlockSpec(block, (lambda i, core: (i, 0)) if rows else (lambda i, core: (0, i))),
        ),
        compiler_params=pltpu.CompilerParams(vmem_limit_bytes=24 << 20),
        cost_estimate=pl.CostEstimate(
            flops=0, bytes_accessed=4 * shape[0] * shape[1] + sum(2 * a.size for a in arrays), transcendentals=0
        ),
        name=name,
    )(core, *arrays)


def per_window(shape):
    zeros = (0,) * (len(shape) - 1)
    return pl.BlockSpec((1, *shape[1:]), lambda w, scal: (w, *zeros))


def half_windows(shape, late):
    zeros = (0,) * (len(shape) - 1)
    if late:
        return pl.BlockSpec((1, *shape[1:]), lambda w, scal: (jnp.maximum(w - shape[0], 0), *zeros))
    return pl.BlockSpec((1, *shape[1:]), lambda w, scal: (jnp.minimum(w, shape[0] - 1), *zeros))


def attention_call(kernel, scalars, inputs, outs, scratch, name, flops, halves=0):
    vmem = (12 << 20) + 10 * math.prod(inputs[1].shape[1:]) * inputs[1].dtype.itemsize
    moved = sum(math.prod(a.shape) * a.dtype.itemsize for a in (*inputs, *outs))
    return pl.pallas_call(
        kernel,
        out_shape=outs,
        grid_spec=pltpu.PrefetchScalarGridSpec(
            num_scalar_prefetch=1,
            grid=(inputs[0].shape[0],),
            in_specs=[per_window(a.shape) for a in inputs],
            out_specs=[per_window(a.shape) for a in outs[: len(outs) - halves]]
            + [half_windows(a.shape, i >= halves // 2) for i, a in enumerate(outs[len(outs) - halves :])],
            scratch_shapes=scratch,
        ),
        compiler_params=pltpu.CompilerParams(vmem_limit_bytes=vmem),
        cost_estimate=pl.CostEstimate(flops=flops, bytes_accessed=moved, transcendentals=0),
        name=name,
    )(scalars, *inputs)


def local(
    tokens,
    attn_gain,
    attn_shift,
    w_query,
    b_query,
    w_keyval,
    b_value,
    w_out,
    b_out,
    mlp_gain,
    mlp_shift,
    w_up,
    b_up,
    w_down,
    b_down,
    doc_lengths,
    cotangent,
):
    tq, windows, width = tokens.shape
    hd = w_keyval.shape[1] // 2
    own_cols = w_query.shape[1]
    seq_size = lax.axis_size("seq")
    cols = own_cols * lax.axis_size("head")
    heads = cols // hd
    seq_total = tq * seq_size * lax.axis_size("head")
    me = lax.axis_index("seq") * lax.axis_size("head") + lax.axis_index("head")
    chunk = min(2 * tq, seq_total)

    core = ("batch", 1)
    head = ("head", 1)
    low = ("seq", 1)
    highs = [("seq", 1 << i) for i in range(1, int(math.log2(seq_size)))]

    def other_half(weight):
        half = weight.shape[0] // 2
        part = lax.dynamic_slice_in_dim(weight, lax.axis_index("batch") * half, half, 0)
        return double([swap(part, head)], core, [0])[0]

    wq_other = other_half(w_query)
    bq_other = swap(b_query, head)
    head_first = bit_of(head) == 0

    def in_order(own, other, dim):
        return jnp.concatenate([jnp.where(head_first, own, other), jnp.where(head_first, other, own)], dim)

    wq_all = in_order(w_query, wq_other, 1)
    bq_all = in_order(b_query, bq_other, 0)
    wo_all = in_order(w_out, other_half(w_out), 0)

    bounds = jnp.cumsum(doc_lengths, axis=1)
    places = me * tq + jnp.arange(tq, dtype=jnp.int32)
    starts = jnp.max(
        jnp.where(bounds[:, :, None] <= places[None, None, :], bounds[:, :, None], 0), axis=1
    )
    scalars = jnp.concatenate([me[None].astype(jnp.int32), starts[:, 0]])
    starts = starts[:, None, :]

    residual = jnp.transpose(tokens, (1, 0, 2)).astype(F32)
    normed = layer_norm(residual, attn_gain, attn_shift).astype(BF)
    value_bias = jnp.concatenate([jnp.zeros((hd,), F32), b_value])
    keyval = (
        jnp.einsum("wtd,dc->wtc", normed, w_keyval, preferred_element_type=F32) + value_bias
    ).astype(BF)

    bits = [*reversed(highs), low, head]

    def gather_blocks(value, order):
        block = value.reshape(value.shape[0], *[1] * len(bits), tq, 2 * hd)
        for step in order:
            block = jnp.concatenate([block, swap(block, step)], 1 + bits.index(step))
        return block.reshape(value.shape[0], seq_total, 2 * hd)

    def reduce_block(block, step):
        kept, sent = jnp.split(block, 2, 1 + bits.index(step))
        return add_low(kept, swap(sent, step))

    half_w = windows // 2
    order_a, order_b = [*reversed(highs), low, head], [*reversed(highs), head, low]
    keyval_all = jnp.concatenate(
        [gather_blocks(keyval[:half_w], order_a), gather_blocks(keyval[half_w:], order_b)], 0
    )

    queries = (
        jnp.einsum("do,wtd->wot", wq_all, normed, preferred_element_type=F32) + bq_all[None, :, None]
    ).astype(BF)

    struct = jax.ShapeDtypeStruct
    lanes = heads * tq
    work = 2 * windows * lanes * (seq_total // 4) * hd
    mixed, log_total = attention_call(
        partial(forward_kernel, heads=heads, hd=hd, chunk=chunk),
        scalars,
        (queries, keyval_all, starts),
        (struct((windows, cols, tq), BF), struct((windows, 1, lanes), F32)),
        [pltpu.VMEM((1, lanes), F32), pltpu.VMEM((1, lanes), F32), pltpu.VMEM((hd, lanes), F32)],
        "attend",
        8 * work,
    )

    branch = jnp.einsum("wot,od->wtd", mixed, wo_all, preferred_element_type=F32)
    middle = residual + (branch + b_out)
    inner = layer_norm(middle, mlp_gain, mlp_shift).astype(BF)
    upstream_low = jnp.transpose(cotangent, (1, 0, 2))
    upstream = upstream_low.astype(F32)

    upward = jnp.einsum("wtd,df->wtf", inner, w_up, preferred_element_type=F32) + b_up
    active = jax.nn.gelu(upward, approximate=True).astype(BF)
    grad_active = jnp.einsum("wtd,fd->wtf", upstream_low, w_down, preferred_element_type=F32)
    gelu_back = jax.vjp(partial(jax.nn.gelu, approximate=True), upward)[1]
    grad_upward = gelu_back(grad_active)[0].astype(BF)

    ff = w_up.shape[1]
    cut = 2 * ff // 3
    spans = (0, cut // 2), (cut, (ff - cut) // 2)
    on_first = bit_of(core) == 0

    def columns(array, span, other):
        first, size = span
        start = first + size * (bit_of(core) ^ other)
        return lax.dynamic_slice_in_dim(array, start, size, 2)

    def part_down(span, other):
        return jnp.einsum("wtf,wtd->fd", columns(active, span, other), upstream_low, preferred_element_type=F32)

    def part_up(span, other):
        return jnp.einsum("wtd,wtf->df", inner, columns(grad_upward, span, other), preferred_element_type=F32)

    def own_part(make, span, got):
        return (make(span, 0) + got.astype(F32)).astype(BF)

    wide = math.gcd(spans[1][1], width)

    def stack(array):
        return jnp.concatenate([array[:, at : at + wide] for at in range(0, array.shape[1], wide)], 0)

    def unstack(array, rows):
        return jnp.concatenate([array[at : at + rows] for at in range(0, array.shape[0], rows)], 1)

    got_down = swap(part_down(spans[0], 1).astype(BF), core)
    got_up = swap(part_up(spans[0], 1).astype(BF), core)
    got_mix = swap(
        jnp.concatenate([stack(part_down(spans[1], 1).astype(BF)), stack(part_up(spans[1], 1).astype(BF))], 0), core
    )
    rows_mix = spans[1][1]
    rows_down = rows_mix * (width // wide)
    pieces = [
        own_part(part_down, spans[0], got_down),
        own_part(part_up, spans[0], got_up),
        jnp.concatenate(
            [
                stack(own_part(part_down, spans[1], unstack(got_mix[:rows_down], rows_mix))),
                stack(own_part(part_up, spans[1], unstack(got_mix[rows_down:], width))),
            ],
            0,
        ),
    ]

    grad_inner = jnp.einsum("wtf,df->wtd", grad_upward, w_up, preferred_element_type=F32)
    norm_back = jax.vjp(layer_norm, middle, mlp_gain, mlp_shift)[1]
    grad_mid_norm, grad_mlp_gain, grad_mlp_shift = norm_back(grad_inner)
    grad_middle = upstream + grad_mid_norm
    grad_branch = grad_middle.astype(BF)
    grad_mixed = jnp.einsum("od,wtd->wot", wo_all, grad_branch, preferred_element_type=F32).astype(BF)

    own_rows = own_cols // 2

    def core_halves(array):
        array = array.reshape(cols // own_cols, 2, own_rows, width)
        sent = lax.dynamic_index_in_dim(array, 1 - bit_of(core), 1, False)
        kept = lax.dynamic_index_in_dim(array, bit_of(core), 1, False)
        return add_low(kept, swap(sent, core))

    grad_w_out = jnp.einsum("wot,wtd->od", mixed, grad_branch, preferred_element_type=F32).astype(BF)
    out_half = core_halves(grad_w_out)
    out_half = jnp.concatenate([stack(out_half[h]) for h in range(cols // own_cols)], 0)

    near, far = highs[0], highs[1:]
    orders = [near, low, head, *far], [low, head, near, *far], [head, near, low, *far]
    last = len(orders[0]) - 1
    groups = [[pieces[0]], [pieces[1]], [pieces[2], out_half]]
    dims = [[], [], []]

    def reduce_step(at):
        for i in range(3):
            groups[i], dim = halve(groups[i], orders[i][at])
            dims[i].append(dim)

    groups, grad_mixed = tie(groups, grad_mixed)
    reduce_step(0)
    half_keys = struct((half_w, seq_total // 2, 2 * hd), BF)
    grad_queries, *grad_keys = attention_call(
        partial(backward_kernel, heads=heads, hd=hd, chunk=chunk),
        scalars,
        (queries, keyval_all, starts, mixed, log_total, grad_mixed),
        (struct((windows, cols, tq), BF), *[half_keys] * 4),
        [pltpu.VMEM((1, lanes), F32), pltpu.VMEM((hd, lanes), F32)],
        "attend_back",
        20 * work,
        4,
    )
    groups, grad_queries, grad_keys = tie(groups, grad_queries, grad_keys)

    def open_blocks(value, step):
        sides = [1 if other == step else 2 for other in bits]
        return value.reshape(half_w, *sides, tq, 2 * hd)

    def part_query(other):
        half = width // 2
        rows = lax.dynamic_slice_in_dim(normed, half * (bit_of(core) ^ other), half, 2)
        return jnp.einsum("wtd,wot->do", rows, later_queries, preferred_element_type=F32)

    kept_a, sent_a, kept_b, sent_b = grad_keys
    reduce_step(1)
    blocks = [add_low(kept_a, swap(sent_a, head)), add_low(kept_b, swap(sent_b, low))]
    blocks = [open_blocks(blocks[0], head), open_blocks(blocks[1], low)]
    groups, blocks, later_queries = tie(groups, blocks, grad_queries)

    reduce_step(2)
    blocks = [reduce_block(blocks[0], low), reduce_block(blocks[1], head)]
    sent_query = part_query(1).astype(BF)
    groups, blocks, sent_query, active, grad_upward, grad_branch, upstream, later_queries = tie(
        groups, blocks, sent_query, active, grad_upward, grad_branch, upstream, later_queries
    )

    for step in far[:-1]:
        groups = [[add_low(a, g) for a, g in zip(group, swap_all(group, step))] for group in groups]
    far_got = [swap_all(group, far[-1]) for group in groups]
    blocks = reduce_block(jnp.concatenate(blocks, 0), near)
    got_query = swap(sent_query, core)
    query_half = (part_query(0) + got_query.astype(F32)).astype(BF)
    blocks, query_half, active, grad_upward, grad_branch, upstream, later_queries = tie(
        blocks, query_half, active, grad_upward, grad_branch, upstream, later_queries
    )

    for step in far:
        blocks = reduce_block(blocks, step)
    own_head = lax.axis_index("head")
    sent = lax.dynamic_slice_in_dim(query_half, own_cols * (1 - own_head), own_cols, 1)
    kept = lax.dynamic_slice_in_dim(query_half, own_cols * own_head, own_cols, 1)
    query_half = add_low(kept, swap(sent, head))
    result = (
        middle + (jnp.einsum("wtf,fd->wtd", active, w_down, preferred_element_type=F32) + b_down)
    ).astype(BF)
    result = jnp.transpose(result, (1, 0, 2))
    grad_b_up = jnp.sum(grad_upward.astype(F32), axis=(0, 1))
    grad_b_down = jnp.sum(upstream, axis=(0, 1))
    grad_b_out = jnp.sum(grad_branch.astype(F32), axis=(0, 1))
    grad_b_query = jnp.sum(later_queries.astype(F32), axis=(0, 2))
    vectors = [grad_b_up, grad_b_down, grad_mlp_gain, grad_mlp_shift, grad_b_out, grad_b_query]
    blocks, query_half, result, vectors = tie(blocks, query_half, result, vectors)
    grad_keyval = blocks.reshape(windows, tq, 2 * hd)

    grad_w_keyval = jnp.einsum("wtd,wtc->dc", normed, grad_keyval, preferred_element_type=F32)
    grad_b_value = jnp.sum(grad_keyval[:, :, hd:].astype(F32), axis=(0, 1))
    grad_normed = jnp.einsum("wot,do->wtd", grad_queries, wq_all, preferred_element_type=F32)
    grad_normed = grad_normed + jnp.einsum(
        "wtc,dc->wtd", grad_keyval, w_keyval, preferred_element_type=F32
    )
    first_back = jax.vjp(layer_norm, residual, attn_gain, attn_shift)[1]
    grad_input, grad_attn_gain, grad_attn_shift = first_back(grad_normed)
    grad_tokens = jnp.transpose(grad_middle + grad_input, (1, 0, 2))

    def rows_of(vector):
        vector = jnp.pad(vector.astype(F32), (0, (-vector.shape[0]) % width))
        return [vector[at : at + width] for at in range(0, vector.shape[0], width)]

    vectors = [*vectors, grad_attn_gain, grad_attn_shift, grad_b_value]
    rows = [row for vector in vectors for row in rows_of(vector)]
    tall = -(-len(rows) // 16) * 16
    place = lax.broadcasted_iota(jnp.int32, (tall, width), 0)
    packed = jnp.zeros((tall, width), F32)
    for at, row in enumerate(rows):
        packed = jnp.where(place == at, row[None, :], packed)
    small = jnp.concatenate([grad_w_keyval, *[packed[:, at : at + 2 * hd] for at in range(0, width, 2 * hd)]], 0)
    small = small.astype(BF)

    def stack_small(array):
        count = wide // array.shape[1]
        tall = array.shape[0] // count
        return jnp.concatenate([array[at : at + tall] for at in range(0, array.shape[0], tall)], 1)

    def unstack_small(array):
        return jnp.concatenate([array[:, at : at + 2 * hd] for at in range(0, array.shape[1], 2 * hd)], 0)

    (small,), small_dim = halve([small], core)
    small = stack_small(small)
    far_got, small, query_half, grad_tokens = tie(far_got, small, query_half, grad_tokens)
    groups = [[add_low(a, g) for a, g in zip(group, got)] for group, got in zip(groups, far_got)]
    groups, small = tie(groups, small)

    def gather_step(at):
        for i in range(2):
            groups[i] = double(groups[i], orders[i][at], dims[i][at][: len(groups[i])])
        step = orders[2][at]
        *got, small_got = swap_all([*groups[2], small], step)
        lower = bit_of(step) == 0
        groups[2] = [
            jnp.concatenate([jnp.where(lower, a, g), jnp.where(lower, g, a)], d)
            for a, g, d in zip(groups[2], got, dims[2][at])
        ]
        return add_low(small, small_got)

    small = gather_step(2)
    (query_half,), query_dim = halve([query_half], low)
    groups, small, query_half, grad_tokens = tie(groups, small, query_half, grad_tokens)

    small = gather_step(1)
    query_half = add_low(query_half, swap(query_half, near))
    groups, small, query_half = tie(groups, small, query_half)

    out_half = groups[2].pop()
    small = gather_step(0)
    out_other = swap(out_half, core)
    for step in far:
        query_half = add_low(query_half, swap(query_half, step))
    groups, small, query_half, out_other = tie(groups, small, query_half, out_other)

    (down,), (up,), (mix,) = groups
    got_down, got_mix, got_up = swap(down, core), swap(mix, core), swap(up, core)
    (query_half,) = double([query_half], low, query_dim)
    for step in far:
        small = add_low(small, swap(small, step))
    where = lax.axis_index("batch")[None].astype(jnp.int32)
    grad_w_down = assemble(
        partial(assemble_down, wide=wide, rows=rows_mix), where, (down, got_down, mix, got_mix), (ff, width), (rows_mix // 2, width), "down"
    )
    grad_w_up = assemble(
        partial(assemble_up, wide=wide, skip=rows_down), where, (up, got_up, mix, got_mix), (width, ff), (width, rows_mix), "up"
    )

    def both(own, other, dim):
        own, other = own.astype(F32), other.astype(F32)
        return [jnp.where(on_first, own, other), jnp.where(on_first, other, own)]

    out_half, out_other = unstack(out_half, own_rows), unstack(out_other, own_rows)
    query_other = swap(query_half, core)
    grad_w_out = jnp.concatenate(both(out_half, out_other, 0), 0)
    grad_w_query = jnp.concatenate(both(query_half, query_other, 0), 0)

    (small,) = double([unstack_small(small)], core, small_dim)
    small = small.astype(F32)
    grad_w_keyval, packed = small[:width], small[width:]
    packed = jnp.concatenate([packed[at : at + tall] for at in range(0, packed.shape[0], tall)], 1)
    sums, at = [], 0
    for vector in vectors:
        count = -(-vector.shape[0] // width)
        sums.append(packed[at : at + count].reshape(-1)[: vector.shape[0]])
        at += count
    b_up_sum, b_down_sum, mlp_gain_sum, mlp_shift_sum, b_out_sum, b_query_sum, gain_sum, shift_sum, b_value_sum = sums

    return (
        result,
        grad_tokens,
        gain_sum,
        shift_sum,
        grad_w_query,
        lax.dynamic_slice_in_dim(b_query_sum, lax.axis_index("head") * own_cols, own_cols, 0),
        grad_w_keyval,
        b_value_sum,
        grad_w_out,
        b_out_sum,
        mlp_gain_sum,
        mlp_shift_sum,
        grad_w_up,
        b_up_sum,
        grad_w_down,
        b_down_sum,
    )


def solution(mesh):
    return jax.shard_map(
        local,
        mesh=mesh,
        in_specs=(
            P(("seq", "head"), "batch", None),
            P(),
            P(),
            P(None, "head"),
            P("head"),
            P(),
            P(),
            P("head", None),
            P(),
            P(),
            P(),
            P(),
            P(),
            P(),
            P(),
            P("batch", None),
            P(("seq", "head"), "batch", None),
        ),
        out_specs=(
            P(("seq", "head"), "batch", None),
            P(("seq", "head"), "batch", None),
            P(),
            P(),
            P(None, "head"),
            P("head"),
            P(),
            P(),
            P("head", None),
            P(),
            P(),
            P(),
            P(),
            P(),
            P(),
            P(),
        ),
        check_vma=False,
    )
```

```python
from functools import partial
import math

import jax
import jax.numpy as jnp
from jax import lax
from jax.experimental import pallas as pl
from jax.experimental.pallas import tpu as pltpu
from jax.sharding import PartitionSpec as P

EPSILON = 1e-05
MASKED = -1e30
BF = jnp.bfloat16
F32 = jnp.float32
LOG2E = math.log2(math.e)


def layer_norm(inputs, norm_gain, norm_shift):
    center = inputs - jnp.mean(inputs, axis=-1, keepdims=True)
    spread = jnp.mean(center * center, axis=-1, keepdims=True)
    return center * lax.rsqrt(spread + EPSILON) * norm_gain + norm_shift


def swap(value, step):
    axis, flip = step
    size = lax.axis_size(axis)
    return lax.ppermute(value, axis, [(i, i ^ flip) for i in range(size)])


def bit_of(step):
    axis, flip = step
    return (lax.axis_index(axis) // flip) % 2


def split_dim(shape):
    if (shape[0] // 2) % 8 == 0:
        return 0
    return 1


def add_low(kept, got):
    return (kept.astype(F32) + got.astype(F32)).astype(kept.dtype)


def tie(*trees):
    leaves, shape = jax.tree.flatten(trees)
    return jax.tree.unflatten(shape, lax.optimization_barrier(leaves))


def halve(arrays, step):
    bit = bit_of(step)
    dims = [split_dim(a.shape) for a in arrays]
    halves = [a.shape[d] // 2 for a, d in zip(arrays, dims)]
    sent = [lax.dynamic_slice_in_dim(a, (1 - bit) * h, h, d) for a, h, d in zip(arrays, halves, dims)]
    kept = [lax.dynamic_slice_in_dim(a, bit * h, h, d) for a, h, d in zip(arrays, halves, dims)]
    return [add_low(k, g) for k, g in zip(kept, swap_all(sent, step))], dims


def swap_all(arrays, step):
    if len({a.shape[1] for a in arrays}) > 1:
        return [swap(a, step) for a in arrays]
    got = swap(jnp.concatenate(arrays, 0) if len(arrays) > 1 else arrays[0], step)
    at, out = 0, []
    for a in arrays:
        out.append(got[at : at + a.shape[0]])
        at += a.shape[0]
    return out


def double(arrays, step, dims):
    got = swap_all(arrays, step)
    first = bit_of(step) == 0
    return [
        jnp.concatenate([jnp.where(first, a, g), jnp.where(first, g, a)], d) for a, g, d in zip(arrays, got, dims)
    ]


def dot(a, b, dims):
    return lax.dot_general(a, b, (dims, ((), ())), preferred_element_type=F32)


def side_by_side(rows, heads, hd):
    return jnp.concatenate([rows[h * hd : (h + 1) * hd, :] for h in range(heads)], axis=1)


def chunk_pos(me, j, chunk, tq):
    base = ((me * tq) // chunk) ^ j
    rows = lax.broadcasted_iota(jnp.int32, (chunk, tq), 0)
    return base * chunk, base * chunk + (rows ^ ((me * tq) % chunk))


def forward_kernel(scal, q_ref, kv_ref, lo_ref, out_ref, lse_ref, m_s, l_s, acc_s, *, heads, hd, chunk):
    w = pl.program_id(0)
    me = scal[0]
    tq = q_ref.shape[2]
    lo_min = scal[1 + w]
    first = me * tq
    scale2 = LOG2E / math.sqrt(hd)
    zeros = jnp.zeros((hd, tq), BF)
    lo = lo_ref[0]
    query = first + lax.broadcasted_iota(jnp.int32, (chunk, tq), 1)
    m_s[...] = jnp.full(m_s.shape, MASKED, F32)
    l_s[...] = jnp.zeros(l_s.shape, F32)
    acc_s[...] = jnp.zeros(acc_s.shape, F32)

    def body(j, carry):
        base, pos = chunk_pos(me, j, chunk, tq)

        @pl.when((base < first + tq) & (base + chunk > lo_min))
        def _():
            kv = kv_ref[0, pl.ds(pl.multiple_of(j * chunk, chunk), chunk), :]
            kv_t = kv.T
            allowed = (pos >= lo) & (pos <= query)
            for h in range(heads):
                cols = slice(h * tq, (h + 1) * tq)
                q_pad = jnp.concatenate([q_ref[0, h * hd : (h + 1) * hd, :], zeros], axis=0)
                s = jnp.where(allowed, dot(kv, q_pad, ((1,), (0,))), MASKED)
                m_old = m_s[:, cols]
                m_new = jnp.maximum(m_old, jnp.max(s, axis=0, keepdims=True))
                p = jnp.exp2((s - m_new) * scale2)
                alpha = jnp.exp2((m_old - m_new) * scale2)
                m_s[:, cols] = m_new
                l_s[:, cols] = l_s[:, cols] * alpha + jnp.sum(p, axis=0, keepdims=True)
                pv = dot(kv_t, p.astype(BF), ((1,), (0,)))
                acc_s[:, cols] = acc_s[:, cols] * alpha + pv[hd:, :]

        return carry

    lax.fori_loop(0, kv_ref.shape[1] // chunk, body, 0)
    total = l_s[...]
    out = acc_s[...] / total
    lse_ref[0] = m_s[...] * scale2 + jnp.log2(total)
    for h in range(heads):
        out_ref[0, h * hd : (h + 1) * hd, :] = out[:, h * tq : (h + 1) * tq].astype(BF)


def backward_kernel(
    scal, q_ref, kv_ref, lo_ref, out_ref, lse_ref, do_ref, dq_ref, *refs, heads, hd, chunk
):
    *dkv_refs, qx_s, dox_s, dq_s, p_s, ds_s = refs
    w = pl.program_id(0)
    me = scal[0]
    tq = q_ref.shape[2]
    lo_min = scal[1 + w]
    first = me * tq
    scale = 1.0 / math.sqrt(hd)
    scale2 = LOG2E * scale
    group = 2
    lanes = group * tq
    lo = lo_ref[0]
    query = first + lax.broadcasted_iota(jnp.int32, (chunk, tq), 1)
    dq_s[...] = jnp.zeros(dq_s.shape, F32)
    row = lax.broadcasted_iota(jnp.int32, (hd, tq), 0)

    def terms(value):
        out = jnp.zeros((hd, tq), F32)
        for i in range(3):
            part = value.astype(BF).astype(F32)
            out = jnp.where(row == i, part, out)
            value = value - part
        return out.astype(BF)

    for h in range(heads):
        rows, cols = slice(h * hd, (h + 1) * hd), slice(h * tq, (h + 1) * tq)
        do = do_ref[0, rows, :]
        delta = jnp.sum(out_ref[0, rows, :].astype(F32) * do.astype(F32), axis=0, keepdims=True)
        qx_s[:hd, cols] = q_ref[0, rows, :]
        qx_s[hd:, cols] = terms(lse_ref[0, :, cols] * (-1.0 / scale2))
        dox_s[:hd, cols] = terms(-delta)
        dox_s[hd:, cols] = do
    lane = lax.broadcasted_iota(jnp.int32, (chunk, 2 * hd), 1)

    def body(j, carry):
        base, pos = chunk_pos(me, j, chunk, tq)
        here = pl.ds(pl.multiple_of(j * chunk, chunk), chunk)
        needed = (base < first + tq) & (base + chunk > lo_min)

        def store(value):
            kept_a, sent_a, kept_b, sent_b = dkv_refs

            @pl.when(w < pl.num_programs(0) // 2)
            def _():
                rows = pl.ds(pl.multiple_of(j * tq, tq), tq)
                kept_a[0, rows, :] = value[:tq]
                sent_a[0, rows, :] = value[tq:]

            @pl.when(w >= pl.num_programs(0) // 2)
            def _():
                rows = pl.ds(pl.multiple_of((j // 2) * chunk, chunk), chunk)

                @pl.when(j % 2 == 0)
                def _():
                    kept_b[0, rows, :] = value

                @pl.when(j % 2 == 1)
                def _():
                    sent_b[0, rows, :] = value

        @pl.when(jnp.logical_not(needed))
        def _():
            store(jnp.zeros((chunk, 2 * hd), BF))

        @pl.when(needed)
        def _():
            kv = kv_ref[0, here, :]
            one, nought = jnp.ones_like(kv), jnp.zeros_like(kv)
            key_one = jnp.where(lane < hd, kv, jnp.where(lane < hd + 3, one, nought))
            one_value = jnp.where(lane >= hd, kv, jnp.where(lane < 3, one, nought))
            allowed = (pos >= lo) & (pos <= query)
            allowed = jnp.concatenate([allowed] * group, axis=1)
            for g in range(heads // group):
                cols = slice(g * lanes, (g + 1) * lanes)
                p = jnp.exp2(dot(key_one, qx_s[:, cols], ((1,), (0,))) * scale2)
                p = jnp.where(allowed, p, 0.0)
                ds_s[:, cols] = (p * dot(one_value, dox_s[:, cols], ((1,), (0,)))).astype(BF)
                p_s[:, cols] = p.astype(BF)
            dk = dot(ds_s[...], qx_s[...], ((1,), (1,)))
            dv = dot(p_s[...], dox_s[...], ((1,), (1,)))
            dq_s[...] = dq_s[...] + dot(kv.T, ds_s[...], ((1,), (0,)))[:hd, :]
            dkv = jnp.where(lane < hd, dk * scale, dv)
            store(dkv.astype(BF))

        return carry

    lax.fori_loop(0, kv_ref.shape[1] // chunk, body, 0)
    for h in range(heads):
        dq_ref[0, h * hd : (h + 1) * hd, :] = (dq_s[:, h * tq : (h + 1) * tq] * scale).astype(BF)


def assemble_kernel(core, own, *refs, first, wide, count):
    out = refs[-1]
    i = pl.program_id(0)

    @pl.when(i < first)
    def _():
        out[...] = own[...].astype(F32)

    @pl.when(i >= first)
    def _():
        for c in range(count):
            out[:, c * wide : (c + 1) * wide] = refs[c][...].astype(F32)


def assemble(core, own, mix, previous, shape, block, wide, skip, name):
    by_rows = block[1] == shape[1]
    axis = 0 if by_rows else 1
    first = own.shape[axis] // block[axis]
    second = (shape[axis] - 2 * own.shape[axis]) // block[axis] // 2
    count = block[1] // wide

    def at(place):
        return (place, 0) if by_rows else (0, place)

    def mix_at(c):
        return lambda i, core: (skip // block[0] + c * second * by_rows + c * (not by_rows) + jnp.maximum(i - first, 0), 0)

    def out_at(i, core):
        return at(jnp.where(i < first, core[0] * first + i, 2 * first + core[0] * second + i - first))

    in_specs = [pl.BlockSpec(block, lambda i, core: at(jnp.minimum(i, first - 1)))]
    in_specs += [pl.BlockSpec((block[0], wide), mix_at(c)) for c in range(count)]
    arrays = [own, *[mix] * count]
    if previous is not None:
        in_specs.append(pl.BlockSpec(memory_space=pl.ANY))
        arrays.append(previous)
    return pl.pallas_call(
        partial(assemble_kernel, first=first, wide=wide, count=count),
        out_shape=jax.ShapeDtypeStruct(shape, F32),
        grid_spec=pltpu.PrefetchScalarGridSpec(
            num_scalar_prefetch=1,
            grid=(first + second,),
            in_specs=in_specs,
            out_specs=pl.BlockSpec(block, out_at),
        ),
        input_output_aliases={} if previous is None else {len(arrays): 0},
        compiler_params=pltpu.CompilerParams(vmem_limit_bytes=16 << 20),
        cost_estimate=pl.CostEstimate(flops=0, bytes_accessed=3 * shape[0] * shape[1], transcendentals=0),
        name=name,
    )(core, *arrays)


def per_window(shape):
    zeros = (0,) * (len(shape) - 1)
    return pl.BlockSpec((1, *shape[1:]), lambda w, scal: (w, *zeros))


def half_windows(shape, late):
    zeros = (0,) * (len(shape) - 1)
    if late:
        return pl.BlockSpec((1, *shape[1:]), lambda w, scal: (jnp.maximum(w - shape[0], 0), *zeros))
    return pl.BlockSpec((1, *shape[1:]), lambda w, scal: (jnp.minimum(w, shape[0] - 1), *zeros))


def attention_call(kernel, scalars, inputs, outs, scratch, name, flops, halves=0):
    vmem = (12 << 20) + 10 * math.prod(inputs[1].shape[1:]) * inputs[1].dtype.itemsize
    moved = sum(math.prod(a.shape) * a.dtype.itemsize for a in (*inputs, *outs))
    return pl.pallas_call(
        kernel,
        out_shape=outs,
        grid_spec=pltpu.PrefetchScalarGridSpec(
            num_scalar_prefetch=1,
            grid=(inputs[0].shape[0],),
            in_specs=[per_window(a.shape) for a in inputs],
            out_specs=[per_window(a.shape) for a in outs[: len(outs) - halves]]
            + [half_windows(a.shape, i >= halves // 2) for i, a in enumerate(outs[len(outs) - halves :])],
            scratch_shapes=scratch,
        ),
        compiler_params=pltpu.CompilerParams(vmem_limit_bytes=vmem),
        cost_estimate=pl.CostEstimate(flops=flops, bytes_accessed=moved, transcendentals=0),
        name=name,
    )(scalars, *inputs)


def local(
    tokens,
    attn_gain,
    attn_shift,
    w_query,
    b_query,
    w_keyval,
    b_value,
    w_out,
    b_out,
    mlp_gain,
    mlp_shift,
    w_up,
    b_up,
    w_down,
    b_down,
    doc_lengths,
    cotangent,
):
    tq, windows, width = tokens.shape
    hd = w_keyval.shape[1] // 2
    own_cols = w_query.shape[1]
    seq_size = lax.axis_size("seq")
    cols = own_cols * lax.axis_size("head")
    heads = cols // hd
    seq_total = tq * seq_size * lax.axis_size("head")
    me = lax.axis_index("seq") * lax.axis_size("head") + lax.axis_index("head")
    chunk = min(2 * tq, seq_total)

    core = ("batch", 1)
    head = ("head", 1)
    low = ("seq", 1)
    highs = [("seq", 1 << i) for i in range(1, int(math.log2(seq_size)))]

    def other_half(weight):
        half = weight.shape[0] // 2
        part = lax.dynamic_slice_in_dim(weight, lax.axis_index("batch") * half, half, 0)
        return double([swap(part, head)], core, [0])[0]

    wq_other = other_half(w_query)
    bq_other = swap(b_query, head)
    head_first = bit_of(head) == 0

    def in_order(own, other, dim):
        return jnp.concatenate([jnp.where(head_first, own, other), jnp.where(head_first, other, own)], dim)

    wq_all = in_order(w_query, wq_other, 1)
    bq_all = in_order(b_query, bq_other, 0)

    bounds = jnp.cumsum(doc_lengths, axis=1)
    places = me * tq + jnp.arange(tq, dtype=jnp.int32)
    starts = jnp.max(
        jnp.where(bounds[:, :, None] <= places[None, None, :], bounds[:, :, None], 0), axis=1
    )
    scalars = jnp.concatenate([me[None].astype(jnp.int32), starts[:, 0]])
    starts = starts[:, None, :]

    residual = jnp.transpose(tokens, (1, 0, 2)).astype(F32)
    normed = layer_norm(residual, attn_gain, attn_shift).astype(BF)
    value_bias = jnp.concatenate([jnp.zeros((hd,), F32), b_value])
    keyval = (
        jnp.einsum("wtd,dc->wtc", normed, w_keyval, preferred_element_type=F32) + value_bias
    ).astype(BF)

    bits = [*reversed(highs), low, head]

    def gather_step(block, step):
        return jnp.concatenate([block, swap(block, step)], 1 + bits.index(step))

    def reduce_block(block, step):
        kept, sent = jnp.split(block, 2, 1 + bits.index(step))
        return add_low(kept, swap(sent, step))

    half_w = windows // 2
    block = keyval.reshape(windows, *[1] * len(bits), tq, 2 * hd)
    for step in reversed(highs):
        block = gather_step(block, step)
    keyval_all = jnp.concatenate(
        [
            gather_step(gather_step(block[:half_w], low), head).reshape(half_w, seq_total, 2 * hd),
            gather_step(gather_step(block[half_w:], head), low).reshape(half_w, seq_total, 2 * hd),
        ],
        0,
    )
    keyval_all, w_out = tie(keyval_all, w_out)
    wo_all = in_order(w_out, swap(w_out, head), 0)

    queries = (
        jnp.einsum("do,wtd->wot", wq_all, normed, preferred_element_type=F32) + bq_all[None, :, None]
    ).astype(BF)

    struct = jax.ShapeDtypeStruct
    lanes = heads * tq
    work = 2 * windows * lanes * (seq_total // 4) * hd
    mixed, log_total = attention_call(
        partial(forward_kernel, heads=heads, hd=hd, chunk=chunk),
        scalars,
        (queries, keyval_all, starts),
        (struct((windows, cols, tq), BF), struct((windows, 1, lanes), F32)),
        [pltpu.VMEM((1, lanes), F32), pltpu.VMEM((1, lanes), F32), pltpu.VMEM((hd, lanes), F32)],
        "attend",
        8 * work,
    )

    branch = jnp.einsum("wot,od->wtd", mixed, wo_all, preferred_element_type=F32)
    middle = residual + (branch + b_out)
    inner = layer_norm(middle, mlp_gain, mlp_shift).astype(BF)
    upstream_low = jnp.transpose(cotangent, (1, 0, 2))
    upstream = upstream_low.astype(F32)

    upward = jnp.einsum("wtd,df->wtf", inner, w_up, preferred_element_type=F32) + b_up
    active = jax.nn.gelu(upward, approximate=True).astype(BF)
    grad_active = jnp.einsum("wtd,fd->wtf", upstream_low, w_down, preferred_element_type=F32)
    gelu_back = jax.vjp(partial(jax.nn.gelu, approximate=True), upward)[1]
    grad_upward = gelu_back(grad_active)[0].astype(BF)

    ff = w_up.shape[1]
    cut = 2 * ff // 3
    spans = (0, cut // 2), (cut, (ff - cut) // 2)
    on_first = bit_of(core) == 0

    def columns(array, span, other):
        first, size = span
        start = first + size * (bit_of(core) ^ other)
        return lax.dynamic_slice_in_dim(array, start, size, 2)

    def part_down(span, other):
        return jnp.einsum("wtf,wtd->fd", columns(active, span, other), upstream_low, preferred_element_type=F32)

    def part_up(span, other):
        return jnp.einsum("wtd,wtf->df", inner, columns(grad_upward, span, other), preferred_element_type=F32)

    def own_part(make, span, got):
        return (make(span, 0) + got.astype(F32)).astype(BF)

    wide = math.gcd(spans[1][1], width)

    def stack(array):
        return jnp.concatenate([array[:, at : at + wide] for at in range(0, array.shape[1], wide)], 0)

    def unstack(array, rows):
        return jnp.concatenate([array[at : at + rows] for at in range(0, array.shape[0], rows)], 1)

    got_down = swap(part_down(spans[0], 1).astype(BF), core)
    got_up = swap(part_up(spans[0], 1).astype(BF), core)
    got_mix = swap(
        jnp.concatenate([stack(part_down(spans[1], 1).astype(BF)), stack(part_up(spans[1], 1).astype(BF))], 0), core
    )
    rows_mix = spans[1][1]
    rows_down = rows_mix * (width // wide)
    pieces = [
        own_part(part_down, spans[0], got_down),
        own_part(part_up, spans[0], got_up),
        jnp.concatenate(
            [
                stack(own_part(part_down, spans[1], unstack(got_mix[:rows_down], rows_mix))),
                stack(own_part(part_up, spans[1], unstack(got_mix[rows_down:], width))),
            ],
            0,
        ),
    ]

    grad_inner = jnp.einsum("wtf,df->wtd", grad_upward, w_up, preferred_element_type=F32)
    norm_back = jax.vjp(layer_norm, middle, mlp_gain, mlp_shift)[1]
    grad_mid_norm, grad_mlp_gain, grad_mlp_shift = norm_back(grad_inner)
    grad_middle = upstream + grad_mid_norm
    grad_branch = grad_middle.astype(BF)
    grad_mixed = jnp.einsum("od,wtd->wot", wo_all, grad_branch, preferred_element_type=F32).astype(BF)

    own_rows = own_cols // 2

    def core_halves(array):
        array = array.reshape(cols // own_cols, 2, own_rows, width)
        sent = lax.dynamic_index_in_dim(array, 1 - bit_of(core), 1, False)
        kept = lax.dynamic_index_in_dim(array, bit_of(core), 1, False)
        return add_low(kept, swap(sent, core))

    grad_w_out = jnp.einsum("wot,wtd->od", mixed, grad_branch, preferred_element_type=F32).astype(BF)
    out_half = core_halves(grad_w_out)
    out_half = jnp.concatenate([stack(out_half[h]) for h in range(cols // own_cols)], 0)

    near, far = highs[0], highs[1:]
    orders = [near, low, head, *far], [low, head, near, *far], [head, near, low, *far]
    last = len(orders[0]) - 1
    groups = [[pieces[0]], [pieces[1]], [pieces[2], out_half]]
    dims = [[], [], []]

    def reduce_step(at):
        for i in range(3):
            groups[i], dim = halve(groups[i], orders[i][at])
            dims[i].append(dim)

    groups, grad_mixed = tie(groups, grad_mixed)
    reduce_step(0)
    half_keys = struct((half_w, seq_total // 2, 2 * hd), BF)
    grad_queries, *grad_keys = attention_call(
        partial(backward_kernel, heads=heads, hd=hd, chunk=chunk),
        scalars,
        (queries, keyval_all, starts, mixed, log_total, grad_mixed),
        (struct((windows, cols, tq), BF), *[half_keys] * 4),
        [pltpu.VMEM((2 * hd, lanes), BF)] * 2 + [pltpu.VMEM((hd, lanes), F32)] + [pltpu.VMEM((chunk, lanes), BF)] * 2,
        "attend_back",
        20 * work,
        4,
    )
    groups, grad_queries, grad_keys = tie(groups, grad_queries, grad_keys)

    def open_blocks(value, step):
        sides = [1 if other == step else 2 for other in bits]
        return value.reshape(half_w, *sides, tq, 2 * hd)

    def part_query(other):
        half = width // 2
        rows = lax.dynamic_slice_in_dim(normed, half * (bit_of(core) ^ other), half, 2)
        return jnp.einsum("wtd,wot->do", rows, later_queries, preferred_element_type=F32)

    kept_a, sent_a, kept_b, sent_b = grad_keys
    reduce_step(1)
    blocks = [add_low(kept_a, swap(sent_a, head)), add_low(kept_b, swap(sent_b, low))]
    blocks = [open_blocks(blocks[0], head), open_blocks(blocks[1], low)]
    groups, blocks, later_queries = tie(groups, blocks, grad_queries)

    reduce_step(2)
    blocks = [reduce_block(blocks[0], low), reduce_block(blocks[1], head)]
    sent_query = part_query(1).astype(BF)
    groups, blocks, sent_query, active, grad_upward, grad_branch, upstream, later_queries = tie(
        groups, blocks, sent_query, active, grad_upward, grad_branch, upstream, later_queries
    )

    for step in far[:-1]:
        groups = [[add_low(a, g) for a, g in zip(group, swap_all(group, step))] for group in groups]
    far_got = [None, *[swap_all(group, far[-1]) for group in groups[1:]]]
    blocks = reduce_block(jnp.concatenate(blocks, 0), near)
    got_query = swap(sent_query, core)
    query_half = (part_query(0) + got_query.astype(F32)).astype(BF)
    blocks, query_half, active, grad_upward, grad_branch, upstream, later_queries = tie(
        blocks, query_half, active, grad_upward, grad_branch, upstream, later_queries
    )

    for step in far:
        blocks = reduce_block(blocks, step)
    own_head = lax.axis_index("head")
    sent = lax.dynamic_slice_in_dim(query_half, own_cols * (1 - own_head), own_cols, 1)
    kept = lax.dynamic_slice_in_dim(query_half, own_cols * own_head, own_cols, 1)
    query_half = add_low(kept, swap(sent, head))
    result = (
        middle + (jnp.einsum("wtf,fd->wtd", active, w_down, preferred_element_type=F32) + b_down)
    ).astype(BF)
    result = jnp.transpose(result, (1, 0, 2))
    grad_b_up = jnp.sum(grad_upward.astype(F32), axis=(0, 1))
    grad_b_down = jnp.sum(upstream, axis=(0, 1))
    grad_b_out = jnp.sum(grad_branch.astype(F32), axis=(0, 1))
    grad_b_query = jnp.sum(later_queries.astype(F32), axis=(0, 2))
    vectors = [grad_b_up, grad_b_down, grad_mlp_gain, grad_mlp_shift, grad_b_out, grad_b_query]
    blocks, query_half, result, vectors, groups = tie(blocks, query_half, result, vectors, groups)
    far_got[0] = swap_all(groups[0], far[-1])
    grad_keyval = blocks.reshape(windows, tq, 2 * hd)

    grad_w_keyval = jnp.einsum("wtd,wtc->dc", normed, grad_keyval, preferred_element_type=F32)
    grad_b_value = jnp.sum(grad_keyval[:, :, hd:].astype(F32), axis=(0, 1))
    grad_normed = jnp.einsum("wot,do->wtd", grad_queries, wq_all, preferred_element_type=F32)
    grad_normed = grad_normed + jnp.einsum(
        "wtc,dc->wtd", grad_keyval, w_keyval, preferred_element_type=F32
    )
    first_back = jax.vjp(layer_norm, residual, attn_gain, attn_shift)[1]
    grad_input, grad_attn_gain, grad_attn_shift = first_back(grad_normed)
    grad_tokens = jnp.transpose(grad_middle + grad_input, (1, 0, 2))

    def rows_of(vector):
        vector = jnp.pad(vector.astype(F32), (0, (-vector.shape[0]) % width))
        return [vector[at : at + width] for at in range(0, vector.shape[0], width)]

    vectors = [*vectors, grad_attn_gain, grad_attn_shift, grad_b_value]
    rows = [row for vector in vectors for row in rows_of(vector)]
    tall = -(-len(rows) // 16) * 16
    place = lax.broadcasted_iota(jnp.int32, (tall, width), 0)
    packed = jnp.zeros((tall, width), F32)
    for at, row in enumerate(rows):
        packed = jnp.where(place == at, row[None, :], packed)
    small = jnp.concatenate([grad_w_keyval, *[packed[:, at : at + 2 * hd] for at in range(0, width, 2 * hd)]], 0)
    small = small.astype(BF)

    def stack_small(array):
        count = wide // array.shape[1]
        tall = array.shape[0] // count
        return jnp.concatenate([array[at : at + tall] for at in range(0, array.shape[0], tall)], 1)

    def unstack_small(array):
        return jnp.concatenate([array[:, at : at + 2 * hd] for at in range(0, array.shape[1], 2 * hd)], 0)

    (small,), small_dim = halve([small], core)
    small = stack_small(small)
    far_got, small, query_half, grad_tokens = tie(far_got, small, query_half, grad_tokens)
    groups = [[add_low(a, g) for a, g in zip(group, got)] for group, got in zip(groups, far_got)]
    groups, small = tie(groups, small)

    def gather_step(at, join=None):
        for i in range(2):
            groups[i] = double(groups[i], orders[i][at], dims[i][at][: len(groups[i])])
        step = orders[2][at]
        got = swap_all(groups[2] if join is None else [*groups[2], join], step)
        lower = bit_of(step) == 0
        groups[2] = [
            jnp.concatenate([jnp.where(lower, a, g), jnp.where(lower, g, a)], d)
            for a, g, d in zip(groups[2], got, dims[2][at])
        ]
        return join if join is None else add_low(join, got[-1])

    small = gather_step(2, small)
    (query_half,), query_dim = halve([query_half], low)
    groups, small, query_half, grad_tokens = tie(groups, small, query_half, grad_tokens)

    small = gather_step(1, small)
    query_half = add_low(query_half, swap(query_half, near))
    groups, small, query_half = tie(groups, small, query_half)

    def both(own, other, dim):
        own, other = own.astype(F32), other.astype(F32)
        return [jnp.where(on_first, own, other), jnp.where(on_first, other, own)]

    out_half = groups[2].pop()
    gather_step(0)
    for step in far:
        query_half = add_low(query_half, swap(query_half, step))
    for step in [*far, head]:
        small = add_low(small, swap(small, step))
    (query_half,) = double([query_half], low, query_dim)
    (small,) = double([unstack_small(small)], core, small_dim)
    query_other = swap(query_half, core)
    out_other = swap(out_half, core)
    out_half, out_other = unstack(out_half, own_rows), unstack(out_other, own_rows)
    grad_w_out = jnp.concatenate(both(out_half, out_other, 0), 0)
    small = small.astype(F32)
    grad_w_keyval, packed = small[:width], small[width:]
    packed = jnp.concatenate([packed[at : at + tall] for at in range(0, packed.shape[0], tall)], 1)
    sums, at = [], 0
    for vector in vectors:
        count = -(-vector.shape[0] // width)
        sums.append(packed[at : at + count].reshape(-1)[: vector.shape[0]])
        at += count
    sums[5] = lax.dynamic_slice_in_dim(sums[5], lax.axis_index("head") * own_cols, own_cols, 0)
    groups, sums, grad_w_keyval, grad_w_out, query_half, query_other = tie(
        groups, sums, grad_w_keyval, grad_w_out, query_half, query_other
    )

    (down,), (up,), (mix,) = groups
    got_down, got_mix, got_up = swap(down, core), swap(mix, core), swap(up, core)
    where = lax.axis_index("batch")[None].astype(jnp.int32)
    down_block, up_block = (rows_mix // 2, width), (width, rows_mix)
    own_down = assemble(where, down, mix, None, (ff, width), down_block, wide, 0, "own_down")
    own_up = assemble(where, up, mix, None, (width, ff), up_block, wide, rows_down, "own_up")
    got_down, got_mix, got_up, own_down, own_up = tie(got_down, got_mix, got_up, own_down, own_up)
    grad_w_down = assemble(1 - where, got_down, got_mix, own_down, (ff, width), down_block, wide, 0, "got_down")
    grad_w_up = assemble(1 - where, got_up, got_mix, own_up, (width, ff), up_block, wide, rows_down, "got_up")

    grad_w_query = jnp.concatenate(both(query_half, query_other, 0), 0)
    b_up_sum, b_down_sum, mlp_gain_sum, mlp_shift_sum, b_out_sum, b_query_sum, gain_sum, shift_sum, b_value_sum = sums

    return (
        result,
        grad_tokens,
        gain_sum,
        shift_sum,
        grad_w_query,
        b_query_sum,
        grad_w_keyval,
        b_value_sum,
        grad_w_out,
        b_out_sum,
        mlp_gain_sum,
        mlp_shift_sum,
        grad_w_up,
        b_up_sum,
        grad_w_down,
        b_down_sum,
    )


def solution(mesh):
    return jax.shard_map(
        local,
        mesh=mesh,
        in_specs=(
            P(("seq", "head"), "batch", None),
            P(),
            P(),
            P(None, "head"),
            P("head"),
            P(),
            P(),
            P("head", None),
            P(),
            P(),
            P(),
            P(),
            P(),
            P(),
            P(),
            P("batch", None),
            P(("seq", "head"), "batch", None),
        ),
        out_specs=(
            P(("seq", "head"), "batch", None),
            P(("seq", "head"), "batch", None),
            P(),
            P(),
            P(None, "head"),
            P("head"),
            P(),
            P(),
            P("head", None),
            P(),
            P(),
            P(),
            P(),
            P(),
            P(),
            P(),
        ),
        check_vma=False,
    )
```

```python
from functools import partial
import math

import jax
import jax.numpy as jnp
from jax import lax
from jax.experimental import pallas as pl
from jax.experimental.pallas import tpu as pltpu
from jax.sharding import PartitionSpec as P

EPSILON = 1e-05
MASKED = -1e30
BF = jnp.bfloat16
F32 = jnp.float32
LOG2E = math.log2(math.e)


def layer_norm(inputs, norm_gain, norm_shift):
    center = inputs - jnp.mean(inputs, axis=-1, keepdims=True)
    spread = jnp.mean(center * center, axis=-1, keepdims=True)
    return center * lax.rsqrt(spread + EPSILON) * norm_gain + norm_shift


def swap(value, step):
    axis, flip = step
    size = lax.axis_size(axis)
    return lax.ppermute(value, axis, [(i, i ^ flip) for i in range(size)])


def bit_of(step):
    axis, flip = step
    return (lax.axis_index(axis) // flip) % 2


def split_dim(shape):
    if (shape[0] // 2) % 8 == 0:
        return 0
    return 1


def add_low(kept, got):
    return (kept.astype(F32) + got.astype(F32)).astype(kept.dtype)


def tie(*trees):
    leaves, shape = jax.tree.flatten(trees)
    return jax.tree.unflatten(shape, lax.optimization_barrier(leaves))


def halve(arrays, step):
    bit = bit_of(step)
    dims = [split_dim(a.shape) for a in arrays]
    halves = [a.shape[d] // 2 for a, d in zip(arrays, dims)]
    sent = [lax.dynamic_slice_in_dim(a, (1 - bit) * h, h, d) for a, h, d in zip(arrays, halves, dims)]
    kept = [lax.dynamic_slice_in_dim(a, bit * h, h, d) for a, h, d in zip(arrays, halves, dims)]
    return [add_low(k, g) for k, g in zip(kept, swap_all(sent, step))], dims


def swap_all(arrays, step):
    if len({a.shape[1] for a in arrays}) > 1:
        return [swap(a, step) for a in arrays]
    got = swap(jnp.concatenate(arrays, 0) if len(arrays) > 1 else arrays[0], step)
    at, out = 0, []
    for a in arrays:
        out.append(got[at : at + a.shape[0]])
        at += a.shape[0]
    return out


def double(arrays, step, dims):
    got = swap_all(arrays, step)
    first = bit_of(step) == 0
    return [
        jnp.concatenate([jnp.where(first, a, g), jnp.where(first, g, a)], d) for a, g, d in zip(arrays, got, dims)
    ]


def dot(a, b, dims):
    return lax.dot_general(a, b, (dims, ((), ())), preferred_element_type=F32)


def side_by_side(rows, heads, hd):
    return jnp.concatenate([rows[h * hd : (h + 1) * hd, :] for h in range(heads)], axis=1)


def chunk_pos(me, j, chunk, tq):
    base = ((me * tq) // chunk) ^ j
    rows = lax.broadcasted_iota(jnp.int32, (chunk, tq), 0)
    return base * chunk, base * chunk + (rows ^ ((me * tq) % chunk))


def forward_kernel(scal, q_ref, kv_ref, lo_ref, out_ref, lse_ref, m_s, l_s, acc_s, *, heads, hd, chunk):
    w = pl.program_id(0)
    me = scal[0]
    tq = q_ref.shape[2]
    lo_min = scal[1 + w]
    first = me * tq
    scale2 = LOG2E / math.sqrt(hd)
    zeros = jnp.zeros((hd, tq), BF)
    lo = lo_ref[0]
    query = first + lax.broadcasted_iota(jnp.int32, (chunk, tq), 1)
    m_s[...] = jnp.full(m_s.shape, MASKED, F32)
    l_s[...] = jnp.zeros(l_s.shape, F32)
    acc_s[...] = jnp.zeros(acc_s.shape, F32)

    def body(j, carry):
        base, pos = chunk_pos(me, j, chunk, tq)

        @pl.when((base < first + tq) & (base + chunk > lo_min))
        def _():
            kv = kv_ref[0, pl.ds(pl.multiple_of(j * chunk, chunk), chunk), :]
            kv_t = kv.T
            allowed = (pos >= lo) & (pos <= query)
            for h in range(heads):
                cols = slice(h * tq, (h + 1) * tq)
                q_pad = jnp.concatenate([q_ref[0, h * hd : (h + 1) * hd, :], zeros], axis=0)
                s = jnp.where(allowed, dot(kv, q_pad, ((1,), (0,))), MASKED)
                m_old = m_s[:, cols]
                m_new = jnp.maximum(m_old, jnp.max(s, axis=0, keepdims=True))
                p = jnp.exp2((s - m_new) * scale2)
                alpha = jnp.exp2((m_old - m_new) * scale2)
                m_s[:, cols] = m_new
                l_s[:, cols] = l_s[:, cols] * alpha + jnp.sum(p, axis=0, keepdims=True)
                pv = dot(kv_t, p.astype(BF), ((1,), (0,)))
                acc_s[:, cols] = acc_s[:, cols] * alpha + pv[hd:, :]

        return carry

    lax.fori_loop(0, kv_ref.shape[1] // chunk, body, 0)
    total = l_s[...]
    out = acc_s[...] / total
    lse_ref[0] = m_s[...] * scale2 + jnp.log2(total)
    for h in range(heads):
        out_ref[0, h * hd : (h + 1) * hd, :] = out[:, h * tq : (h + 1) * tq].astype(BF)


def backward_kernel(
    scal, q_ref, kv_ref, lo_ref, out_ref, lse_ref, do_ref, dq_ref, *refs, heads, hd, chunk
):
    *dkv_refs, qx_s, dox_s, dq_s, p_s, ds_s = refs
    w = pl.program_id(0)
    me = scal[0]
    tq = q_ref.shape[2]
    lo_min = scal[1 + w]
    first = me * tq
    scale = 1.0 / math.sqrt(hd)
    scale2 = LOG2E * scale
    group = 2
    lanes = group * tq
    lo = lo_ref[0]
    query = first + lax.broadcasted_iota(jnp.int32, (chunk, tq), 1)
    dq_s[...] = jnp.zeros(dq_s.shape, F32)
    row = lax.broadcasted_iota(jnp.int32, (hd, tq), 0)

    def terms(value):
        out = jnp.zeros((hd, tq), F32)
        for i in range(3):
            part = value.astype(BF).astype(F32)
            out = jnp.where(row == i, part, out)
            value = value - part
        return out.astype(BF)

    for h in range(heads):
        rows, cols = slice(h * hd, (h + 1) * hd), slice(h * tq, (h + 1) * tq)
        do = do_ref[0, rows, :]
        delta = jnp.sum(out_ref[0, rows, :].astype(F32) * do.astype(F32), axis=0, keepdims=True)
        qx_s[:hd, cols] = q_ref[0, rows, :]
        qx_s[hd:, cols] = terms(lse_ref[0, :, cols] * (-1.0 / scale2))
        dox_s[:hd, cols] = terms(-delta)
        dox_s[hd:, cols] = do
    lane = lax.broadcasted_iota(jnp.int32, (chunk, 2 * hd), 1)

    def body(j, carry):
        base, pos = chunk_pos(me, j, chunk, tq)
        here = pl.ds(pl.multiple_of(j * chunk, chunk), chunk)
        needed = (base < first + tq) & (base + chunk > lo_min)

        def store(value):
            kept_a, sent_a, kept_b, sent_b = dkv_refs

            @pl.when(w < pl.num_programs(0) // 2)
            def _():
                rows = pl.ds(pl.multiple_of(j * tq, tq), tq)
                kept_a[0, rows, :] = value[:tq]
                sent_a[0, rows, :] = value[tq:]

            @pl.when(w >= pl.num_programs(0) // 2)
            def _():
                rows = pl.ds(pl.multiple_of((j // 2) * chunk, chunk), chunk)

                @pl.when(j % 2 == 0)
                def _():
                    kept_b[0, rows, :] = value

                @pl.when(j % 2 == 1)
                def _():
                    sent_b[0, rows, :] = value

        @pl.when(jnp.logical_not(needed))
        def _():
            store(jnp.zeros((chunk, 2 * hd), BF))

        @pl.when(needed)
        def _():
            kv = kv_ref[0, here, :]
            one, nought = jnp.ones_like(kv), jnp.zeros_like(kv)
            key_one = jnp.where(lane < hd, kv, jnp.where(lane < hd + 3, one, nought))
            one_value = jnp.where(lane >= hd, kv, jnp.where(lane < 3, one, nought))
            allowed = (pos >= lo) & (pos <= query)
            allowed = jnp.concatenate([allowed] * group, axis=1)
            for g in range(heads // group):
                cols = slice(g * lanes, (g + 1) * lanes)
                p = jnp.exp2(dot(key_one, qx_s[:, cols], ((1,), (0,))) * scale2)
                p = jnp.where(allowed, p, 0.0)
                ds_s[:, cols] = (p * dot(one_value, dox_s[:, cols], ((1,), (0,)))).astype(BF)
                p_s[:, cols] = p.astype(BF)
            dk = dot(ds_s[...], qx_s[...], ((1,), (1,)))
            dv = dot(p_s[...], dox_s[...], ((1,), (1,)))
            dq_s[...] = dq_s[...] + dot(kv.T, ds_s[...], ((1,), (0,)))[:hd, :]
            dkv = jnp.where(lane < hd, dk * scale, dv)
            store(dkv.astype(BF))

        return carry

    lax.fori_loop(0, kv_ref.shape[1] // chunk, body, 0)
    for h in range(heads):
        dq_ref[0, h * hd : (h + 1) * hd, :] = (dq_s[:, h * tq : (h + 1) * tq] * scale).astype(BF)


def assemble_kernel(core, own, *refs, first, wide, count):
    out = refs[-1]
    i = pl.program_id(0)

    @pl.when(i < first)
    def _():
        out[...] = own[...].astype(F32)

    @pl.when(i >= first)
    def _():
        for c in range(count):
            out[:, c * wide : (c + 1) * wide] = refs[c][...].astype(F32)


def assemble(core, own, mix, previous, shape, block, wide, skip, name):
    by_rows = block[1] == shape[1]
    axis = 0 if by_rows else 1
    first = own.shape[axis] // block[axis]
    second = (shape[axis] - 2 * own.shape[axis]) // block[axis] // 2
    count = block[1] // wide

    def at(place):
        return (place, 0) if by_rows else (0, place)

    def mix_at(c):
        return lambda i, core: (skip // block[0] + c * second * by_rows + c * (not by_rows) + jnp.maximum(i - first, 0), 0)

    def out_at(i, core):
        return at(jnp.where(i < first, core[0] * first + i, 2 * first + core[0] * second + i - first))

    in_specs = [pl.BlockSpec(block, lambda i, core: at(jnp.minimum(i, first - 1)))]
    in_specs += [pl.BlockSpec((block[0], wide), mix_at(c)) for c in range(count)]
    arrays = [own, *[mix] * count]
    if previous is not None:
        in_specs.append(pl.BlockSpec(memory_space=pl.ANY))
        arrays.append(previous)
    return pl.pallas_call(
        partial(assemble_kernel, first=first, wide=wide, count=count),
        out_shape=jax.ShapeDtypeStruct(shape, F32),
        grid_spec=pltpu.PrefetchScalarGridSpec(
            num_scalar_prefetch=1,
            grid=(first + second,),
            in_specs=in_specs,
            out_specs=pl.BlockSpec(block, out_at),
        ),
        input_output_aliases={} if previous is None else {len(arrays): 0},
        compiler_params=pltpu.CompilerParams(vmem_limit_bytes=16 << 20),
        cost_estimate=pl.CostEstimate(flops=0, bytes_accessed=3 * shape[0] * shape[1], transcendentals=0),
        name=name,
    )(core, *arrays)


def per_window(shape):
    zeros = (0,) * (len(shape) - 1)
    return pl.BlockSpec((1, *shape[1:]), lambda w, scal: (w, *zeros))


def half_windows(shape, late):
    zeros = (0,) * (len(shape) - 1)
    if late:
        return pl.BlockSpec((1, *shape[1:]), lambda w, scal: (jnp.maximum(w - shape[0], 0), *zeros))
    return pl.BlockSpec((1, *shape[1:]), lambda w, scal: (jnp.minimum(w, shape[0] - 1), *zeros))


def attention_call(kernel, scalars, inputs, outs, scratch, name, flops, halves=0):
    vmem = (12 << 20) + 10 * math.prod(inputs[1].shape[1:]) * inputs[1].dtype.itemsize
    moved = sum(math.prod(a.shape) * a.dtype.itemsize for a in (*inputs, *outs))
    return pl.pallas_call(
        kernel,
        out_shape=outs,
        grid_spec=pltpu.PrefetchScalarGridSpec(
            num_scalar_prefetch=1,
            grid=(inputs[0].shape[0],),
            in_specs=[per_window(a.shape) for a in inputs],
            out_specs=[per_window(a.shape) for a in outs[: len(outs) - halves]]
            + [half_windows(a.shape, i >= halves // 2) for i, a in enumerate(outs[len(outs) - halves :])],
            scratch_shapes=scratch,
        ),
        compiler_params=pltpu.CompilerParams(vmem_limit_bytes=vmem),
        cost_estimate=pl.CostEstimate(flops=flops, bytes_accessed=moved, transcendentals=0),
        name=name,
    )(scalars, *inputs)


def local(
    tokens,
    attn_gain,
    attn_shift,
    w_query,
    b_query,
    w_keyval,
    b_value,
    w_out,
    b_out,
    mlp_gain,
    mlp_shift,
    w_up,
    b_up,
    w_down,
    b_down,
    doc_lengths,
    cotangent,
):
    tq, windows, width = tokens.shape
    hd = w_keyval.shape[1] // 2
    own_cols = w_query.shape[1]
    seq_size = lax.axis_size("seq")
    cols = own_cols * lax.axis_size("head")
    heads = cols // hd
    seq_total = tq * seq_size * lax.axis_size("head")
    me = lax.axis_index("seq") * lax.axis_size("head") + lax.axis_index("head")
    chunk = min(2 * tq, seq_total)

    core = ("batch", 1)
    head = ("head", 1)
    low = ("seq", 1)
    highs = [("seq", 1 << i) for i in range(1, int(math.log2(seq_size)))]

    def other_half(weight):
        half = weight.shape[0] // 2
        part = lax.dynamic_slice_in_dim(weight, lax.axis_index("batch") * half, half, 0)
        return double([swap(part, head)], core, [0])[0]

    wq_other = other_half(w_query)
    bq_other = swap(b_query, head)
    head_first = bit_of(head) == 0

    def in_order(own, other, dim):
        return jnp.concatenate([jnp.where(head_first, own, other), jnp.where(head_first, other, own)], dim)

    wq_all = in_order(w_query, wq_other, 1)
    bq_all = in_order(b_query, bq_other, 0)

    bounds = jnp.cumsum(doc_lengths, axis=1)
    places = me * tq + jnp.arange(tq, dtype=jnp.int32)
    starts = jnp.max(
        jnp.where(bounds[:, :, None] <= places[None, None, :], bounds[:, :, None], 0), axis=1
    )
    scalars = jnp.concatenate([me[None].astype(jnp.int32), starts[:, 0]])
    starts = starts[:, None, :]

    residual = jnp.transpose(tokens, (1, 0, 2)).astype(F32)
    normed = layer_norm(residual, attn_gain, attn_shift).astype(BF)
    value_bias = jnp.concatenate([jnp.zeros((hd,), F32), b_value])
    keyval = (
        jnp.einsum("wtd,dc->wtc", normed, w_keyval, preferred_element_type=F32) + value_bias
    ).astype(BF)

    bits = [*reversed(highs), low, head]

    def gather_step(block, step):
        return jnp.concatenate([block, swap(block, step)], 1 + bits.index(step))

    def reduce_block(block, step):
        kept, sent = jnp.split(block, 2, 1 + bits.index(step))
        return add_low(kept, swap(sent, step))

    half_w = windows // 2
    block = keyval.reshape(windows, *[1] * len(bits), tq, 2 * hd)
    for step in reversed(highs):
        block = gather_step(block, step)
    keyval_all = jnp.concatenate(
        [
            gather_step(gather_step(block[:half_w], low), head).reshape(half_w, seq_total, 2 * hd),
            gather_step(gather_step(block[half_w:], head), low).reshape(half_w, seq_total, 2 * hd),
        ],
        0,
    )
    keyval_all, w_out = tie(keyval_all, w_out)
    wo_all = in_order(w_out, swap(w_out, head), 0)

    queries = (
        jnp.einsum("do,wtd->wot", wq_all, normed, preferred_element_type=F32) + bq_all[None, :, None]
    ).astype(BF)

    struct = jax.ShapeDtypeStruct
    lanes = heads * tq
    work = 2 * windows * lanes * (seq_total // 4) * hd
    mixed, log_total = attention_call(
        partial(forward_kernel, heads=heads, hd=hd, chunk=chunk),
        scalars,
        (queries, keyval_all, starts),
        (struct((windows, cols, tq), BF), struct((windows, 1, lanes), F32)),
        [pltpu.VMEM((1, lanes), F32), pltpu.VMEM((1, lanes), F32), pltpu.VMEM((hd, lanes), F32)],
        "attend",
        8 * work,
    )

    branch = jnp.einsum("wot,od->wtd", mixed, wo_all, preferred_element_type=F32)
    middle = residual + (branch + b_out)
    inner = layer_norm(middle, mlp_gain, mlp_shift).astype(BF)
    upstream_low = jnp.transpose(cotangent, (1, 0, 2))
    upstream = upstream_low.astype(F32)

    upward = jnp.einsum("wtd,df->wtf", inner, w_up, preferred_element_type=F32) + b_up
    active = jax.nn.gelu(upward, approximate=True).astype(BF)
    grad_active = jnp.einsum("wtd,fd->wtf", upstream_low, w_down, preferred_element_type=F32)
    gelu_back = jax.vjp(partial(jax.nn.gelu, approximate=True), upward)[1]
    grad_upward = gelu_back(grad_active)[0].astype(BF)

    ff = w_up.shape[1]
    cut = 2 * ff // 3
    spans = (0, cut // 2), (cut, (ff - cut) // 2)
    on_first = bit_of(core) == 0

    def columns(array, span, other):
        first, size = span
        start = first + size * (bit_of(core) ^ other)
        return lax.dynamic_slice_in_dim(array, start, size, 2)

    def part_down(span, other):
        return jnp.einsum("wtf,wtd->fd", columns(active, span, other), upstream_low, preferred_element_type=F32)

    def part_up(span, other):
        return jnp.einsum("wtd,wtf->df", inner, columns(grad_upward, span, other), preferred_element_type=F32)

    def own_part(make, span, got):
        return (make(span, 0) + got.astype(F32)).astype(BF)

    wide = math.gcd(spans[1][1], width)

    def stack(array):
        return jnp.concatenate([array[:, at : at + wide] for at in range(0, array.shape[1], wide)], 0)

    def unstack(array, rows):
        return jnp.concatenate([array[at : at + rows] for at in range(0, array.shape[0], rows)], 1)

    got_down = swap(part_down(spans[0], 1).astype(BF), core)
    got_up = swap(part_up(spans[0], 1).astype(BF), core)
    got_mix = swap(
        jnp.concatenate([stack(part_down(spans[1], 1).astype(BF)), stack(part_up(spans[1], 1).astype(BF))], 0), core
    )
    rows_mix = spans[1][1]
    rows_down = rows_mix * (width // wide)
    pieces = [
        own_part(part_down, spans[0], got_down),
        own_part(part_up, spans[0], got_up),
        jnp.concatenate(
            [
                stack(own_part(part_down, spans[1], unstack(got_mix[:rows_down], rows_mix))),
                stack(own_part(part_up, spans[1], unstack(got_mix[rows_down:], width))),
            ],
            0,
        ),
    ]

    grad_inner = jnp.einsum("wtf,df->wtd", grad_upward, w_up, preferred_element_type=F32)
    norm_back = jax.vjp(layer_norm, middle, mlp_gain, mlp_shift)[1]
    grad_mid_norm, grad_mlp_gain, grad_mlp_shift = norm_back(grad_inner)
    grad_middle = upstream + grad_mid_norm
    grad_branch = grad_middle.astype(BF)
    grad_mixed = jnp.einsum("od,wtd->wot", wo_all, grad_branch, preferred_element_type=F32).astype(BF)

    own_rows = own_cols // 2

    def core_halves(array):
        array = array.reshape(cols // own_cols, 2, own_rows, width)
        sent = lax.dynamic_index_in_dim(array, 1 - bit_of(core), 1, False)
        kept = lax.dynamic_index_in_dim(array, bit_of(core), 1, False)
        return add_low(kept, swap(sent, core))

    grad_w_out = jnp.einsum("wot,wtd->od", mixed, grad_branch, preferred_element_type=F32).astype(BF)
    out_half = core_halves(grad_w_out)
    out_half = jnp.concatenate([stack(out_half[h]) for h in range(cols // own_cols)], 0)

    near, far = highs[0], highs[1:]
    orders = [near, low, head, *far], [low, head, near, *far], [head, near, low, *far]
    last = len(orders[0]) - 1
    groups = [[pieces[0]], [pieces[1]], [pieces[2], out_half]]
    dims = [[], [], []]

    def reduce_step(at):
        for i in range(3):
            groups[i], dim = halve(groups[i], orders[i][at])
            dims[i].append(dim)

    groups, grad_mixed = tie(groups, grad_mixed)
    reduce_step(0)
    half_keys = struct((half_w, seq_total // 2, 2 * hd), BF)
    grad_queries, *grad_keys = attention_call(
        partial(backward_kernel, heads=heads, hd=hd, chunk=chunk),
        scalars,
        (queries, keyval_all, starts, mixed, log_total, grad_mixed),
        (struct((windows, cols, tq), BF), *[half_keys] * 4),
        [pltpu.VMEM((2 * hd, lanes), BF)] * 2 + [pltpu.VMEM((hd, lanes), F32)] + [pltpu.VMEM((chunk, lanes), BF)] * 2,
        "attend_back",
        20 * work,
        4,
    )
    groups, grad_queries, grad_keys = tie(groups, grad_queries, grad_keys)

    def open_blocks(value, step):
        sides = [1 if other == step else 2 for other in bits]
        return value.reshape(half_w, *sides, tq, 2 * hd)

    def part_query(other):
        half = width // 2
        rows = lax.dynamic_slice_in_dim(normed, half * (bit_of(core) ^ other), half, 2)
        return jnp.einsum("wtd,wot->do", rows, later_queries, preferred_element_type=F32)

    kept_a, sent_a, kept_b, sent_b = grad_keys
    reduce_step(1)
    blocks = [add_low(kept_a, swap(sent_a, head)), add_low(kept_b, swap(sent_b, low))]
    blocks = [open_blocks(blocks[0], head), open_blocks(blocks[1], low)]
    groups, blocks, later_queries = tie(groups, blocks, grad_queries)

    reduce_step(2)
    blocks = [reduce_block(blocks[0], low), reduce_block(blocks[1], head)]
    sent_query = part_query(1).astype(BF)
    groups, blocks, sent_query, active, grad_upward, grad_branch, upstream, later_queries = tie(
        groups, blocks, sent_query, active, grad_upward, grad_branch, upstream, later_queries
    )

    for step in far[:-1]:
        groups = [[add_low(a, g) for a, g in zip(group, swap_all(group, step))] for group in groups]
    far_got = [None, *[swap_all(group, far[-1]) for group in groups[1:]]]
    blocks = reduce_block(jnp.concatenate(blocks, 0), near)
    got_query = swap(sent_query, core)
    query_half = (part_query(0) + got_query.astype(F32)).astype(BF)
    blocks, query_half, active, grad_upward, grad_branch, upstream, later_queries = tie(
        blocks, query_half, active, grad_upward, grad_branch, upstream, later_queries
    )

    for step in far:
        blocks = reduce_block(blocks, step)
    own_head = lax.axis_index("head")
    sent = lax.dynamic_slice_in_dim(query_half, own_cols * (1 - own_head), own_cols, 1)
    kept = lax.dynamic_slice_in_dim(query_half, own_cols * own_head, own_cols, 1)
    query_half = add_low(kept, swap(sent, head))
    result = (
        middle + (jnp.einsum("wtf,fd->wtd", active, w_down, preferred_element_type=F32) + b_down)
    ).astype(BF)
    result = jnp.transpose(result, (1, 0, 2))
    grad_b_up = jnp.sum(grad_upward.astype(F32), axis=(0, 1))
    grad_b_down = jnp.sum(upstream, axis=(0, 1))
    grad_b_out = jnp.sum(grad_branch.astype(F32), axis=(0, 1))
    grad_b_query = jnp.sum(later_queries.astype(F32), axis=(0, 2))
    vectors = [grad_b_up, grad_b_down, grad_mlp_gain, grad_mlp_shift, grad_b_out, grad_b_query]
    blocks, query_half, result, vectors, groups = tie(blocks, query_half, result, vectors, groups)
    far_got[0] = swap_all(groups[0], far[-1])
    grad_keyval = blocks.reshape(windows, tq, 2 * hd)

    grad_w_keyval = jnp.einsum("wtd,wtc->dc", normed, grad_keyval, preferred_element_type=F32)
    grad_b_value = jnp.sum(grad_keyval[:, :, hd:].astype(F32), axis=(0, 1))
    grad_normed = jnp.einsum("wot,do->wtd", grad_queries, wq_all, preferred_element_type=F32)
    grad_normed = grad_normed + jnp.einsum(
        "wtc,dc->wtd", grad_keyval, w_keyval, preferred_element_type=F32
    )
    first_back = jax.vjp(layer_norm, residual, attn_gain, attn_shift)[1]
    grad_input, grad_attn_gain, grad_attn_shift = first_back(grad_normed)
    grad_tokens = jnp.transpose(grad_middle + grad_input, (1, 0, 2))

    def rows_of(vector):
        vector = jnp.pad(vector.astype(F32), (0, (-vector.shape[0]) % width))
        return [vector[at : at + width] for at in range(0, vector.shape[0], width)]

    vectors = [*vectors, grad_attn_gain, grad_attn_shift, grad_b_value]
    rows = [row for vector in vectors for row in rows_of(vector)]
    tall = -(-len(rows) // 16) * 16
    place = lax.broadcasted_iota(jnp.int32, (tall, width), 0)
    packed = jnp.zeros((tall, width), F32)
    for at, row in enumerate(rows):
        packed = jnp.where(place == at, row[None, :], packed)
    small = jnp.concatenate([grad_w_keyval, *[packed[:, at : at + 2 * hd] for at in range(0, width, 2 * hd)]], 0)
    small = small.astype(BF)

    def stack_small(array):
        count = wide // array.shape[1]
        tall = array.shape[0] // count
        return jnp.concatenate([array[at : at + tall] for at in range(0, array.shape[0], tall)], 1)

    def unstack_small(array):
        return jnp.concatenate([array[:, at : at + 2 * hd] for at in range(0, array.shape[1], 2 * hd)], 0)

    (small,), small_dim = halve([small], core)
    small = stack_small(small)
    far_got, small, query_half, grad_tokens = tie(far_got, small, query_half, grad_tokens)
    groups = [[add_low(a, g) for a, g in zip(group, got)] for group, got in zip(groups, far_got)]
    groups, small = tie(groups, small)

    def gather_step(at, join=None):
        for i in range(2):
            groups[i] = double(groups[i], orders[i][at], dims[i][at][: len(groups[i])])
        step = orders[2][at]
        got = swap_all(groups[2] if join is None else [*groups[2], join], step)
        lower = bit_of(step) == 0
        groups[2] = [
            jnp.concatenate([jnp.where(lower, a, g), jnp.where(lower, g, a)], d)
            for a, g, d in zip(groups[2], got, dims[2][at])
        ]
        return join if join is None else add_low(join, got[-1])

    small = gather_step(2, small)
    (query_half,), query_dim = halve([query_half], low)
    groups, small, query_half, grad_tokens = tie(groups, small, query_half, grad_tokens)

    small = gather_step(1, small)
    query_half = add_low(query_half, swap(query_half, near))
    groups, small, query_half = tie(groups, small, query_half)

    def both(own, other, dim):
        own, other = own.astype(F32), other.astype(F32)
        return [jnp.where(on_first, own, other), jnp.where(on_first, other, own)]

    out_half = groups[2].pop()
    gather_step(0)
    for step in far:
        query_half = add_low(query_half, swap(query_half, step))
    for step in far:
        small = add_low(small, swap(small, step))
    small, out_half = tie(small, out_half)
    small = add_low(small, swap(small, head))
    (query_half,) = double([query_half], low, query_dim)
    (small,) = double([unstack_small(small)], core, small_dim)
    query_other = swap(query_half, core)
    out_other = swap(out_half, core)
    out_half, out_other = unstack(out_half, own_rows), unstack(out_other, own_rows)
    grad_w_out = jnp.concatenate(both(out_half, out_other, 0), 0)
    small = small.astype(F32)
    grad_w_keyval, packed = small[:width], small[width:]
    packed = jnp.concatenate([packed[at : at + tall] for at in range(0, packed.shape[0], tall)], 1)
    sums, at = [], 0
    for vector in vectors:
        count = -(-vector.shape[0] // width)
        sums.append(packed[at : at + count].reshape(-1)[: vector.shape[0]])
        at += count
    sums[5] = lax.dynamic_slice_in_dim(sums[5], lax.axis_index("head") * own_cols, own_cols, 0)
    groups, sums, grad_w_keyval, grad_w_out, query_half, query_other = tie(
        groups, sums, grad_w_keyval, grad_w_out, query_half, query_other
    )

    (down,), (up,), (mix,) = groups
    got_down, got_mix, got_up = swap(down, core), swap(mix, core), swap(up, core)
    where = lax.axis_index("batch")[None].astype(jnp.int32)
    down_block, up_block = (rows_mix // 2, width), (width, rows_mix)
    own_down = assemble(where, down, mix, None, (ff, width), down_block, wide, 0, "own_down")
    own_up = assemble(where, up, mix, None, (width, ff), up_block, wide, rows_down, "own_up")
    got_down, got_mix, got_up, own_down, own_up = tie(got_down, got_mix, got_up, own_down, own_up)
    grad_w_down = assemble(1 - where, got_down, got_mix, own_down, (ff, width), down_block, wide, 0, "got_down")
    grad_w_up = assemble(1 - where, got_up, got_mix, own_up, (width, ff), up_block, wide, rows_down, "got_up")

    grad_w_query = jnp.concatenate(both(query_half, query_other, 0), 0)
    b_up_sum, b_down_sum, mlp_gain_sum, mlp_shift_sum, b_out_sum, b_query_sum, gain_sum, shift_sum, b_value_sum = sums

    return (
        result,
        grad_tokens,
        gain_sum,
        shift_sum,
        grad_w_query,
        b_query_sum,
        grad_w_keyval,
        b_value_sum,
        grad_w_out,
        b_out_sum,
        mlp_gain_sum,
        mlp_shift_sum,
        grad_w_up,
        b_up_sum,
        grad_w_down,
        b_down_sum,
    )


def solution(mesh):
    return jax.shard_map(
        local,
        mesh=mesh,
        in_specs=(
            P(("seq", "head"), "batch", None),
            P(),
            P(),
            P(None, "head"),
            P("head"),
            P(),
            P(),
            P("head", None),
            P(),
            P(),
            P(),
            P(),
            P(),
            P(),
            P(),
            P("batch", None),
            P(("seq", "head"), "batch", None),
        ),
        out_specs=(
            P(("seq", "head"), "batch", None),
            P(("seq", "head"), "batch", None),
            P(),
            P(),
            P(None, "head"),
            P("head"),
            P(),
            P(),
            P("head", None),
            P(),
            P(),
            P(),
            P(),
            P(),
            P(),
            P(),
        ),
        check_vma=False,
    )
```

```python
from functools import partial
import math

import jax
import jax.numpy as jnp
from jax import lax
from jax.experimental import pallas as pl
from jax.experimental.pallas import tpu as pltpu
from jax.sharding import PartitionSpec as P

EPSILON = 1e-05
MASKED = -1e30
BF = jnp.bfloat16
F32 = jnp.float32
LOG2E = math.log2(math.e)


def layer_norm(inputs, norm_gain, norm_shift):
    center = inputs - jnp.mean(inputs, axis=-1, keepdims=True)
    spread = jnp.mean(center * center, axis=-1, keepdims=True)
    return center * lax.rsqrt(spread + EPSILON) * norm_gain + norm_shift


def swap(value, step):
    axis, flip = step
    size = lax.axis_size(axis)
    return lax.ppermute(value, axis, [(i, i ^ flip) for i in range(size)])


def bit_of(step):
    axis, flip = step
    return (lax.axis_index(axis) // flip) % 2


def split_dim(shape):
    if (shape[0] // 2) % 8 == 0:
        return 0
    return 1


def add_low(kept, got):
    return (kept.astype(F32) + got.astype(F32)).astype(kept.dtype)


def tie(*trees):
    leaves, shape = jax.tree.flatten(trees)
    return jax.tree.unflatten(shape, lax.optimization_barrier(leaves))


def halve(arrays, step):
    bit = bit_of(step)
    dims = [split_dim(a.shape) for a in arrays]
    halves = [a.shape[d] // 2 for a, d in zip(arrays, dims)]
    sent = [lax.dynamic_slice_in_dim(a, (1 - bit) * h, h, d) for a, h, d in zip(arrays, halves, dims)]
    kept = [lax.dynamic_slice_in_dim(a, bit * h, h, d) for a, h, d in zip(arrays, halves, dims)]
    return [add_low(k, g) for k, g in zip(kept, swap_all(sent, step))], dims


def swap_all(arrays, step):
    if len({a.shape[1] for a in arrays}) > 1:
        return [swap(a, step) for a in arrays]
    got = swap(jnp.concatenate(arrays, 0) if len(arrays) > 1 else arrays[0], step)
    at, out = 0, []
    for a in arrays:
        out.append(got[at : at + a.shape[0]])
        at += a.shape[0]
    return out


def double(arrays, step, dims):
    got = swap_all(arrays, step)
    first = bit_of(step) == 0
    return [
        jnp.concatenate([jnp.where(first, a, g), jnp.where(first, g, a)], d) for a, g, d in zip(arrays, got, dims)
    ]


def dot(a, b, dims):
    return lax.dot_general(a, b, (dims, ((), ())), preferred_element_type=F32)


def side_by_side(rows, heads, hd):
    return jnp.concatenate([rows[h * hd : (h + 1) * hd, :] for h in range(heads)], axis=1)


def chunk_pos(me, j, chunk, tq):
    base = ((me * tq) // chunk) ^ j
    rows = lax.broadcasted_iota(jnp.int32, (chunk, tq), 0)
    return base * chunk, base * chunk + (rows ^ ((me * tq) % chunk))


def forward_kernel(scal, q_ref, kv_ref, lo_ref, out_ref, lse_ref, m_s, l_s, acc_s, *, heads, hd, chunk):
    w = pl.program_id(0)
    me = scal[0]
    tq = q_ref.shape[2]
    lo_min = scal[1 + w]
    first = me * tq
    scale2 = LOG2E / math.sqrt(hd)
    zeros = jnp.zeros((hd, tq), BF)
    lo = lo_ref[0]
    query = first + lax.broadcasted_iota(jnp.int32, (chunk, tq), 1)
    m_s[...] = jnp.full(m_s.shape, MASKED, F32)
    l_s[...] = jnp.zeros(l_s.shape, F32)
    acc_s[...] = jnp.zeros(acc_s.shape, F32)

    def body(j, carry):
        base, pos = chunk_pos(me, j, chunk, tq)

        @pl.when((base < first + tq) & (base + chunk > lo_min))
        def _():
            kv = kv_ref[0, pl.ds(pl.multiple_of(j * chunk, chunk), chunk), :]
            kv_t = kv.T
            allowed = (pos >= lo) & (pos <= query)
            for h in range(heads):
                cols = slice(h * tq, (h + 1) * tq)
                q_pad = jnp.concatenate([q_ref[0, h * hd : (h + 1) * hd, :], zeros], axis=0)
                s = jnp.where(allowed, dot(kv, q_pad, ((1,), (0,))), MASKED)
                m_old = m_s[:, cols]
                m_new = jnp.maximum(m_old, jnp.max(s, axis=0, keepdims=True))
                p = jnp.exp2((s - m_new) * scale2)
                alpha = jnp.exp2((m_old - m_new) * scale2)
                m_s[:, cols] = m_new
                l_s[:, cols] = l_s[:, cols] * alpha + jnp.sum(p, axis=0, keepdims=True)
                pv = dot(kv_t, p.astype(BF), ((1,), (0,)))
                acc_s[:, cols] = acc_s[:, cols] * alpha + pv[hd:, :]

        return carry

    lax.fori_loop(0, kv_ref.shape[1] // chunk, body, 0)
    total = l_s[...]
    out = acc_s[...] / total
    lse_ref[0] = m_s[...] * scale2 + jnp.log2(total)
    for h in range(heads):
        out_ref[0, h * hd : (h + 1) * hd, :] = out[:, h * tq : (h + 1) * tq].astype(BF)


def backward_kernel(
    scal, q_ref, kv_ref, lo_ref, out_ref, lse_ref, do_ref, dq_ref, *refs, heads, hd, chunk
):
    *dkv_refs, qx_s, dox_s, dq_s, p_s, ds_s = refs
    w = pl.program_id(0)
    me = scal[0]
    tq = q_ref.shape[2]
    lo_min = scal[1 + w]
    first = me * tq
    scale = 1.0 / math.sqrt(hd)
    scale2 = LOG2E * scale
    group = 2
    lanes = group * tq
    lo = lo_ref[0]
    query = first + lax.broadcasted_iota(jnp.int32, (chunk, tq), 1)
    dq_s[...] = jnp.zeros(dq_s.shape, F32)
    row = lax.broadcasted_iota(jnp.int32, (hd, tq), 0)

    def terms(value):
        out = jnp.zeros((hd, tq), F32)
        for i in range(3):
            part = value.astype(BF).astype(F32)
            out = jnp.where(row == i, part, out)
            value = value - part
        return out.astype(BF)

    for h in range(heads):
        rows, cols = slice(h * hd, (h + 1) * hd), slice(h * tq, (h + 1) * tq)
        do = do_ref[0, rows, :]
        delta = jnp.sum(out_ref[0, rows, :].astype(F32) * do.astype(F32), axis=0, keepdims=True)
        qx_s[:hd, cols] = q_ref[0, rows, :]
        qx_s[hd:, cols] = terms(lse_ref[0, :, cols] * (-1.0 / scale2))
        dox_s[:hd, cols] = terms(-delta)
        dox_s[hd:, cols] = do
    lane = lax.broadcasted_iota(jnp.int32, (chunk, 2 * hd), 1)

    def body(j, carry):
        base, pos = chunk_pos(me, j, chunk, tq)
        here = pl.ds(pl.multiple_of(j * chunk, chunk), chunk)
        needed = (base < first + tq) & (base + chunk > lo_min)

        def store(value):
            kept_a, sent_a, kept_b, sent_b = dkv_refs

            @pl.when(w < pl.num_programs(0) // 2)
            def _():
                rows = pl.ds(pl.multiple_of(j * tq, tq), tq)
                kept_a[0, rows, :] = value[:tq]
                sent_a[0, rows, :] = value[tq:]

            @pl.when(w >= pl.num_programs(0) // 2)
            def _():
                rows = pl.ds(pl.multiple_of((j // 2) * chunk, chunk), chunk)

                @pl.when(j % 2 == 0)
                def _():
                    kept_b[0, rows, :] = value

                @pl.when(j % 2 == 1)
                def _():
                    sent_b[0, rows, :] = value

        @pl.when(jnp.logical_not(needed))
        def _():
            store(jnp.zeros((chunk, 2 * hd), BF))

        @pl.when(needed)
        def _():
            kv = kv_ref[0, here, :]
            one, nought = jnp.ones_like(kv), jnp.zeros_like(kv)
            key_one = jnp.where(lane < hd, kv, jnp.where(lane < hd + 3, one, nought))
            one_value = jnp.where(lane >= hd, kv, jnp.where(lane < 3, one, nought))
            allowed = (pos >= lo) & (pos <= query)
            allowed = jnp.concatenate([allowed] * group, axis=1)
            for g in range(heads // group):
                cols = slice(g * lanes, (g + 1) * lanes)
                p = jnp.exp2(dot(key_one, qx_s[:, cols], ((1,), (0,))) * scale2)
                p = jnp.where(allowed, p, 0.0)
                ds_s[:, cols] = (p * dot(one_value, dox_s[:, cols], ((1,), (0,)))).astype(BF)
                p_s[:, cols] = p.astype(BF)
            dk = dot(ds_s[...], qx_s[...], ((1,), (1,)))
            dv = dot(p_s[...], dox_s[...], ((1,), (1,)))
            dq_s[...] = dq_s[...] + dot(kv.T, ds_s[...], ((1,), (0,)))[:hd, :]
            dkv = jnp.where(lane < hd, dk * scale, dv)
            store(dkv.astype(BF))

        return carry

    lax.fori_loop(0, kv_ref.shape[1] // chunk, body, 0)
    for h in range(heads):
        dq_ref[0, h * hd : (h + 1) * hd, :] = (dq_s[:, h * tq : (h + 1) * tq] * scale).astype(BF)


def assemble_kernel(core, own, *refs, first, wide, count):
    out = refs[-1]
    i = pl.program_id(0)

    @pl.when(i < first)
    def _():
        out[...] = own[...].astype(F32)

    @pl.when(i >= first)
    def _():
        for c in range(count):
            out[:, c * wide : (c + 1) * wide] = refs[c][...].astype(F32)


def assemble(core, own, mix, previous, shape, block, wide, skip, name):
    by_rows = block[1] == shape[1]
    axis = 0 if by_rows else 1
    first = own.shape[axis] // block[axis]
    second = (shape[axis] - 2 * own.shape[axis]) // block[axis] // 2
    count = block[1] // wide

    def at(place):
        return (place, 0) if by_rows else (0, place)

    def mix_at(c):
        return lambda i, core: (skip // block[0] + c * second * by_rows + c * (not by_rows) + jnp.maximum(i - first, 0), 0)

    def out_at(i, core):
        return at(jnp.where(i < first, core[0] * first + i, 2 * first + core[0] * second + i - first))

    in_specs = [pl.BlockSpec(block, lambda i, core: at(jnp.minimum(i, first - 1)))]
    in_specs += [pl.BlockSpec((block[0], wide), mix_at(c)) for c in range(count)]
    arrays = [own, *[mix] * count]
    if previous is not None:
        in_specs.append(pl.BlockSpec(memory_space=pl.ANY))
        arrays.append(previous)
    return pl.pallas_call(
        partial(assemble_kernel, first=first, wide=wide, count=count),
        out_shape=jax.ShapeDtypeStruct(shape, F32),
        grid_spec=pltpu.PrefetchScalarGridSpec(
            num_scalar_prefetch=1,
            grid=(first + second,),
            in_specs=in_specs,
            out_specs=pl.BlockSpec(block, out_at),
        ),
        input_output_aliases={} if previous is None else {len(arrays): 0},
        compiler_params=pltpu.CompilerParams(vmem_limit_bytes=16 << 20),
        cost_estimate=pl.CostEstimate(flops=0, bytes_accessed=3 * shape[0] * shape[1], transcendentals=0),
        name=name,
    )(core, *arrays)


def per_window(shape):
    zeros = (0,) * (len(shape) - 1)
    return pl.BlockSpec((1, *shape[1:]), lambda w, scal: (w, *zeros))


def half_windows(shape, late):
    zeros = (0,) * (len(shape) - 1)
    if late:
        return pl.BlockSpec((1, *shape[1:]), lambda w, scal: (jnp.maximum(w - shape[0], 0), *zeros))
    return pl.BlockSpec((1, *shape[1:]), lambda w, scal: (jnp.minimum(w, shape[0] - 1), *zeros))


def attention_call(kernel, scalars, inputs, outs, scratch, name, flops, halves=0):
    vmem = (12 << 20) + 10 * math.prod(inputs[1].shape[1:]) * inputs[1].dtype.itemsize
    moved = sum(math.prod(a.shape) * a.dtype.itemsize for a in (*inputs, *outs))
    return pl.pallas_call(
        kernel,
        out_shape=outs,
        grid_spec=pltpu.PrefetchScalarGridSpec(
            num_scalar_prefetch=1,
            grid=(inputs[0].shape[0],),
            in_specs=[per_window(a.shape) for a in inputs],
            out_specs=[per_window(a.shape) for a in outs[: len(outs) - halves]]
            + [half_windows(a.shape, i >= halves // 2) for i, a in enumerate(outs[len(outs) - halves :])],
            scratch_shapes=scratch,
        ),
        compiler_params=pltpu.CompilerParams(vmem_limit_bytes=vmem),
        cost_estimate=pl.CostEstimate(flops=flops, bytes_accessed=moved, transcendentals=0),
        name=name,
    )(scalars, *inputs)


def local(
    tokens,
    attn_gain,
    attn_shift,
    w_query,
    b_query,
    w_keyval,
    b_value,
    w_out,
    b_out,
    mlp_gain,
    mlp_shift,
    w_up,
    b_up,
    w_down,
    b_down,
    doc_lengths,
    cotangent,
):
    tq, windows, width = tokens.shape
    hd = w_keyval.shape[1] // 2
    own_cols = w_query.shape[1]
    seq_size = lax.axis_size("seq")
    cols = own_cols * lax.axis_size("head")
    heads = cols // hd
    seq_total = tq * seq_size * lax.axis_size("head")
    me = lax.axis_index("seq") * lax.axis_size("head") + lax.axis_index("head")
    chunk = min(2 * tq, seq_total)

    core = ("batch", 1)
    head = ("head", 1)
    low = ("seq", 1)
    highs = [("seq", 1 << i) for i in range(1, int(math.log2(seq_size)))]

    def other_half(weight):
        half = weight.shape[0] // 2
        part = lax.dynamic_slice_in_dim(weight, lax.axis_index("batch") * half, half, 0)
        return double([swap(part, head)], core, [0])[0]

    wq_other = other_half(w_query)
    bq_other = swap(b_query, head)
    head_first = bit_of(head) == 0

    def in_order(own, other, dim):
        return jnp.concatenate([jnp.where(head_first, own, other), jnp.where(head_first, other, own)], dim)

    wq_all = in_order(w_query, wq_other, 1)
    bq_all = in_order(b_query, bq_other, 0)

    bounds = jnp.cumsum(doc_lengths, axis=1)
    places = me * tq + jnp.arange(tq, dtype=jnp.int32)
    starts = jnp.max(
        jnp.where(bounds[:, :, None] <= places[None, None, :], bounds[:, :, None], 0), axis=1
    )
    scalars = jnp.concatenate([me[None].astype(jnp.int32), starts[:, 0]])
    starts = starts[:, None, :]

    residual = jnp.transpose(tokens, (1, 0, 2)).astype(F32)
    normed = layer_norm(residual, attn_gain, attn_shift).astype(BF)
    value_bias = jnp.concatenate([jnp.zeros((hd,), F32), b_value])
    keyval = (
        jnp.einsum("wtd,dc->wtc", normed, w_keyval, preferred_element_type=F32) + value_bias
    ).astype(BF)

    bits = [*reversed(highs), low, head]

    def gather_step(block, step):
        return jnp.concatenate([block, swap(block, step)], 1 + bits.index(step))

    def reduce_block(block, step):
        kept, sent = jnp.split(block, 2, 1 + bits.index(step))
        return add_low(kept, swap(sent, step))

    half_w = windows // 2
    block = keyval.reshape(windows, *[1] * len(bits), tq, 2 * hd)
    for step in reversed(highs):
        block = gather_step(block, step)
    keyval_all = jnp.concatenate(
        [
            gather_step(gather_step(block[:half_w], low), head).reshape(half_w, seq_total, 2 * hd),
            gather_step(gather_step(block[half_w:], head), low).reshape(half_w, seq_total, 2 * hd),
        ],
        0,
    )
    keyval_all, w_out = tie(keyval_all, w_out)
    wo_all = in_order(w_out, swap(w_out, head), 0)

    queries = (
        jnp.einsum("do,wtd->wot", wq_all, normed, preferred_element_type=F32) + bq_all[None, :, None]
    ).astype(BF)

    struct = jax.ShapeDtypeStruct
    lanes = heads * tq
    work = 2 * windows * lanes * (seq_total // 4) * hd
    mixed, log_total = attention_call(
        partial(forward_kernel, heads=heads, hd=hd, chunk=chunk),
        scalars,
        (queries, keyval_all, starts),
        (struct((windows, cols, tq), BF), struct((windows, 1, lanes), F32)),
        [pltpu.VMEM((1, lanes), F32), pltpu.VMEM((1, lanes), F32), pltpu.VMEM((hd, lanes), F32)],
        "attend",
        8 * work,
    )

    branch = jnp.einsum("wot,od->wtd", mixed, wo_all, preferred_element_type=F32)
    middle = residual + (branch + b_out)
    inner = layer_norm(middle, mlp_gain, mlp_shift).astype(BF)
    upstream_low = jnp.transpose(cotangent, (1, 0, 2))
    upstream = upstream_low.astype(F32)

    upward = jnp.einsum("wtd,df->wtf", inner, w_up, preferred_element_type=F32) + b_up
    active = jax.nn.gelu(upward, approximate=True).astype(BF)
    grad_active = jnp.einsum("wtd,fd->wtf", upstream_low, w_down, preferred_element_type=F32)
    gelu_back = jax.vjp(partial(jax.nn.gelu, approximate=True), upward)[1]
    grad_upward = gelu_back(grad_active)[0].astype(BF)

    ff = w_up.shape[1]
    cut = 2 * ff // 3
    spans = (0, cut // 2), (cut, (ff - cut) // 2)
    on_first = bit_of(core) == 0

    def columns(array, span, other):
        first, size = span
        start = first + size * (bit_of(core) ^ other)
        return lax.dynamic_slice_in_dim(array, start, size, 2)

    def part_down(span, other):
        return jnp.einsum("wtf,wtd->fd", columns(active, span, other), upstream_low, preferred_element_type=F32)

    def part_up(span, other):
        return jnp.einsum("wtd,wtf->df", inner, columns(grad_upward, span, other), preferred_element_type=F32)

    def own_part(make, span, got):
        return (make(span, 0) + got.astype(F32)).astype(BF)

    wide = math.gcd(spans[1][1], width)

    def stack(array):
        return jnp.concatenate([array[:, at : at + wide] for at in range(0, array.shape[1], wide)], 0)

    def unstack(array, rows):
        return jnp.concatenate([array[at : at + rows] for at in range(0, array.shape[0], rows)], 1)

    got_down = swap(part_down(spans[0], 1).astype(BF), core)
    got_up = swap(part_up(spans[0], 1).astype(BF), core)
    got_mix = swap(
        jnp.concatenate([stack(part_down(spans[1], 1).astype(BF)), stack(part_up(spans[1], 1).astype(BF))], 0), core
    )
    rows_mix = spans[1][1]
    rows_down = rows_mix * (width // wide)
    pieces = [
        own_part(part_down, spans[0], got_down),
        own_part(part_up, spans[0], got_up),
        jnp.concatenate(
            [
                stack(own_part(part_down, spans[1], unstack(got_mix[:rows_down], rows_mix))),
                stack(own_part(part_up, spans[1], unstack(got_mix[rows_down:], width))),
            ],
            0,
        ),
    ]

    grad_inner = jnp.einsum("wtf,df->wtd", grad_upward, w_up, preferred_element_type=F32)
    norm_back = jax.vjp(layer_norm, middle, mlp_gain, mlp_shift)[1]
    grad_mid_norm, grad_mlp_gain, grad_mlp_shift = norm_back(grad_inner)
    grad_middle = upstream + grad_mid_norm
    grad_branch = grad_middle.astype(BF)
    grad_mixed = jnp.einsum("od,wtd->wot", wo_all, grad_branch, preferred_element_type=F32).astype(BF)

    own_rows = own_cols // 2

    def core_halves(array):
        array = array.reshape(cols // own_cols, 2, own_rows, width)
        sent = lax.dynamic_index_in_dim(array, 1 - bit_of(core), 1, False)
        kept = lax.dynamic_index_in_dim(array, bit_of(core), 1, False)
        return add_low(kept, swap(sent, core))

    grad_w_out = jnp.einsum("wot,wtd->od", mixed, grad_branch, preferred_element_type=F32).astype(BF)
    out_half = core_halves(grad_w_out)
    out_half = jnp.concatenate([stack(out_half[h]) for h in range(cols // own_cols)], 0)

    near, far = highs[0], highs[1:]
    orders = [near, low, head, *far], [low, head, near, *far], [head, near, low, *far]
    last = len(orders[0]) - 1
    groups = [[pieces[0]], [pieces[1]], [pieces[2], out_half]]
    dims = [[], [], []]

    def reduce_step(at):
        for i in range(3):
            groups[i], dim = halve(groups[i], orders[i][at])
            dims[i].append(dim)

    groups, grad_mixed = tie(groups, grad_mixed)
    reduce_step(0)
    half_keys = struct((half_w, seq_total // 2, 2 * hd), BF)
    grad_queries, *grad_keys = attention_call(
        partial(backward_kernel, heads=heads, hd=hd, chunk=chunk),
        scalars,
        (queries, keyval_all, starts, mixed, log_total, grad_mixed),
        (struct((windows, cols, tq), BF), *[half_keys] * 4),
        [pltpu.VMEM((2 * hd, lanes), BF)] * 2 + [pltpu.VMEM((hd, lanes), F32)] + [pltpu.VMEM((chunk, lanes), BF)] * 2,
        "attend_back",
        20 * work,
        4,
    )
    groups, grad_queries, grad_keys = tie(groups, grad_queries, grad_keys)

    def open_blocks(value, step):
        sides = [1 if other == step else 2 for other in bits]
        return value.reshape(half_w, *sides, tq, 2 * hd)

    def part_query(other):
        half = width // 2
        rows = lax.dynamic_slice_in_dim(normed, half * (bit_of(core) ^ other), half, 2)
        return jnp.einsum("wtd,wot->do", rows, later_queries, preferred_element_type=F32)

    kept_a, sent_a, kept_b, sent_b = grad_keys
    reduce_step(1)
    blocks = [add_low(kept_a, swap(sent_a, head)), add_low(kept_b, swap(sent_b, low))]
    blocks = [open_blocks(blocks[0], head), open_blocks(blocks[1], low)]
    groups, blocks, later_queries = tie(groups, blocks, grad_queries)

    reduce_step(2)
    blocks = [reduce_block(blocks[0], low), reduce_block(blocks[1], head)]
    sent_query = part_query(1).astype(BF)
    groups, blocks, sent_query, active, grad_upward, grad_branch, upstream, later_queries = tie(
        groups, blocks, sent_query, active, grad_upward, grad_branch, upstream, later_queries
    )

    for step in far[:-1]:
        groups = [[add_low(a, g) for a, g in zip(group, swap_all(group, step))] for group in groups]
    far_got = [None, *[swap_all(group, far[-1]) for group in groups[1:]]]
    blocks = reduce_block(jnp.concatenate(blocks, 0), near)
    got_query = swap(sent_query, core)
    query_half = (part_query(0) + got_query.astype(F32)).astype(BF)
    blocks, query_half, active, grad_upward, grad_branch, upstream, later_queries = tie(
        blocks, query_half, active, grad_upward, grad_branch, upstream, later_queries
    )

    for step in far:
        blocks = reduce_block(blocks, step)
    own_head = lax.axis_index("head")
    sent = lax.dynamic_slice_in_dim(query_half, own_cols * (1 - own_head), own_cols, 1)
    kept = lax.dynamic_slice_in_dim(query_half, own_cols * own_head, own_cols, 1)
    query_half = add_low(kept, swap(sent, head))
    result = (
        middle + (jnp.einsum("wtf,fd->wtd", active, w_down, preferred_element_type=F32) + b_down)
    ).astype(BF)
    result = jnp.transpose(result, (1, 0, 2))
    grad_b_up = jnp.sum(grad_upward.astype(F32), axis=(0, 1))
    grad_b_down = jnp.sum(upstream, axis=(0, 1))
    grad_b_out = jnp.sum(grad_branch.astype(F32), axis=(0, 1))
    grad_b_query = jnp.sum(later_queries.astype(F32), axis=(0, 2))
    vectors = [grad_b_up, grad_b_down, grad_mlp_gain, grad_mlp_shift, grad_b_out, grad_b_query]
    blocks, query_half, result, vectors, groups = tie(blocks, query_half, result, vectors, groups)
    far_got[0] = swap_all(groups[0], far[-1])
    grad_keyval = blocks.reshape(windows, tq, 2 * hd)

    grad_w_keyval = jnp.einsum("wtd,wtc->dc", normed, grad_keyval, preferred_element_type=F32)
    grad_b_value = jnp.sum(grad_keyval[:, :, hd:].astype(F32), axis=(0, 1))
    grad_normed = jnp.einsum("wot,do->wtd", grad_queries, wq_all, preferred_element_type=F32)
    grad_normed = grad_normed + jnp.einsum(
        "wtc,dc->wtd", grad_keyval, w_keyval, preferred_element_type=F32
    )
    first_back = jax.vjp(layer_norm, residual, attn_gain, attn_shift)[1]
    grad_input, grad_attn_gain, grad_attn_shift = first_back(grad_normed)
    grad_tokens = jnp.transpose(grad_middle + grad_input, (1, 0, 2))

    def rows_of(vector):
        vector = jnp.pad(vector.astype(F32), (0, (-vector.shape[0]) % width))
        return [vector[at : at + width] for at in range(0, vector.shape[0], width)]

    vectors = [*vectors, grad_attn_gain, grad_attn_shift, grad_b_value]
    rows = [row for vector in vectors for row in rows_of(vector)]
    tall = -(-len(rows) // 16) * 16
    place = lax.broadcasted_iota(jnp.int32, (tall, width), 0)
    packed = jnp.zeros((tall, width), F32)
    for at, row in enumerate(rows):
        packed = jnp.where(place == at, row[None, :], packed)
    small = jnp.concatenate([grad_w_keyval, *[packed[:, at : at + 2 * hd] for at in range(0, width, 2 * hd)]], 0)
    small = small.astype(BF)

    def stack_small(array):
        count = wide // array.shape[1]
        tall = array.shape[0] // count
        return jnp.concatenate([array[at : at + tall] for at in range(0, array.shape[0], tall)], 1)

    def unstack_small(array):
        return jnp.concatenate([array[:, at : at + 2 * hd] for at in range(0, array.shape[1], 2 * hd)], 0)

    (small,), small_dim = halve([small], core)
    small = stack_small(small)
    far_got, small, query_half, grad_tokens = tie(far_got, small, query_half, grad_tokens)
    groups = [[add_low(a, g) for a, g in zip(group, got)] for group, got in zip(groups, far_got)]
    groups, small = tie(groups, small)

    def gather_step(at, join=None):
        for i in range(2):
            groups[i] = double(groups[i], orders[i][at], dims[i][at][: len(groups[i])])
        step = orders[2][at]
        got = swap_all(groups[2] if join is None else [*groups[2], join], step)
        lower = bit_of(step) == 0
        groups[2] = [
            jnp.concatenate([jnp.where(lower, a, g), jnp.where(lower, g, a)], d)
            for a, g, d in zip(groups[2], got, dims[2][at])
        ]
        return join if join is None else add_low(join, got[-1])

    small = gather_step(2, small)
    (query_half,), query_dim = halve([query_half], low)
    groups, small, query_half, grad_tokens = tie(groups, small, query_half, grad_tokens)

    small = gather_step(1, small)
    query_half = add_low(query_half, swap(query_half, near))
    groups, small, query_half = tie(groups, small, query_half)

    def both(own, other, dim):
        own, other = own.astype(F32), other.astype(F32)
        return [jnp.where(on_first, own, other), jnp.where(on_first, other, own)]

    out_half = groups[2].pop()
    for step in far:
        query_half = add_low(query_half, swap(query_half, step))
    small = gather_step(0, small)
    (query_half,) = double([query_half], low, query_dim)
    query_other = swap(query_half, core)
    out_other = swap(out_half, core)
    out_half, out_other = unstack(out_half, own_rows), unstack(out_other, own_rows)
    grad_w_out = jnp.concatenate(both(out_half, out_other, 0), 0)
    groups, small, grad_w_out, query_half, query_other = tie(groups, small, grad_w_out, query_half, query_other)

    (down,), (up,), (mix,) = groups
    got_down, got_mix, got_up = swap(down, core), swap(mix, core), swap(up, core)
    for step in far:
        small = add_low(small, swap(small, step))
    (small,) = double([unstack_small(small)], core, small_dim)
    small = small.astype(F32)
    grad_w_keyval, packed = small[:width], small[width:]
    packed = jnp.concatenate([packed[at : at + tall] for at in range(0, packed.shape[0], tall)], 1)
    sums, at = [], 0
    for vector in vectors:
        count = -(-vector.shape[0] // width)
        sums.append(packed[at : at + count].reshape(-1)[: vector.shape[0]])
        at += count
    sums[5] = lax.dynamic_slice_in_dim(sums[5], lax.axis_index("head") * own_cols, own_cols, 0)
    where = lax.axis_index("batch")[None].astype(jnp.int32)
    down_block, up_block = (rows_mix // 2, width), (width, rows_mix)
    own_down = assemble(where, down, mix, None, (ff, width), down_block, wide, 0, "own_down")
    own_up = assemble(where, up, mix, None, (width, ff), up_block, wide, rows_down, "own_up")
    got_down, got_mix, got_up, own_down, own_up = tie(got_down, got_mix, got_up, own_down, own_up)
    grad_w_down = assemble(1 - where, got_down, got_mix, own_down, (ff, width), down_block, wide, 0, "got_down")
    grad_w_up = assemble(1 - where, got_up, got_mix, own_up, (width, ff), up_block, wide, rows_down, "got_up")

    grad_w_query = jnp.concatenate(both(query_half, query_other, 0), 0)
    b_up_sum, b_down_sum, mlp_gain_sum, mlp_shift_sum, b_out_sum, b_query_sum, gain_sum, shift_sum, b_value_sum = sums

    return (
        result,
        grad_tokens,
        gain_sum,
        shift_sum,
        grad_w_query,
        b_query_sum,
        grad_w_keyval,
        b_value_sum,
        grad_w_out,
        b_out_sum,
        mlp_gain_sum,
        mlp_shift_sum,
        grad_w_up,
        b_up_sum,
        grad_w_down,
        b_down_sum,
    )


def solution(mesh):
    return jax.shard_map(
        local,
        mesh=mesh,
        in_specs=(
            P(("seq", "head"), "batch", None),
            P(),
            P(),
            P(None, "head"),
            P("head"),
            P(),
            P(),
            P("head", None),
            P(),
            P(),
            P(),
            P(),
            P(),
            P(),
            P(),
            P("batch", None),
            P(("seq", "head"), "batch", None),
        ),
        out_specs=(
            P(("seq", "head"), "batch", None),
            P(("seq", "head"), "batch", None),
            P(),
            P(),
            P(None, "head"),
            P("head"),
            P(),
            P(),
            P("head", None),
            P(),
            P(),
            P(),
            P(),
            P(),
            P(),
            P(),
        ),
        check_vma=False,
    )
```

```python
from functools import partial
import math

import jax
import jax.numpy as jnp
from jax import lax
from jax.experimental import pallas as pl
from jax.experimental.pallas import tpu as pltpu
from jax.sharding import PartitionSpec as P

EPSILON = 1e-05
MASKED = -1e30
BF = jnp.bfloat16
F32 = jnp.float32
LOG2E = math.log2(math.e)


def layer_norm(inputs, norm_gain, norm_shift):
    center = inputs - jnp.mean(inputs, axis=-1, keepdims=True)
    spread = jnp.mean(center * center, axis=-1, keepdims=True)
    return center * lax.rsqrt(spread + EPSILON) * norm_gain + norm_shift


def swap(value, step):
    axis, flip = step
    size = lax.axis_size(axis)
    return lax.ppermute(value, axis, [(i, i ^ flip) for i in range(size)])


def bit_of(step):
    axis, flip = step
    return (lax.axis_index(axis) // flip) % 2


def split_dim(shape):
    if (shape[0] // 2) % 8 == 0:
        return 0
    return 1


def add_low(kept, got):
    return (kept.astype(F32) + got.astype(F32)).astype(kept.dtype)


def tie(*trees):
    leaves, shape = jax.tree.flatten(trees)
    return jax.tree.unflatten(shape, lax.optimization_barrier(leaves))


def halve(arrays, step):
    bit = bit_of(step)
    dims = [split_dim(a.shape) for a in arrays]
    halves = [a.shape[d] // 2 for a, d in zip(arrays, dims)]
    sent = [lax.dynamic_slice_in_dim(a, (1 - bit) * h, h, d) for a, h, d in zip(arrays, halves, dims)]
    kept = [lax.dynamic_slice_in_dim(a, bit * h, h, d) for a, h, d in zip(arrays, halves, dims)]
    return [add_low(k, g) for k, g in zip(kept, swap_all(sent, step))], dims


def swap_all(arrays, step):
    if len({a.shape[1] for a in arrays}) > 1:
        return [swap(a, step) for a in arrays]
    got = swap(jnp.concatenate(arrays, 0) if len(arrays) > 1 else arrays[0], step)
    at, out = 0, []
    for a in arrays:
        out.append(got[at : at + a.shape[0]])
        at += a.shape[0]
    return out


def double(arrays, step, dims):
    got = swap_all(arrays, step)
    first = bit_of(step) == 0
    return [
        jnp.concatenate([jnp.where(first, a, g), jnp.where(first, g, a)], d) for a, g, d in zip(arrays, got, dims)
    ]


def dot(a, b, dims):
    return lax.dot_general(a, b, (dims, ((), ())), preferred_element_type=F32)


def side_by_side(rows, heads, hd):
    return jnp.concatenate([rows[h * hd : (h + 1) * hd, :] for h in range(heads)], axis=1)


def chunk_pos(me, j, chunk, tq):
    base = ((me * tq) // chunk) ^ j
    rows = lax.broadcasted_iota(jnp.int32, (chunk, tq), 0)
    return base * chunk, base * chunk + (rows ^ ((me * tq) % chunk))


def forward_kernel(scal, q_ref, kv_ref, lo_ref, out_ref, lse_ref, m_s, l_s, acc_s, *, heads, hd, chunk):
    w = pl.program_id(0)
    me = scal[0]
    tq = q_ref.shape[2]
    lo_min = scal[1 + w]
    first = me * tq
    scale2 = LOG2E / math.sqrt(hd)
    zeros = jnp.zeros((hd, tq), BF)
    lo = lo_ref[0]
    query = first + lax.broadcasted_iota(jnp.int32, (chunk, tq), 1)
    m_s[...] = jnp.full(m_s.shape, MASKED, F32)
    l_s[...] = jnp.zeros(l_s.shape, F32)
    acc_s[...] = jnp.zeros(acc_s.shape, F32)

    def body(j, carry):
        base, pos = chunk_pos(me, j, chunk, tq)

        @pl.when((base < first + tq) & (base + chunk > lo_min))
        def _():
            kv = kv_ref[0, pl.ds(pl.multiple_of(j * chunk, chunk), chunk), :]
            kv_t = kv.T
            allowed = (pos >= lo) & (pos <= query)
            for h in range(heads):
                cols = slice(h * tq, (h + 1) * tq)
                q_pad = jnp.concatenate([q_ref[0, h * hd : (h + 1) * hd, :], zeros], axis=0)
                s = jnp.where(allowed, dot(kv, q_pad, ((1,), (0,))), MASKED)
                m_old = m_s[:, cols]
                m_new = jnp.maximum(m_old, jnp.max(s, axis=0, keepdims=True))
                p = jnp.exp2((s - m_new) * scale2)
                alpha = jnp.exp2((m_old - m_new) * scale2)
                m_s[:, cols] = m_new
                l_s[:, cols] = l_s[:, cols] * alpha + jnp.sum(p, axis=0, keepdims=True)
                pv = dot(kv_t, p.astype(BF), ((1,), (0,)))
                acc_s[:, cols] = acc_s[:, cols] * alpha + pv[hd:, :]

        return carry

    lax.fori_loop(0, kv_ref.shape[1] // chunk, body, 0)
    total = l_s[...]
    out = acc_s[...] / total
    lse_ref[0] = m_s[...] * scale2 + jnp.log2(total)
    for h in range(heads):
        out_ref[0, h * hd : (h + 1) * hd, :] = out[:, h * tq : (h + 1) * tq].astype(BF)


def backward_kernel(
    scal, q_ref, kv_ref, lo_ref, out_ref, lse_ref, do_ref, dq_ref, *refs, heads, hd, chunk
):
    *dkv_refs, qx_s, dox_s, dq_s, p_s, ds_s = refs
    w = pl.program_id(0)
    me = scal[0]
    tq = q_ref.shape[2]
    lo_min = scal[1 + w]
    first = me * tq
    scale = 1.0 / math.sqrt(hd)
    scale2 = LOG2E * scale
    group = 2
    lanes = group * tq
    lo = lo_ref[0]
    query = first + lax.broadcasted_iota(jnp.int32, (chunk, tq), 1)
    dq_s[...] = jnp.zeros(dq_s.shape, F32)
    row = lax.broadcasted_iota(jnp.int32, (hd, tq), 0)

    def terms(value):
        out = jnp.zeros((hd, tq), F32)
        for i in range(3):
            part = value.astype(BF).astype(F32)
            out = jnp.where(row == i, part, out)
            value = value - part
        return out.astype(BF)

    for h in range(heads):
        rows, cols = slice(h * hd, (h + 1) * hd), slice(h * tq, (h + 1) * tq)
        do = do_ref[0, rows, :]
        delta = jnp.sum(out_ref[0, rows, :].astype(F32) * do.astype(F32), axis=0, keepdims=True)
        qx_s[:hd, cols] = q_ref[0, rows, :]
        qx_s[hd:, cols] = terms(lse_ref[0, :, cols] * (-1.0 / scale2))
        dox_s[:hd, cols] = terms(-delta)
        dox_s[hd:, cols] = do
    lane = lax.broadcasted_iota(jnp.int32, (chunk, 2 * hd), 1)

    def body(j, carry):
        base, pos = chunk_pos(me, j, chunk, tq)
        here = pl.ds(pl.multiple_of(j * chunk, chunk), chunk)
        needed = (base < first + tq) & (base + chunk > lo_min)

        def store(value):
            kept_a, sent_a, kept_b, sent_b = dkv_refs

            @pl.when(w < pl.num_programs(0) // 2)
            def _():
                rows = pl.ds(pl.multiple_of(j * tq, tq), tq)
                kept_a[0, rows, :] = value[:tq]
                sent_a[0, rows, :] = value[tq:]

            @pl.when(w >= pl.num_programs(0) // 2)
            def _():
                rows = pl.ds(pl.multiple_of((j // 2) * chunk, chunk), chunk)

                @pl.when(j % 2 == 0)
                def _():
                    kept_b[0, rows, :] = value

                @pl.when(j % 2 == 1)
                def _():
                    sent_b[0, rows, :] = value

        @pl.when(jnp.logical_not(needed))
        def _():
            store(jnp.zeros((chunk, 2 * hd), BF))

        @pl.when(needed)
        def _():
            kv = kv_ref[0, here, :]
            one, nought = jnp.ones_like(kv), jnp.zeros_like(kv)
            key_one = jnp.where(lane < hd, kv, jnp.where(lane < hd + 3, one, nought))
            one_value = jnp.where(lane >= hd, kv, jnp.where(lane < 3, one, nought))
            allowed = (pos >= lo) & (pos <= query)
            allowed = jnp.concatenate([allowed] * group, axis=1)
            for g in range(heads // group):
                cols = slice(g * lanes, (g + 1) * lanes)
                p = jnp.exp2(dot(key_one, qx_s[:, cols], ((1,), (0,))) * scale2)
                p = jnp.where(allowed, p, 0.0)
                ds_s[:, cols] = (p * dot(one_value, dox_s[:, cols], ((1,), (0,)))).astype(BF)
                p_s[:, cols] = p.astype(BF)
            dk = dot(ds_s[...], qx_s[...], ((1,), (1,)))
            dv = dot(p_s[...], dox_s[...], ((1,), (1,)))
            dq_s[...] = dq_s[...] + dot(kv.T, ds_s[...], ((1,), (0,)))[:hd, :]
            dkv = jnp.where(lane < hd, dk * scale, dv)
            store(dkv.astype(BF))

        return carry

    lax.fori_loop(0, kv_ref.shape[1] // chunk, body, 0)
    for h in range(heads):
        dq_ref[0, h * hd : (h + 1) * hd, :] = (dq_s[:, h * tq : (h + 1) * tq] * scale).astype(BF)


def assemble_kernel(core, own, *refs, first, wide, count):
    out = refs[-1]
    i = pl.program_id(0)

    @pl.when(i < first)
    def _():
        out[...] = own[...].astype(F32)

    @pl.when(i >= first)
    def _():
        for c in range(count):
            out[:, c * wide : (c + 1) * wide] = refs[c][...].astype(F32)


def assemble(core, own, mix, previous, shape, block, wide, skip, name):
    by_rows = block[1] == shape[1]
    axis = 0 if by_rows else 1
    first = own.shape[axis] // block[axis]
    second = (shape[axis] - 2 * own.shape[axis]) // block[axis] // 2
    count = block[1] // wide

    def at(place):
        return (place, 0) if by_rows else (0, place)

    def mix_at(c):
        return lambda i, core: (skip // block[0] + c * second * by_rows + c * (not by_rows) + jnp.maximum(i - first, 0), 0)

    def out_at(i, core):
        return at(jnp.where(i < first, core[0] * first + i, 2 * first + core[0] * second + i - first))

    in_specs = [pl.BlockSpec(block, lambda i, core: at(jnp.minimum(i, first - 1)))]
    in_specs += [pl.BlockSpec((block[0], wide), mix_at(c)) for c in range(count)]
    arrays = [own, *[mix] * count]
    if previous is not None:
        in_specs.append(pl.BlockSpec(memory_space=pl.ANY))
        arrays.append(previous)
    return pl.pallas_call(
        partial(assemble_kernel, first=first, wide=wide, count=count),
        out_shape=jax.ShapeDtypeStruct(shape, F32),
        grid_spec=pltpu.PrefetchScalarGridSpec(
            num_scalar_prefetch=1,
            grid=(first + second,),
            in_specs=in_specs,
            out_specs=pl.BlockSpec(block, out_at),
        ),
        input_output_aliases={} if previous is None else {len(arrays): 0},
        compiler_params=pltpu.CompilerParams(vmem_limit_bytes=16 << 20),
        cost_estimate=pl.CostEstimate(flops=0, bytes_accessed=3 * shape[0] * shape[1], transcendentals=0),
        name=name,
    )(core, *arrays)


def per_window(shape):
    zeros = (0,) * (len(shape) - 1)
    return pl.BlockSpec((1, *shape[1:]), lambda w, scal: (w, *zeros))


def half_windows(shape, late):
    zeros = (0,) * (len(shape) - 1)
    if late:
        return pl.BlockSpec((1, *shape[1:]), lambda w, scal: (jnp.maximum(w - shape[0], 0), *zeros))
    return pl.BlockSpec((1, *shape[1:]), lambda w, scal: (jnp.minimum(w, shape[0] - 1), *zeros))


def attention_call(kernel, scalars, inputs, outs, scratch, name, flops, halves=0):
    vmem = (12 << 20) + 10 * math.prod(inputs[1].shape[1:]) * inputs[1].dtype.itemsize
    moved = sum(math.prod(a.shape) * a.dtype.itemsize for a in (*inputs, *outs))
    return pl.pallas_call(
        kernel,
        out_shape=outs,
        grid_spec=pltpu.PrefetchScalarGridSpec(
            num_scalar_prefetch=1,
            grid=(inputs[0].shape[0],),
            in_specs=[per_window(a.shape) for a in inputs],
            out_specs=[per_window(a.shape) for a in outs[: len(outs) - halves]]
            + [half_windows(a.shape, i >= halves // 2) for i, a in enumerate(outs[len(outs) - halves :])],
            scratch_shapes=scratch,
        ),
        compiler_params=pltpu.CompilerParams(vmem_limit_bytes=vmem),
        cost_estimate=pl.CostEstimate(flops=flops, bytes_accessed=moved, transcendentals=0),
        name=name,
    )(scalars, *inputs)


def local(
    tokens,
    attn_gain,
    attn_shift,
    w_query,
    b_query,
    w_keyval,
    b_value,
    w_out,
    b_out,
    mlp_gain,
    mlp_shift,
    w_up,
    b_up,
    w_down,
    b_down,
    doc_lengths,
    cotangent,
):
    tq, windows, width = tokens.shape
    hd = w_keyval.shape[1] // 2
    own_cols = w_query.shape[1]
    seq_size = lax.axis_size("seq")
    cols = own_cols * lax.axis_size("head")
    heads = cols // hd
    seq_total = tq * seq_size * lax.axis_size("head")
    me = lax.axis_index("seq") * lax.axis_size("head") + lax.axis_index("head")
    chunk = min(2 * tq, seq_total)

    core = ("batch", 1)
    head = ("head", 1)
    low = ("seq", 1)
    highs = [("seq", 1 << i) for i in range(1, int(math.log2(seq_size)))]

    def other_half(weight):
        half = weight.shape[0] // 2
        part = lax.dynamic_slice_in_dim(weight, lax.axis_index("batch") * half, half, 0)
        return double([swap(part, head)], core, [0])[0]

    wq_other = other_half(w_query)
    bq_other = swap(b_query, head)
    head_first = bit_of(head) == 0

    def in_order(own, other, dim):
        return jnp.concatenate([jnp.where(head_first, own, other), jnp.where(head_first, other, own)], dim)

    wq_all = in_order(w_query, wq_other, 1)
    bq_all = in_order(b_query, bq_other, 0)

    bounds = jnp.cumsum(doc_lengths, axis=1)
    places = me * tq + jnp.arange(tq, dtype=jnp.int32)
    starts = jnp.max(
        jnp.where(bounds[:, :, None] <= places[None, None, :], bounds[:, :, None], 0), axis=1
    )
    scalars = jnp.concatenate([me[None].astype(jnp.int32), starts[:, 0]])
    starts = starts[:, None, :]

    residual = jnp.transpose(tokens, (1, 0, 2)).astype(F32)
    normed = layer_norm(residual, attn_gain, attn_shift).astype(BF)
    value_bias = jnp.concatenate([jnp.zeros((hd,), F32), b_value])
    keyval = (
        jnp.einsum("wtd,dc->wtc", normed, w_keyval, preferred_element_type=F32) + value_bias
    ).astype(BF)

    bits = [*reversed(highs), low, head]

    def gather_step(block, step):
        return jnp.concatenate([block, swap(block, step)], 1 + bits.index(step))

    def reduce_block(block, step):
        kept, sent = jnp.split(block, 2, 1 + bits.index(step))
        return add_low(kept, swap(sent, step))

    half_w = windows // 2
    block = keyval.reshape(windows, *[1] * len(bits), tq, 2 * hd)
    for step in reversed(highs):
        block = gather_step(block, step)
    keyval_all = jnp.concatenate(
        [
            gather_step(gather_step(block[:half_w], low), head).reshape(half_w, seq_total, 2 * hd),
            gather_step(gather_step(block[half_w:], head), low).reshape(half_w, seq_total, 2 * hd),
        ],
        0,
    )
    keyval_all, w_out = tie(keyval_all, w_out)
    wo_all = in_order(w_out, swap(w_out, head), 0)

    queries = (
        jnp.einsum("do,wtd->wot", wq_all, normed, preferred_element_type=F32) + bq_all[None, :, None]
    ).astype(BF)

    struct = jax.ShapeDtypeStruct
    lanes = heads * tq
    work = 2 * windows * lanes * (seq_total // 4) * hd
    mixed, log_total = attention_call(
        partial(forward_kernel, heads=heads, hd=hd, chunk=chunk),
        scalars,
        (queries, keyval_all, starts),
        (struct((windows, cols, tq), BF), struct((windows, 1, lanes), F32)),
        [pltpu.VMEM((1, lanes), F32), pltpu.VMEM((1, lanes), F32), pltpu.VMEM((hd, lanes), F32)],
        "attend",
        8 * work,
    )

    branch = jnp.einsum("wot,od->wtd", mixed, wo_all, preferred_element_type=F32)
    middle = residual + (branch + b_out)
    inner = layer_norm(middle, mlp_gain, mlp_shift).astype(BF)
    upstream_low = jnp.transpose(cotangent, (1, 0, 2))
    upstream = upstream_low.astype(F32)

    upward = jnp.einsum("wtd,df->wtf", inner, w_up, preferred_element_type=F32) + b_up
    active = jax.nn.gelu(upward, approximate=True).astype(BF)
    grad_active = jnp.einsum("wtd,fd->wtf", upstream_low, w_down, preferred_element_type=F32)
    gelu_back = jax.vjp(partial(jax.nn.gelu, approximate=True), upward)[1]
    grad_upward = gelu_back(grad_active)[0].astype(BF)

    ff = w_up.shape[1]
    cut = 2 * ff // 3
    spans = (0, cut // 2), (cut, (ff - cut) // 2)
    on_first = bit_of(core) == 0

    def columns(array, span, other):
        first, size = span
        start = first + size * (bit_of(core) ^ other)
        return lax.dynamic_slice_in_dim(array, start, size, 2)

    def part_down(span, other):
        return jnp.einsum("wtf,wtd->fd", columns(active, span, other), upstream_low, preferred_element_type=F32)

    def part_up(span, other):
        return jnp.einsum("wtd,wtf->df", inner, columns(grad_upward, span, other), preferred_element_type=F32)

    def own_part(make, span, got):
        return (make(span, 0) + got.astype(F32)).astype(BF)

    wide = math.gcd(spans[1][1], width)

    def stack(array):
        return jnp.concatenate([array[:, at : at + wide] for at in range(0, array.shape[1], wide)], 0)

    def unstack(array, rows):
        return jnp.concatenate([array[at : at + rows] for at in range(0, array.shape[0], rows)], 1)

    got_down = swap(part_down(spans[0], 1).astype(BF), core)
    got_up = swap(part_up(spans[0], 1).astype(BF), core)
    got_mix = swap(
        jnp.concatenate([stack(part_down(spans[1], 1).astype(BF)), stack(part_up(spans[1], 1).astype(BF))], 0), core
    )
    rows_mix = spans[1][1]
    rows_down = rows_mix * (width // wide)
    pieces = [
        own_part(part_down, spans[0], got_down),
        own_part(part_up, spans[0], got_up),
        jnp.concatenate(
            [
                stack(own_part(part_down, spans[1], unstack(got_mix[:rows_down], rows_mix))),
                stack(own_part(part_up, spans[1], unstack(got_mix[rows_down:], width))),
            ],
            0,
        ),
    ]

    grad_inner = jnp.einsum("wtf,df->wtd", grad_upward, w_up, preferred_element_type=F32)
    norm_back = jax.vjp(layer_norm, middle, mlp_gain, mlp_shift)[1]
    grad_mid_norm, grad_mlp_gain, grad_mlp_shift = norm_back(grad_inner)
    grad_middle = upstream + grad_mid_norm
    grad_branch = grad_middle.astype(BF)
    grad_mixed = jnp.einsum("od,wtd->wot", wo_all, grad_branch, preferred_element_type=F32).astype(BF)

    own_rows = own_cols // 2

    def core_halves(array):
        array = array.reshape(cols // own_cols, 2, own_rows, width)
        sent = lax.dynamic_index_in_dim(array, 1 - bit_of(core), 1, False)
        kept = lax.dynamic_index_in_dim(array, bit_of(core), 1, False)
        return add_low(kept, swap(sent, core))

    grad_w_out = jnp.einsum("wot,wtd->od", mixed, grad_branch, preferred_element_type=F32).astype(BF)
    out_half = core_halves(grad_w_out)
    out_half = jnp.concatenate([stack(out_half[h]) for h in range(cols // own_cols)], 0)

    near, far = highs[0], highs[1:]
    orders = [near, low, head, *far], [low, head, near, *far], [head, near, low, *far]
    last = len(orders[0]) - 1
    groups = [[pieces[0]], [pieces[1]], [pieces[2], out_half]]
    dims = [[], [], []]

    def reduce_step(at):
        for i in range(3):
            groups[i], dim = halve(groups[i], orders[i][at])
            dims[i].append(dim)

    groups, grad_mixed = tie(groups, grad_mixed)
    reduce_step(0)
    half_keys = struct((half_w, seq_total // 2, 2 * hd), BF)
    grad_queries, *grad_keys = attention_call(
        partial(backward_kernel, heads=heads, hd=hd, chunk=chunk),
        scalars,
        (queries, keyval_all, starts, mixed, log_total, grad_mixed),
        (struct((windows, cols, tq), BF), *[half_keys] * 4),
        [pltpu.VMEM((2 * hd, lanes), BF)] * 2 + [pltpu.VMEM((hd, lanes), F32)] + [pltpu.VMEM((chunk, lanes), BF)] * 2,
        "attend_back",
        20 * work,
        4,
    )
    groups, grad_queries, grad_keys = tie(groups, grad_queries, grad_keys)

    def open_blocks(value, step):
        sides = [1 if other == step else 2 for other in bits]
        return value.reshape(half_w, *sides, tq, 2 * hd)

    def part_query(other):
        half = width // 2
        rows = lax.dynamic_slice_in_dim(normed, half * (bit_of(core) ^ other), half, 2)
        return jnp.einsum("wtd,wot->do", rows, later_queries, preferred_element_type=F32)

    kept_a, sent_a, kept_b, sent_b = grad_keys
    reduce_step(1)
    blocks = [add_low(kept_a, swap(sent_a, head)), add_low(kept_b, swap(sent_b, low))]
    blocks = [open_blocks(blocks[0], head), open_blocks(blocks[1], low)]
    groups, blocks, later_queries = tie(groups, blocks, grad_queries)

    reduce_step(2)
    blocks = [reduce_block(blocks[0], low), reduce_block(blocks[1], head)]
    sent_query = part_query(1).astype(BF)
    groups, blocks, sent_query, active, grad_upward, grad_branch, upstream, later_queries = tie(
        groups, blocks, sent_query, active, grad_upward, grad_branch, upstream, later_queries
    )

    for step in far[:-1]:
        groups = [[add_low(a, g) for a, g in zip(group, swap_all(group, step))] for group in groups]
    far_got = [None, *[swap_all(group, far[-1]) for group in groups[1:]]]
    blocks = reduce_block(jnp.concatenate(blocks, 0), near)
    got_query = swap(sent_query, core)
    query_half = (part_query(0) + got_query.astype(F32)).astype(BF)
    blocks, query_half, active, grad_upward, grad_branch, upstream, later_queries = tie(
        blocks, query_half, active, grad_upward, grad_branch, upstream, later_queries
    )

    for step in far:
        blocks = reduce_block(blocks, step)
    own_head = lax.axis_index("head")
    sent = lax.dynamic_slice_in_dim(query_half, own_cols * (1 - own_head), own_cols, 1)
    kept = lax.dynamic_slice_in_dim(query_half, own_cols * own_head, own_cols, 1)
    query_half = add_low(kept, swap(sent, head))
    result = (
        middle + (jnp.einsum("wtf,fd->wtd", active, w_down, preferred_element_type=F32) + b_down)
    ).astype(BF)
    result = jnp.transpose(result, (1, 0, 2))
    grad_b_up = jnp.sum(grad_upward.astype(F32), axis=(0, 1))
    grad_b_down = jnp.sum(upstream, axis=(0, 1))
    grad_b_out = jnp.sum(grad_branch.astype(F32), axis=(0, 1))
    grad_b_query = jnp.sum(later_queries.astype(F32), axis=(0, 2))
    vectors = [grad_b_up, grad_b_down, grad_mlp_gain, grad_mlp_shift, grad_b_out, grad_b_query]
    blocks, groups[0] = tie(blocks, groups[0])
    far_got[0] = swap_all(groups[0], far[-1])
    blocks, query_half, result, vectors = tie(blocks, query_half, result, vectors)
    grad_keyval = blocks.reshape(windows, tq, 2 * hd)

    grad_w_keyval = jnp.einsum("wtd,wtc->dc", normed, grad_keyval, preferred_element_type=F32)
    grad_b_value = jnp.sum(grad_keyval[:, :, hd:].astype(F32), axis=(0, 1))
    grad_normed = jnp.einsum("wot,do->wtd", grad_queries, wq_all, preferred_element_type=F32)
    grad_normed = grad_normed + jnp.einsum(
        "wtc,dc->wtd", grad_keyval, w_keyval, preferred_element_type=F32
    )
    first_back = jax.vjp(layer_norm, residual, attn_gain, attn_shift)[1]
    grad_input, grad_attn_gain, grad_attn_shift = first_back(grad_normed)
    grad_tokens = jnp.transpose(grad_middle + grad_input, (1, 0, 2))

    def rows_of(vector):
        vector = jnp.pad(vector.astype(F32), (0, (-vector.shape[0]) % width))
        return [vector[at : at + width] for at in range(0, vector.shape[0], width)]

    vectors = [*vectors, grad_attn_gain, grad_attn_shift, grad_b_value]
    rows = [row for vector in vectors for row in rows_of(vector)]
    tall = -(-len(rows) // 16) * 16
    place = lax.broadcasted_iota(jnp.int32, (tall, width), 0)
    packed = jnp.zeros((tall, width), F32)
    for at, row in enumerate(rows):
        packed = jnp.where(place == at, row[None, :], packed)
    small = jnp.concatenate([grad_w_keyval, *[packed[:, at : at + 2 * hd] for at in range(0, width, 2 * hd)]], 0)
    small = small.astype(BF)

    def stack_small(array):
        count = wide // array.shape[1]
        tall = array.shape[0] // count
        return jnp.concatenate([array[at : at + tall] for at in range(0, array.shape[0], tall)], 1)

    def unstack_small(array):
        return jnp.concatenate([array[:, at : at + 2 * hd] for at in range(0, array.shape[1], 2 * hd)], 0)

    (small,), small_dim = halve([small], core)
    small = stack_small(small)
    far_got, small, query_half, grad_tokens = tie(far_got, small, query_half, grad_tokens)
    groups = [[add_low(a, g) for a, g in zip(group, got)] for group, got in zip(groups, far_got)]
    groups, small = tie(groups, small)

    def gather_step(at, join=None):
        for i in range(2):
            groups[i] = double(groups[i], orders[i][at], dims[i][at][: len(groups[i])])
        step = orders[2][at]
        got = swap_all(groups[2] if join is None else [*groups[2], join], step)
        lower = bit_of(step) == 0
        groups[2] = [
            jnp.concatenate([jnp.where(lower, a, g), jnp.where(lower, g, a)], d)
            for a, g, d in zip(groups[2], got, dims[2][at])
        ]
        return join if join is None else add_low(join, got[-1])

    small = gather_step(2, small)
    (query_half,), query_dim = halve([query_half], low)
    groups, small, query_half, grad_tokens = tie(groups, small, query_half, grad_tokens)

    small = gather_step(1, small)
    query_half = add_low(query_half, swap(query_half, near))
    groups, small, query_half = tie(groups, small, query_half)

    def both(own, other, dim):
        own, other = own.astype(F32), other.astype(F32)
        return [jnp.where(on_first, own, other), jnp.where(on_first, other, own)]

    out_half = groups[2].pop()
    gather_step(0)
    for step in far:
        query_half = add_low(query_half, swap(query_half, step))
    for step in [*far, head]:
        small = add_low(small, swap(small, step))
    (query_half,) = double([query_half], low, query_dim)
    (small,) = double([unstack_small(small)], core, small_dim)
    query_other = swap(query_half, core)
    out_other = swap(out_half, core)
    out_half, out_other = unstack(out_half, own_rows), unstack(out_other, own_rows)
    grad_w_out = jnp.concatenate(both(out_half, out_other, 0), 0)
    small = small.astype(F32)
    grad_w_keyval, packed = small[:width], small[width:]
    packed = jnp.concatenate([packed[at : at + tall] for at in range(0, packed.shape[0], tall)], 1)
    sums, at = [], 0
    for vector in vectors:
        count = -(-vector.shape[0] // width)
        sums.append(packed[at : at + count].reshape(-1)[: vector.shape[0]])
        at += count
    sums[5] = lax.dynamic_slice_in_dim(sums[5], lax.axis_index("head") * own_cols, own_cols, 0)
    groups, sums, grad_w_keyval, grad_w_out, query_half, query_other = tie(
        groups, sums, grad_w_keyval, grad_w_out, query_half, query_other
    )

    (down,), (up,), (mix,) = groups
    got_down, got_mix, got_up = swap(down, core), swap(mix, core), swap(up, core)
    where = lax.axis_index("batch")[None].astype(jnp.int32)
    down_block, up_block = (rows_mix // 2, width), (width, rows_mix)
    own_down = assemble(where, down, mix, None, (ff, width), down_block, wide, 0, "own_down")
    own_up = assemble(where, up, mix, None, (width, ff), up_block, wide, rows_down, "own_up")
    got_down, got_mix, got_up, own_down, own_up = tie(got_down, got_mix, got_up, own_down, own_up)
    grad_w_down = assemble(1 - where, got_down, got_mix, own_down, (ff, width), down_block, wide, 0, "got_down")
    grad_w_up = assemble(1 - where, got_up, got_mix, own_up, (width, ff), up_block, wide, rows_down, "got_up")

    grad_w_query = jnp.concatenate(both(query_half, query_other, 0), 0)
    b_up_sum, b_down_sum, mlp_gain_sum, mlp_shift_sum, b_out_sum, b_query_sum, gain_sum, shift_sum, b_value_sum = sums

    return (
        result,
        grad_tokens,
        gain_sum,
        shift_sum,
        grad_w_query,
        b_query_sum,
        grad_w_keyval,
        b_value_sum,
        grad_w_out,
        b_out_sum,
        mlp_gain_sum,
        mlp_shift_sum,
        grad_w_up,
        b_up_sum,
        grad_w_down,
        b_down_sum,
    )


def solution(mesh):
    return jax.shard_map(
        local,
        mesh=mesh,
        in_specs=(
            P(("seq", "head"), "batch", None),
            P(),
            P(),
            P(None, "head"),
            P("head"),
            P(),
            P(),
            P("head", None),
            P(),
            P(),
            P(),
            P(),
            P(),
            P(),
            P(),
            P("batch", None),
            P(("seq", "head"), "batch", None),
        ),
        out_specs=(
            P(("seq", "head"), "batch", None),
            P(("seq", "head"), "batch", None),
            P(),
            P(),
            P(None, "head"),
            P("head"),
            P(),
            P(),
            P("head", None),
            P(),
            P(),
            P(),
            P(),
            P(),
            P(),
            P(),
        ),
        check_vma=False,
    )
```
